32 devices in a mesh: blk: 8 (over z, x), slab: 4 (over y, core).
Axes of the slice: x: 2, y: 2, z: 4, core: 2. Of those that a mesh axis runs over, the one named last changes fastest.
Arguments:
- states_in: float32 [256, 8, 8, 1024], P('blk', None, 'slab'), may hold values from -6 to 6
- region: int32 [8, 1024], P('slab'), may hold values from 0 to 3
- onsite_table: float32 [4, 8, 8], replicated, may hold values from -1.75 to 1.75
- hop_table: float32 [4, 8], replicated, may hold values from 0.05 to 0.3
- coupling_x: float32 [8, 8], replicated, may hold values from -0.875 to 0.875
- coupling_y: float32 [8, 8], replicated, may hold values from -0.875 to 0.875
Outputs:
- states_out: float32 [256, 8, 8, 1024], P('blk', None, 'slab')
- projected: float32 [256, 256], P('blk')
The draws below stay inside these ranges and needn't reach their ends.
Inputs may be any that keep to these rules, and one draw needn't show every extreme that they name: `region`: material codes.
All inputs are finite; a program needn't handle non-finite values.
Results may differ from the reference program's by a relative error of at most 0.000084.
Values sent between devices are 32-bit elements; how exact they have to be, the bound alone decides.
No kernel may reach another device: no remote copies, remote signals or barrier semaphores. Data moves between devices by JAX's collectives and lax.ppermute only.
A program may use at most 128 MiB of HBM per device.

```python
import math
import jax
import jax.numpy as jnp
from jax import lax

S = 256
BANDS = 8
MATERIALS = 4
NY = 1024
DEGREE = 4
PANEL = 32
NX = 8


def place_ends(array, rng, low, largest):
    place = [jax.random.randint(jax.random.fold_in(rng, axis), (), 0, length) for axis, length in enumerate(array.shape)]
    widest = array.shape.index(max(array.shape))
    neighbour = place[:widest] + [(place[widest] + 1) % array.shape[widest]] + place[widest + 1:]
    return array.at[tuple(place)].set(low).at[tuple(neighbour)].set(largest)


def block_levels(rng, dims, cuts, low, top_value):
    factor_of, own = 1.0, jax.random.fold_in(rng, 6)
    for position, blocks in cuts:
        draws = jnp.exp(jax.random.uniform(jax.random.fold_in(own, position), (blocks,), jnp.float32, low / len(cuts), top_value / len(cuts)))
        factor_of = factor_of * jnp.repeat(draws, dims[position] // blocks).reshape([-1 if axis == position else 1 for axis in range(len(dims))])
    return factor_of


def normal_values(own_key, dims, scale, bound, split=(), kind=jnp.bfloat16):
    level = block_levels(own_key, dims, split, -0.22, 0.18) if split else 1.0
    drawn = jax.random.normal(own_key, dims, jnp.float32) * scale * level
    return jnp.minimum(jnp.maximum(drawn, -bound), bound).astype(kind)


def setup_inputs(seed: int = 0) -> dict:
    arg_keys = jax.random.split(jax.random.key(seed), 7)
    states_in = normal_values(arg_keys[0], (S, BANDS, NX, NY), 1.0, 6.0, ((0, 8), (2, 4)), jnp.float32)
    region = place_ends(jax.random.randint(arg_keys[1], (NX, NY), 0, MATERIALS), jax.random.fold_in(arg_keys[1], 1), 0, MATERIALS - 1).astype(jnp.int32)
    onsite_table = normal_values(arg_keys[2], (MATERIALS, BANDS, BANDS), 0.3, 1.75, (), jnp.float32)
    hop_table = jnp.clip(jnp.exp(jax.random.uniform(arg_keys[3], (MATERIALS, BANDS), jnp.float32, math.log(0.05), math.log(0.3))), 0.05, 0.3)
    coupling_x = normal_values(arg_keys[4], (BANDS, BANDS), 0.15, 0.875, (), jnp.float32)
    coupling_y = normal_values(arg_keys[5], (BANDS, BANDS), 0.15, 0.875, (), jnp.float32)
    return {"states_in": states_in, "region": region, "onsite_table": onsite_table, "hop_table": hop_table, "coupling_x": coupling_x, "coupling_y": coupling_y}


SHIFT = 1.0
SCALE = 3.0

def mixing(onsite_table, coupling_x, coupling_y):
    onsite = 0.5 * (onsite_table + jnp.swapaxes(onsite_table, 1, 2))
    blocks = [onsite[material] for material in range(onsite.shape[0])]
    return jnp.concatenate(blocks + [0.5 * (coupling_x - coupling_x.T), 0.5 * (coupling_y - coupling_y.T)], axis=1)

def masks_of(region):
    codes = jnp.arange(MATERIALS, dtype=jnp.int32)
    return (region[None] == codes[:, None, None]).astype(jnp.float32)

def apply_padded(padded, hop_padded, material_masks, mixing_matrix):
    centre = padded[:, :, 1:-1, 1:-1]
    hop_centre = hop_padded[:, 1:-1, 1:-1]
    kinetic = jnp.zeros_like(centre)
    sides = ((padded[:, :, 2:, 1:-1], hop_padded[:, 2:, 1:-1]), (padded[:, :, :-2, 1:-1], hop_padded[:, :-2, 1:-1]), (padded[:, :, 1:-1, 2:], hop_padded[:, 1:-1, 2:]), (padded[:, :, 1:-1, :-2], hop_padded[:, 1:-1, :-2]))
    for field_side, hop_side in sides:
        kinetic = kinetic + (0.5 * (hop_centre + hop_side))[None] * (centre - field_side)
    deriv_rows = 0.5 * (padded[:, :, 2:, 1:-1] - padded[:, :, :-2, 1:-1])
    deriv_cols = 0.5 * (padded[:, :, 1:-1, 2:] - padded[:, :, 1:-1, :-2])
    pieces = [material_masks[material][None, None] * centre for material in range(material_masks.shape[0])]
    stacked = jnp.concatenate(pieces + [deriv_rows, deriv_cols], axis=1)
    mixed = jnp.einsum('bc,scxy->sbxy', mixing_matrix, stacked, precision=lax.Precision.HIGHEST)
    return mixed + kinetic

def chebyshev(field, apply_fn):

    def scaled(value):
        return (apply_fn(value) - SHIFT * value) / SCALE
    previous = field
    current = scaled(field)
    for repeat in range(DEGREE - 1):
        previous, current = (current, 2.0 * scaled(current) - previous)
    return current

def reference(states_in, region, onsite_table, hop_table, coupling_x, coupling_y):
    mixing_matrix = mixing(onsite_table, coupling_x, coupling_y)
    material_masks = masks_of(region)
    hop_field = jnp.einsum('mb,mxy->bxy', hop_table, material_masks, precision=lax.Precision.HIGHEST)
    hop_padded = jnp.pad(hop_field, ((0, 0), (1, 1), (1, 1)))

    def apply_full(field):
        padded = jnp.pad(field, ((0, 0), (0, 0), (1, 1), (1, 1)))
        return apply_padded(padded, hop_padded, material_masks, mixing_matrix)
    groups = S // PANEL
    blocks = states_in.reshape(groups, PANEL, BANDS, NX, NY)
    filtered = lax.map(lambda state_block: chebyshev(state_block, apply_full), blocks)
    filtered_flat = filtered.reshape(S, -1)
    entries = float(BANDS * NX * NY)
    gram_matrix = jnp.dot(filtered_flat.astype(jnp.float32), filtered_flat.T.astype(jnp.float32), precision=lax.Precision.HIGHEST, preferred_element_type=jnp.float32) / entries

    def moment_columns(state_block):
        image = apply_full(state_block).reshape(PANEL, -1)
        return jnp.dot(filtered_flat.astype(jnp.float32), image.T.astype(jnp.float32), precision=lax.Precision.HIGHEST, preferred_element_type=jnp.float32) / entries
    pieces = lax.map(moment_columns, filtered)
    moment = jnp.transpose(pieces, (1, 0, 2)).reshape(S, S)
    factor = jnp.linalg.cholesky(gram_matrix)
    basis_flat = lax.linalg.triangular_solve(factor, filtered_flat, left_side=True, lower=True)
    half_done = lax.linalg.triangular_solve(factor, moment, left_side=True, lower=True)
    projected = lax.linalg.triangular_solve(factor, half_done.T, left_side=True, lower=True).T
    return (basis_flat.reshape(S, BANDS, NX, NY), projected)
```

```python
import jax
import jax.numpy as jnp
from jax import lax
from jax.experimental import pallas as pl
from jax.experimental.pallas import tpu as pltpu
from jax.sharding import PartitionSpec as P

BANDS = 8
MATERIALS = 4
PANEL = 32
SHIFT = 1.0
SCALE = 3.0
LANES = 128
ALL = ("blk", "slab")
LEFT = 4
WINDOW = 42
VMEM = pltpu.CompilerParams(vmem_limit_bytes=56 * 1024 * 1024)
HIGHEST = lax.Precision.HIGHEST


def dot(left, right, dims=((1,), (0,)), precision=None):
    return lax.dot_general(
        left, right, (dims, ((), ())), precision=precision, preferred_element_type=jnp.float32
    )


def split(value):
    high = value.astype(jnp.bfloat16)
    return high, (value - high.astype(jnp.float32)).astype(jnp.bfloat16)


def exchange(pieces, unit):
    count = len(pieces)
    lane = lax.broadcasted_iota(jnp.int32, pieces[0].shape, 1) // unit
    step = count // 2
    while step:
        low = (lane // step) % 2 == 0
        out = list(pieces)
        for i in range(count):
            if (i // step) % 2 == 0:
                a, c = pieces[i], pieces[i + step]
                out[i] = jnp.where(low, a, pltpu.roll(c, step * unit, 1))
                out[i + step] = jnp.where(low, pltpu.roll(a, LANES - step * unit, 1), c)
        pieces = out
        step //= 2
    return pieces


def pack_kernel(x_ref, o_ref, scr):
    scr[0 : LEFT * 4, :] = jnp.zeros((LEFT * 4, LANES), jnp.float32)
    tail = (LEFT + 1024) * 4
    scr[tail:, :] = jnp.zeros((scr.shape[0] - tail, LANES), jnp.float32)
    for tile in range(8):
        for r in range(4):
            row, high = r // 2, r % 2
            parts = [
                x_ref[pl.ds(((high * 4 + low) * 8 + tile) * 2 + row, 32, stride=128), :]
                for low in range(4)
            ]
            turned = jnp.concatenate(parts, axis=0).T
            scr[pl.ds((LEFT + 128 * tile) * 4 + r, 128, stride=4), :] = turned
    for d in range(32):
        o_ref[d] = scr[128 * d : 128 * d + WINDOW * 4, :]


def pack(x):
    rows = x.reshape(32, 8, 2, 8, LANES).transpose(0, 1, 3, 2, 4).reshape(4096, LANES)
    return pl.pallas_call(
        pack_kernel,
        out_shape=jax.ShapeDtypeStruct((32, WINDOW * 4, LANES), jnp.float32),
        scratch_shapes=[pltpu.VMEM((4136, LANES), jnp.float32)],
        compiler_params=VMEM,
        name="pack",
    )(rows)


def unpack_kernel(r_ref, o_ref):
    for tile in range(8):
        for r in range(4):
            row, high = r // 2, r % 2
            turned = r_ref[pl.ds(tile * 512 + r, 128, stride=4), :].T
            for low in range(4):
                o_ref[pl.ds(((high * 4 + low) * 8 + tile) * 2 + row, 32, stride=128), :] = turned[
                    32 * low : 32 * low + 32
                ]


def unpack(blocks):
    rows = pl.pallas_call(
        unpack_kernel,
        out_shape=jax.ShapeDtypeStruct((4096, LANES), jnp.float32),
        compiler_params=VMEM,
        name="unpack",
    )(blocks.reshape(4096, LANES))
    return rows.reshape(32, 8, 8, 2, LANES).transpose(0, 1, 3, 2, 4).reshape(32, 8, 2, 1024)


def coef_kernel(reg_ref, onsite_ref, hop_ref, kx_ref, ky_ref, ch_ref, cl_ref):
    def decode(index):
        band = (index % 2) * 4 + (index // 32) % 4
        x = ((index // 8) % 4) * 2 + (index // 2) % 2
        column = (index // 4) % 2
        return band, x, column

    def one_hot(values, shape, axis):
        return (values == lax.broadcasted_iota(jnp.int32, shape, axis)).astype(jnp.float32)

    b_r, x_r, y_r = decode(lax.broadcasted_iota(jnp.int32, (128, 8), 0))
    band_rows = one_hot(b_r, (128, 8), 1)
    b_c, _, _ = decode(lax.broadcasted_iota(jnp.int32, (8, 384), 1))
    band_cols = one_hot(b_c, (8, 384), 0)
    reg = reg_ref[...]
    hop = dot(band_rows, hop_ref[...], ((1,), (1,)), HIGHEST)

    def table_of(offset):
        return dot(one_hot(x_r + offset, (128, 8), 1), reg, precision=HIGHEST)

    def hops(codes):
        total = jnp.zeros_like(codes)
        for m in range(MATERIALS):
            total = total + jnp.where(codes == m + 1.0, hop[:, m : m + 1], 0.0)
        return total

    second = (lax.broadcasted_iota(jnp.int32, (128, LANES), 0) // 4) % 2 == 1

    def aligned(table):
        return jnp.where(second, pltpu.roll(table, LANES - 1, 1), table)

    codes = table_of(0)
    here, up, down = hops(codes), hops(table_of(-1)), hops(table_of(1))
    before, after = pltpu.roll(here, 1, 1), pltpu.roll(here, LANES - 1, 1)
    valid = (codes > 0.5).astype(jnp.float32)
    centre = (0.5 * (4.0 * here + up + down + before + after) - SHIFT) * valid
    fields = [aligned((codes == m + 1.0).astype(jnp.float32)) for m in range(MATERIALS)]
    fields += [aligned(valid), aligned(centre)]
    fields += [aligned(-0.5 * (here + side) * valid) for side in (up, down, before, after)]

    b_r, x_r, y_r = decode(lax.broadcasted_iota(jnp.int32, (128, 384), 0))
    k = lax.broadcasted_iota(jnp.int32, (128, 384), 1)
    b_c, x_c, y_c = decode(k)
    dy = 2 * (k // 128 - 1) + y_c - y_r
    dx = x_c - x_r
    same = b_r == b_c

    def spread(matrix):
        return dot(dot(band_rows, matrix, precision=HIGHEST), band_cols, precision=HIGHEST)

    here_at, up_at, down_at = (dy == 0) & (dx == 0), (dy == 0) & (dx == -1), (dy == 0) & (dx == 1)
    before_at, after_at = (dy == -1) & (dx == 0), (dy == 1) & (dx == 0)
    onsite = [
        jnp.where(here_at, spread(0.5 * (onsite_ref[m] + onsite_ref[m].T)), 0.0) for m in range(MATERIALS)
    ]
    kx = spread(0.5 * (0.5 * (kx_ref[...] - kx_ref[...].T)))
    ky = spread(0.5 * (0.5 * (ky_ref[...] - ky_ref[...].T)))
    mixed = (
        jnp.where(down_at, kx, 0.0)
        - jnp.where(up_at, kx, 0.0)
        + jnp.where(after_at, ky, 0.0)
        - jnp.where(before_at, ky, 0.0)
    )
    places = [here_at & same, up_at & same, down_at & same, before_at & same, after_at & same]
    for pair in range(WINDOW // 2):
        lane = 2 * pair + 1
        scalar = [field[:, lane : lane + 1] for field in fields]
        value = scalar[4] * mixed
        for m in range(MATERIALS):
            value = value + scalar[m] * onsite[m]
        for place, weight in zip(places, scalar[5:]):
            value = value + jnp.where(place, weight, 0.0)
        high, low = split((2.0 / SCALE) * value)
        ch_ref[pair] = high
        cl_ref[pair] = low


def coefficients(reg, onsite_table, hop_table, coupling_x, coupling_y):
    shape = jax.ShapeDtypeStruct((WINDOW // 2, 128, 384), jnp.bfloat16)
    return pl.pallas_call(
        coef_kernel, out_shape=(shape, shape), compiler_params=VMEM, name="coefficients"
    )(reg, onsite_table, hop_table, coupling_x, coupling_y)


def filter_kernel(r_ref, ch_ref, cl_ref, vh_ref, vl_ref, g_ref, m_ref, fa, fb, ah, al, bh, bl):
    pairs = WINDOW // 2
    block = 128
    zero = jnp.zeros((block, 256), jnp.bfloat16)
    for ref in (ah, al, bh, bl):
        ref[0:block, :] = zero
        ref[(pairs + 1) * block :, :] = zero
    for slab in range(4):
        for half in range(2):
            pieces = [r_ref[(half * 4 + j) * 4 + slab] for j in range(4)]
            for low, piece in enumerate(exchange(pieces, 32)):
                high_part, low_part = split(piece)
                for pair in range(pairs):
                    at = pair * block + low * 32 + slab * 8
                    lanes = slice(half * 128, half * 128 + 128)
                    fa[at : at + 8, lanes] = piece[pair * 8 : pair * 8 + 8]
    ah[block : (pairs + 1) * block, :], al[block : (pairs + 1) * block, :] = split(fa[...])

    def product(pair, high, low, first=0, last=3):
        rows = pl.ds((pair + first) * block, (last - first) * block)
        cols = slice(first * block, last * block)
        vh, vl = high[rows, :], low[rows, :]
        c_high, c_low = ch_ref[pair, :, cols], cl_ref[pair, :, cols]
        return dot(c_high, vh) + (dot(c_high, vl) + dot(c_low, vh))

    def store(pair, value, field, high, low):
        field[pl.ds(pair * block, block), :] = value
        rows = pl.ds((pair + 1) * block, block)
        high[rows, :], low[rows, :] = split(value)

    def first(pair, carry):
        store(pair, 0.5 * product(pair, ah, al), fb, bh, bl)
        return carry

    lax.fori_loop(0, pairs, first, 0)

    def later(source_high, source_low, old, high, low):
        def body(pair, carry):
            rows = pl.ds(pair * block, block)
            store(pair, product(pair, source_high, source_low) - old[rows, :], old, high, low)
            return carry

        return body

    lax.fori_loop(1, pairs - 1, later(bh, bl, fa, ah, al), 0)
    lax.fori_loop(1, pairs - 1, later(ah, al, fb, bh, bl), 0)
    lax.fori_loop(2, pairs - 2, later(bh, bl, fa, ah, al), 0)
    own = slice(3 * block, 19 * block)
    top = slice(3 * block, 20 * block)

    def image(pair, carry):
        value = product(pair, ah, al)
        rows = pl.ds((pair + 1) * block, block)
        bh[rows, :], bl[rows, :] = split(value)
        return carry

    lax.fori_loop(3, 18, image, 0)
    value = product(2, ah, al, 1, 3)
    bh[3 * block : 4 * block, :], bl[3 * block : 4 * block, :] = split(value)
    value = product(18, ah, al, 0, 1)
    row = lax.broadcasted_iota(jnp.int32, (block, 256), 0)
    value = jnp.where((row // 4) % 2 == 0, value, 0.0)
    bh[19 * block : 20 * block, :], bl[19 * block : 20 * block, :] = split(value)
    vh_ref[...] = ah[own, :]
    vl_ref[...] = al[own, :]
    dims = ((0,), (0,))
    cross = dot(ah[own, :], al[own, :], dims)
    gram = dot(ah[own, :], ah[own, :], dims) + (cross + cross.T)
    moment = dot(ah[top, :], bh[top, :], dims) + (
        dot(ah[top, :], bl[top, :], dims) + dot(al[top, :], bh[top, :], dims)
    )
    g_ref[...] = gram
    m_ref[...] = (0.5 * SCALE) * moment + SHIFT * gram


def filtered_blocks(received, coef_high, coef_low):
    rows = (WINDOW // 2) * 128
    half = jax.ShapeDtypeStruct((2048, 256), jnp.bfloat16)
    square = jax.ShapeDtypeStruct((256, 256), jnp.float32)
    return pl.pallas_call(
        filter_kernel,
        out_shape=(half, half, square, square),
        scratch_shapes=[pltpu.VMEM((rows, 256), jnp.float32)] * 2
        + [pltpu.VMEM((rows + 256, 256), jnp.bfloat16)] * 4,
        compiler_params=VMEM,
        name="filtered",
    )(received, coef_high, coef_low)


def apply_kernel(vh_ref, vl_ref, w_ref, o_ref, scr):
    wh, wl = split(w_ref[...])
    vh = vh_ref[...]
    scr[...] = dot(vh, wh, ((1,), (1,))) + (
        dot(vh, wl, ((1,), (1,))) + dot(vl_ref[...], wh, ((1,), (1,)))
    )
    for slab in range(4):
        for half in range(2):
            lanes = slice(half * 128, half * 128 + 128)
            pieces = []
            for low in range(4):
                rows = [
                    scr[pair * 128 + low * 32 + slab * 8 : pair * 128 + low * 32 + slab * 8 + 8, lanes]
                    for pair in range(16)
                ]
                pieces.append(jnp.concatenate(rows, axis=0))
            for j, piece in enumerate(exchange(pieces, 32)):
                o_ref[(half * 4 + j) * 4 + slab] = piece


def apply_inverse(vh, vl, inverse):
    return pl.pallas_call(
        apply_kernel,
        out_shape=jax.ShapeDtypeStruct((32, 128, LANES), jnp.float32),
        scratch_shapes=[pltpu.VMEM((2048, 256), jnp.float32)],
        compiler_params=VMEM,
        name="apply_inverse",
    )(vh, vl, inverse)


def total(square):
    count = lax.axis_size(ALL)
    size = square.shape[0]
    parts = square.reshape(count, size // count, size)
    share = lax.all_to_all(parts, ALL, 0, 0, tiled=True).sum(0)
    spread = jnp.broadcast_to(share[None], parts.shape)
    return lax.all_to_all(spread, ALL, 0, 0, tiled=True).reshape(size, size)


def fast(states_in, region, onsite_table, hop_table, coupling_x, coupling_y):
    slabs = lax.axis_size("slab")
    device = lax.axis_index("blk") * slabs + lax.axis_index("slab")
    codes = (region + 1).astype(jnp.float32)
    codes = lax.all_to_all(jnp.broadcast_to(codes[None], (slabs,) + codes.shape), "slab", 0, 0, tiled=True)
    codes = jnp.pad(codes.reshape(8, 1024), ((0, 0), (LEFT + 1, LANES)))
    codes = lax.dynamic_slice(codes, (0, 32 * device), (8, LANES))
    received = lax.all_to_all(pack(states_in), ALL, 0, 0, tiled=True)
    coef_high, coef_low = coefficients(codes, onsite_table, hop_table, coupling_x, coupling_y)
    vh, vl, gram, moment = filtered_blocks(received, coef_high, coef_low)
    entries = float(BANDS * 8 * 1024)
    gram = total(gram) / entries
    moment = total(moment) / entries
    factor = jnp.linalg.cholesky(gram)
    inverse = lax.linalg.triangular_solve(
        factor, jnp.eye(256, dtype=jnp.float32), left_side=True, lower=True
    )
    states_out = unpack(lax.all_to_all(apply_inverse(vh, vl, inverse), ALL, 0, 0, tiled=True))
    mine = lax.dynamic_slice_in_dim(inverse, lax.axis_index("blk") * 32, 32, 0)
    projected = dot(dot(mine, moment, precision=HIGHEST), inverse, ((1,), (1,)), HIGHEST)
    return states_out, projected


DEGREE = 4


def extended(array, sides, width):
    for axis, dim in sides:
        size, length = (lax.axis_size(axis), array.shape[dim])
        up = [(i, (i + 1) % size) for i in range(size - 1)]
        down = [(j, i) for i, j in up]
        last = lax.slice_in_dim(array, length - width, length, axis=dim)
        leading = lax.slice_in_dim(array, 0, width, axis=dim)
        before = lax.ppermute(last, axis, up)
        after = lax.ppermute(leading, axis, down)
        array = jnp.concatenate([before, array, after], axis=dim)
    return array


def mixing(onsite_table, coupling_x, coupling_y):
    onsite = 0.5 * (onsite_table + jnp.swapaxes(onsite_table, 1, 2))
    blocks = [onsite[material] for material in range(onsite.shape[0])]
    return jnp.concatenate(
        blocks + [0.5 * (coupling_x - coupling_x.T), 0.5 * (coupling_y - coupling_y.T)], axis=1
    )


def masks_of(region):
    codes = jnp.arange(MATERIALS, dtype=jnp.int32)
    return (region[None] == codes[:, None, None]).astype(jnp.float32)


def apply_padded(padded, hop_padded, material_masks, mixing_matrix):
    centre = padded[:, :, 1:-1, 1:-1]
    hop_centre = hop_padded[:, 1:-1, 1:-1]
    kinetic = jnp.zeros_like(centre)
    sides = (
        (padded[:, :, 2:, 1:-1], hop_padded[:, 2:, 1:-1]),
        (padded[:, :, :-2, 1:-1], hop_padded[:, :-2, 1:-1]),
        (padded[:, :, 1:-1, 2:], hop_padded[:, 1:-1, 2:]),
        (padded[:, :, 1:-1, :-2], hop_padded[:, 1:-1, :-2]),
    )
    for field_side, hop_side in sides:
        kinetic = kinetic + (0.5 * (hop_centre + hop_side))[None] * (centre - field_side)
    deriv_rows = 0.5 * (padded[:, :, 2:, 1:-1] - padded[:, :, :-2, 1:-1])
    deriv_cols = 0.5 * (padded[:, :, 1:-1, 2:] - padded[:, :, 1:-1, :-2])
    pieces = [
        material_masks[material][None, None] * centre for material in range(material_masks.shape[0])
    ]
    stacked = jnp.concatenate(pieces + [deriv_rows, deriv_cols], axis=1)
    mixed = jnp.einsum("bc,scxy->sbxy", mixing_matrix, stacked, precision=lax.Precision.HIGHEST)
    return mixed + kinetic


def chebyshev(field, apply_fn):

    def scaled(value):
        return (apply_fn(value) - SHIFT * value) / SCALE

    previous = field
    current = scaled(field)
    for repeat in range(DEGREE - 1):
        previous, current = (current, 2.0 * scaled(current) - previous)
    return current


def inner(left, right):
    return jnp.dot(
        left, right.T, precision=lax.Precision.HIGHEST, preferred_element_type=jnp.float32
    )


def general(states_in, region, onsite_table, hop_table, coupling_x, coupling_y):
    mixing_matrix = mixing(onsite_table, coupling_x, coupling_y)
    material_masks = masks_of(region)
    hop_field = jnp.einsum(
        "mb,mxy->bxy", hop_table, material_masks, precision=lax.Precision.HIGHEST
    )
    hop_rows = extended(hop_field, (("slab", 1),), 1)
    hop_padded = jnp.pad(hop_rows, ((0, 0), (0, 0), (1, 1)))

    def apply_rows(field):
        padded = extended(field, (("slab", 2),), 1)
        padded = jnp.pad(padded, ((0, 0), (0, 0), (0, 0), (1, 1)))
        return apply_padded(padded, hop_padded, material_masks, mixing_matrix)

    filtered = chebyshev(states_in, apply_rows)
    block_count = lax.axis_size("blk")
    slab_count = lax.axis_size("slab")
    states_all = filtered.shape[0] * block_count
    row_count = filtered.shape[2]
    width_all = filtered.shape[3]
    entries = float(BANDS * row_count * slab_count * width_all)
    image = apply_rows(filtered)
    cell_states, cell_image = (
        lax.all_to_all(filtered, "blk", split_axis=3, concat_axis=0, tiled=True),
        lax.all_to_all(image, "blk", split_axis=3, concat_axis=0, tiled=True),
    )
    states_flat = cell_states.reshape(states_all, -1)
    image_flat = cell_image.reshape(states_all, -1)
    moment = lax.psum(inner(states_flat, image_flat) / entries, ("blk", "slab"))

    def panel_step(panel, carry):
        basis_rows, factor_rows = carry
        offset = panel * PANEL
        panel_states = lax.dynamic_slice_in_dim(states_flat, offset, PANEL, 0)
        coeffs = lax.psum(inner(basis_rows, panel_states) / entries, ("blk", "slab"))
        residue = panel_states - jnp.dot(
            coeffs.T,
            basis_rows,
            precision=lax.Precision.HIGHEST,
            preferred_element_type=jnp.float32,
        )
        panel_gram = lax.psum(inner(residue, residue) / entries, ("blk", "slab"))
        panel_factor = jnp.linalg.cholesky(panel_gram)
        panel_basis = lax.linalg.triangular_solve(panel_factor, residue, left_side=True, lower=True)
        basis_rows = lax.dynamic_update_slice_in_dim(basis_rows, panel_basis, offset, 0)
        factor_row = lax.dynamic_update_slice_in_dim(coeffs.T, panel_factor, offset, 1)
        factor_rows = lax.dynamic_update_slice_in_dim(factor_rows, factor_row, offset, 0)
        return (basis_rows, factor_rows)

    start_state = (jnp.zeros_like(states_flat), jnp.zeros((states_all, states_all), jnp.float32))
    basis_flat, factor = lax.fori_loop(0, states_all // PANEL, panel_step, start_state)
    half_done = lax.linalg.triangular_solve(factor, moment, left_side=True, lower=True)
    projected = lax.linalg.triangular_solve(factor, half_done.T, left_side=True, lower=True).T
    basis_cells = basis_flat.reshape(cell_states.shape)
    states_out = lax.all_to_all(basis_cells, "blk", split_axis=0, concat_axis=3, tiled=True)
    owned = states_all // block_count
    projected_rows = lax.dynamic_slice_in_dim(projected, lax.axis_index("blk") * owned, owned, 0)
    return (states_out, projected_rows)


def per_device(states_in, region, *tables):
    known = (lax.axis_size("blk"), lax.axis_size("slab")) == (8, 4)
    run = fast if known and states_in.shape == (32, 8, 2, 1024) else general
    return run(states_in, region, *tables)


def solution(mesh):
    return jax.shard_map(
        per_device,
        mesh=mesh,
        in_specs=(P("blk", None, "slab", None), P("slab", None), P(), P(), P(), P()),
        out_specs=(P("blk", None, "slab", None), P("blk", None)),
        check_vma=False,
    )
```

```python
import functools

import jax
import jax.numpy as jnp
from jax import lax
from jax.experimental import pallas as pl
from jax.experimental.pallas import tpu as pltpu
from jax.sharding import PartitionSpec as P

BANDS = 8
MATERIALS = 4
PANEL = 32
SHIFT = 1.0
SCALE = 3.0
LANES = 128
ALL = ("blk", "slab")
LEFT = 4
WINDOW = 42
VMEM = pltpu.CompilerParams(vmem_limit_bytes=56 * 1024 * 1024)
HIGHEST = lax.Precision.HIGHEST
UNROLL = 3
OWN = slice(2 * 128 + 64, 18 * 128 + 64)


def dot(left, right, dims=((1,), (0,)), precision=None):
    return lax.dot_general(
        left, right, (dims, ((), ())), precision=precision, preferred_element_type=jnp.float32
    )


def split(value):
    high = value.astype(jnp.bfloat16)
    return high, (value - high.astype(jnp.float32)).astype(jnp.bfloat16)


def exchange(pieces, unit):
    count = len(pieces)
    lane = lax.broadcasted_iota(jnp.int32, pieces[0].shape, 1) // unit
    step = count // 2
    while step:
        low = (lane // step) % 2 == 0
        out = list(pieces)
        for i in range(count):
            if (i // step) % 2 == 0:
                a, c = pieces[i], pieces[i + step]
                out[i] = jnp.where(low, a, pltpu.roll(c, step * unit, 1))
                out[i + step] = jnp.where(low, pltpu.roll(a, LANES - step * unit, 1), c)
        pieces = out
        step //= 2
    return pieces


def pack_kernel(x_ref, o_ref, scr):
    scr[0 : LEFT * 4, :] = jnp.zeros((LEFT * 4, LANES), jnp.float32)
    tail = (LEFT + 1024) * 4
    scr[tail:, :] = jnp.zeros((scr.shape[0] - tail, LANES), jnp.float32)
    for tile in range(8):
        for r in range(4):
            row, high = r // 2, r % 2
            parts = [
                x_ref[pl.ds(((high * 4 + low) * 8 + tile) * 2 + row, 32, stride=128), :]
                for low in range(4)
            ]
            turned = jnp.concatenate(parts, axis=0).T
            scr[pl.ds((LEFT + 128 * tile) * 4 + r, 128, stride=4), :] = turned
    for d in range(32):
        o_ref[d] = scr[128 * d : 128 * d + WINDOW * 4, :]


def pack(x):
    rows = x.reshape(32, 8, 2, 8, LANES).transpose(0, 1, 3, 2, 4).reshape(4096, LANES)
    return pl.pallas_call(
        pack_kernel,
        out_shape=jax.ShapeDtypeStruct((32, WINDOW * 4, LANES), jnp.float32),
        scratch_shapes=[pltpu.VMEM((4136, LANES), jnp.float32)],
        compiler_params=VMEM,
        name="pack",
    )(rows)


def unpack_kernel(r_ref, o_ref):
    for tile in range(8):
        for r in range(4):
            row, high = r // 2, r % 2
            turned = r_ref[pl.ds(tile * 512 + r, 128, stride=4), :].T
            for low in range(4):
                o_ref[pl.ds(((high * 4 + low) * 8 + tile) * 2 + row, 32, stride=128), :] = turned[
                    32 * low : 32 * low + 32
                ]


def unpack(blocks):
    rows = pl.pallas_call(
        unpack_kernel,
        out_shape=jax.ShapeDtypeStruct((4096, LANES), jnp.float32),
        compiler_params=VMEM,
        name="unpack",
    )(blocks.reshape(4096, LANES))
    return rows.reshape(32, 8, 8, 2, LANES).transpose(0, 1, 3, 2, 4).reshape(32, 8, 2, 1024)


def coef_kernel(reg_ref, onsite_ref, hop_ref, kx_ref, ky_ref, ch_ref, cl_ref):
    def decode(index):
        band = (index % 2) * 4 + ((index // 32) % 2) * 2 + (index // 4) % 2
        x = ((index // 8) % 4) * 2 + (index // 2) % 2
        column = (index // 64) % 2
        return band, x, column

    def one_hot(values, shape, axis):
        return (values == lax.broadcasted_iota(jnp.int32, shape, axis)).astype(jnp.float32)

    b_r, x_r, y_r = decode(lax.broadcasted_iota(jnp.int32, (128, 8), 0))
    band_rows = one_hot(b_r, (128, 8), 1)
    b_c, _, _ = decode(lax.broadcasted_iota(jnp.int32, (8, 256), 1) + 64)
    band_cols = one_hot(b_c, (8, 256), 0)
    reg = reg_ref[...]
    hop = dot(band_rows, hop_ref[...], ((1,), (1,)), HIGHEST)

    def table_of(offset):
        return dot(one_hot(x_r + offset, (128, 8), 1), reg, precision=HIGHEST)

    def hops(codes):
        total = jnp.zeros_like(codes)
        for m in range(MATERIALS):
            total = total + jnp.where(codes == m + 1.0, hop[:, m : m + 1], 0.0)
        return total

    second = lax.broadcasted_iota(jnp.int32, (128, LANES), 0) >= 64

    def aligned(table):
        return jnp.where(second, pltpu.roll(table, LANES - 1, 1), table)

    codes = table_of(0)
    here, up, down = hops(codes), hops(table_of(-1)), hops(table_of(1))
    before, after = pltpu.roll(here, 1, 1), pltpu.roll(here, LANES - 1, 1)
    valid = (codes > 0.5).astype(jnp.float32)
    centre = (0.5 * (4.0 * here + up + down + before + after) - SHIFT) * valid
    fields = [aligned((codes == m + 1.0).astype(jnp.float32)) for m in range(MATERIALS)]
    fields += [aligned(valid), aligned(centre)]
    fields += [aligned(-0.5 * (here + side) * valid) for side in (up, down, before, after)]

    b_r, x_r, y_r = decode(lax.broadcasted_iota(jnp.int32, (128, 256), 0))
    k = lax.broadcasted_iota(jnp.int32, (128, 256), 1)
    b_c, x_c, _ = decode(k + 64)
    dy = k // 64 - 1 - y_r
    dx = x_c - x_r
    same = b_r == b_c

    def spread(matrix):
        return dot(dot(band_rows, matrix, precision=HIGHEST), band_cols, precision=HIGHEST)

    here_at, up_at, down_at = (dy == 0) & (dx == 0), (dy == 0) & (dx == -1), (dy == 0) & (dx == 1)
    before_at, after_at = (dy == -1) & (dx == 0), (dy == 1) & (dx == 0)
    onsite = [
        jnp.where(here_at, spread(0.5 * (onsite_ref[m] + onsite_ref[m].T)), 0.0) for m in range(MATERIALS)
    ]
    kx = spread(0.5 * (0.5 * (kx_ref[...] - kx_ref[...].T)))
    ky = spread(0.5 * (0.5 * (ky_ref[...] - ky_ref[...].T)))
    mixed = (
        jnp.where(down_at, kx, 0.0)
        - jnp.where(up_at, kx, 0.0)
        + jnp.where(after_at, ky, 0.0)
        - jnp.where(before_at, ky, 0.0)
    )
    places = [here_at & same, up_at & same, down_at & same, before_at & same, after_at & same]
    for pair in range(WINDOW // 2):
        lane = 2 * pair + 1
        scalar = [field[:, lane : lane + 1] for field in fields]
        value = scalar[4] * mixed
        for m in range(MATERIALS):
            value = value + scalar[m] * onsite[m]
        for place, weight in zip(places, scalar[5:]):
            value = value + jnp.where(place, weight, 0.0)
        high, low = split((2.0 / SCALE) * value)
        ch_ref[pair] = high
        cl_ref[pair] = low


def coefficients(reg, onsite_table, hop_table, coupling_x, coupling_y):
    shape = jax.ShapeDtypeStruct((WINDOW // 2, 128, 256), jnp.bfloat16)
    return pl.pallas_call(
        coef_kernel, out_shape=(shape, shape), compiler_params=VMEM, name="coefficients"
    )(reg, onsite_table, hop_table, coupling_x, coupling_y)


def halves(even, odd):
    even, odd = (value.reshape(-1, 8, LANES) for value in (even, odd))
    first = lax.broadcasted_iota(jnp.int32, (1, 8, LANES), 1) < 4
    return (
        jnp.where(first, even, pltpu.roll(odd, 4, 1)),
        jnp.where(first, pltpu.roll(even, 4, 1), odd),
    )


def filter_kernel(r_ref, ch_ref, cl_ref, vh_ref, vl_ref, g_ref, fa, fb, ah, al, bh, bl):
    pairs = WINDOW // 2
    block = 128
    edge = 64
    zero = jnp.zeros((edge, 256), jnp.bfloat16)
    for ref in (ah, al, bh, bl):
        ref[0:edge, :] = zero
        ref[pairs * block + edge :, :] = zero
    for slab in range(4):
        for half in range(2):
            lanes = slice(half * 128, half * 128 + 128)
            pieces = exchange([r_ref[(half * 4 + j) * 4 + slab] for j in range(4)], 32)
            for mid in range(2):
                for column, piece in enumerate(halves(pieces[2 * mid], pieces[2 * mid + 1])):
                    for pair in range(pairs):
                        at = pair * block + column * 64 + mid * 32 + slab * 8
                        fa[at : at + 8, lanes] = piece[pair]
    ah[edge : pairs * block + edge, :], al[edge : pairs * block + edge, :] = split(fa[...])

    def product(pair, high, low):
        rows = pl.ds(pair * block, 256)
        vh, vl = high[rows, :], low[rows, :]
        c_high, c_low = ch_ref[pair], cl_ref[pair]
        return dot(
            jnp.concatenate([c_high, c_high, c_low], axis=1), jnp.concatenate([vh, vl, vh], axis=0)
        )

    def store(pair, value, field, high, low):
        field[pl.ds(pair * block, block), :] = value
        rows = pl.ds(pair * block + edge, block)
        high[rows, :], low[rows, :] = split(value)

    def first(pair, carry):
        store(pair, 0.5 * product(pair, ah, al), fb, bh, bl)
        return carry

    lax.fori_loop(0, pairs, first, 0, unroll=UNROLL)

    def later(source_high, source_low, old, high, low):
        def body(pair, carry):
            rows = pl.ds(pair * block, block)
            store(pair, product(pair, source_high, source_low) - old[rows, :], old, high, low)
            return carry

        return body

    lax.fori_loop(1, pairs - 1, later(bh, bl, fa, ah, al), 0, unroll=UNROLL)
    lax.fori_loop(1, pairs - 1, later(ah, al, fb, bh, bl), 0, unroll=UNROLL)
    lax.fori_loop(2, pairs - 2, later(bh, bl, fa, ah, al), 0, unroll=UNROLL)
    vh_ref[...] = ah[...]
    vl_ref[...] = al[...]
    dims = ((0,), (0,))
    cross = dot(ah[OWN, :], al[OWN, :], dims)
    g_ref[...] = dot(ah[OWN, :], ah[OWN, :], dims) + (cross + cross.T)


def filtered_blocks(received, coef_high, coef_low):
    rows = (WINDOW // 2) * 128
    half = jax.ShapeDtypeStruct((rows + 128, 256), jnp.bfloat16)
    square = jax.ShapeDtypeStruct((256, 256), jnp.float32)
    return pl.pallas_call(
        filter_kernel,
        out_shape=(half, half, square),
        scratch_shapes=[pltpu.VMEM((rows, 256), jnp.float32)] * 2
        + [pltpu.VMEM((rows + 128, 256), jnp.bfloat16)] * 4,
        compiler_params=VMEM,
        name="filtered",
    )(received, coef_high, coef_low)


def moment_kernel(vh_ref, vl_ref, ch_ref, cl_ref, g_ref, m_ref, bh, bl):
    block, edge = 128, 64

    def image(pair, rows, drop=0):
        vh, vl = vh_ref[rows, :], vl_ref[rows, :]
        c_high, c_low = ch_ref[pair, :, drop:], cl_ref[pair, :, drop:]
        value = dot(
            jnp.concatenate([c_high, c_high, c_low], axis=1), jnp.concatenate([vh, vl, vh], axis=0)
        )
        at = pl.ds((pair - 2) * block, block)
        bh[at, :], bl[at, :] = split(value)

    def body(pair, carry):
        image(pair, pl.ds(pair * block, 256))
        return carry

    image(2, slice(2 * block + edge, 4 * block), edge)
    lax.fori_loop(3, 18, body, 0, unroll=3)
    rows = slice(18 * block, 18 * block + edge)
    c_high, c_low = ch_ref[18, 0:edge, 0:edge], cl_ref[18, 0:edge, 0:edge]
    value = dot(c_high, vh_ref[rows, :]) + (dot(c_high, vl_ref[rows, :]) + dot(c_low, vh_ref[rows, :]))
    bh[16 * block :, :], bl[16 * block :, :] = split(value)
    dims = ((0,), (0,))
    top = slice(OWN.start, OWN.stop + edge)
    high = vh_ref[top, :]
    moment = dot(high, bh[...], dims) + (dot(high, bl[...], dims) + dot(vl_ref[top, :], bh[...], dims))
    m_ref[...] = (0.5 * SCALE) * moment + SHIFT * g_ref[...]


def moment_of(vh, vl, coef_high, coef_low, gram):
    return pl.pallas_call(
        moment_kernel,
        out_shape=jax.ShapeDtypeStruct((256, 256), jnp.float32),
        scratch_shapes=[pltpu.VMEM((16 * 128 + 64, 256), jnp.bfloat16)] * 2,
        compiler_params=VMEM,
        cost_estimate=pl.CostEstimate(flops=int(4e9), transcendentals=0, bytes_accessed=int(1e7)),
        name="moment",
    )(vh, vl, coef_high, coef_low, gram)


def panel_inverse(block):
    row = lax.broadcasted_iota(jnp.int32, (8, LANES), 0)
    lane = lax.broadcasted_iota(jnp.int32, (8, LANES), 1)

    def spread(tile, k):
        return jnp.broadcast_to(tile[k % 8 : k % 8 + 1], (8, LANES))

    cols = [
        [jnp.broadcast_to(block[8 * t : 8 * t + 8, j : j + 1], (8, LANES)) for t in range(4)]
        for j in range(32)
    ]
    inverse = [(lane == row + 8 * t).astype(jnp.float32) for t in range(4)]
    pivots = [jnp.ones((8, LANES), jnp.float32) for t in range(4)]
    for k in range(32):
        own = k // 8
        pivot = spread(cols[k][own], k)
        pivots[own] = jnp.where(row == k % 8, pivot, pivots[own])
        scale = 1.0 / pivot
        ratio = {t: cols[k][t] * scale for t in range(own, 4)}
        ratio[own] = jnp.where(row > k % 8, ratio[own], 0.0)
        line = spread(inverse[own], k)
        for j in range(k + 1, 32):
            weight = spread(ratio[j // 8], j)
            for t in range(j // 8, 4):
                cols[j][t] = cols[j][t] - cols[k][t] * weight
        for t in range(own, 4):
            inverse[t] = inverse[t] - ratio[t] * line
    return jnp.concatenate([inverse[t] * lax.rsqrt(pivots[t]) for t in range(4)], axis=0)


def half_inverse(aug):
    def panel(p, carry):
        rows = pl.ds(pl.multiple_of(32 * p, 32), 32)
        lines = aug[rows, :]
        inverse = panel_inverse(pltpu.roll(lines[:, :LANES], LANES - 32 * p, 1))
        lines = dot(inverse[:, :32], lines, precision=HIGHEST)
        aug[rows, :] = lines
        lane = lax.broadcasted_iota(jnp.int32, (32, LANES), 1)
        upper = jnp.where(lane >= 32 * (p + 1), lines[:, :LANES], 0.0)
        aug[...] = aug[...] - dot(upper, lines, ((0,), (0,)), HIGHEST)
        return carry

    lax.fori_loop(0, 4, panel, 0)


def basis_kernel(entries, g_ref, vh_ref, vl_ref, w_ref, o_ref, aug, scr):
    row = lax.broadcasted_iota(jnp.int32, (LANES, LANES), 0)
    eye = (row == lax.broadcasted_iota(jnp.int32, (LANES, LANES), 1)).astype(jnp.float32)
    scale = 1.0 / entries
    aug[:, :LANES] = g_ref[:LANES, :LANES] * scale
    aug[:, LANES:] = eye
    half_inverse(aug)
    first = aug[:, LANES:]
    upper = dot(first, g_ref[:LANES, LANES:] * scale, precision=HIGHEST)
    aug[:, :LANES] = g_ref[LANES:, LANES:] * scale - dot(upper, upper, ((0,), (0,)), HIGHEST)
    aug[:, LANES:] = eye
    half_inverse(aug)
    second = aug[:, LANES:]
    corner = dot(upper, first, ((0,), (0,)), HIGHEST)
    w_ref[:LANES, :LANES] = first
    w_ref[:LANES, LANES:] = jnp.zeros((LANES, LANES), jnp.float32)
    w_ref[LANES:, :LANES] = -dot(second, corner, precision=HIGHEST)
    w_ref[LANES:, LANES:] = second
    wh, wl = split(w_ref[...])
    vh = vh_ref[OWN, :]
    scr[...] = dot(vh, wh, ((1,), (1,))) + (
        dot(vh, wl, ((1,), (1,))) + dot(vl_ref[OWN, :], wh, ((1,), (1,)))
    )
    for slab in range(4):
        for half in range(2):
            lanes = slice(half * 128, half * 128 + 128)
            pieces = []
            for mid in range(2):
                columns = []
                for column in range(2):
                    at = column * 64 + mid * 32 + slab * 8
                    columns.append(
                        jnp.concatenate(
                            [scr[pair * 128 + at : pair * 128 + at + 8, lanes] for pair in range(16)], axis=0
                        )
                    )
                pieces += [value.reshape(128, LANES) for value in halves(*columns)]
            for j, piece in enumerate(exchange(pieces, 32)):
                o_ref[(half * 4 + j) * 4 + slab] = piece


def basis(gram, entries, vh, vl):
    return pl.pallas_call(
        functools.partial(basis_kernel, entries),
        out_shape=(
            jax.ShapeDtypeStruct((256, 256), jnp.float32),
            jax.ShapeDtypeStruct((32, 128, LANES), jnp.float32),
        ),
        scratch_shapes=[pltpu.VMEM((LANES, 256), jnp.float32), pltpu.VMEM((2048, 256), jnp.float32)],
        compiler_params=VMEM,
        cost_estimate=pl.CostEstimate(flops=int(4e9), transcendentals=0, bytes_accessed=int(2e7)),
        name="basis",
    )(gram, vh, vl)


def parts_of(square):
    count = lax.axis_size(ALL)
    return square.reshape(count, -1, square.shape[1])


def swap(parts):
    return lax.all_to_all(parts, ALL, 0, 0, tiled=True)


def for_all(share):
    return jnp.broadcast_to(share[None], (lax.axis_size(ALL),) + share.shape)


def project_kernel(entries, moment_ref, w_ref, p_ref):
    first = pl.multiple_of(32 * lax.axis_index("blk"), 32)
    half_done = dot(w_ref[pl.ds(first, 32), :], moment_ref[...], precision=HIGHEST) * (1.0 / entries)
    p_ref[...] = dot(half_done, w_ref[...], ((1,), (1,)), HIGHEST)


def project(moment, inverse, entries):
    return pl.pallas_call(
        functools.partial(project_kernel, entries),
        out_shape=jax.ShapeDtypeStruct((32, 256), jnp.float32),
        compiler_params=VMEM,
        name="project",
    )(moment, inverse)


def fast(states_in, region, onsite_table, hop_table, coupling_x, coupling_y):
    device = lax.axis_index("blk") * lax.axis_size("slab") + lax.axis_index("slab")
    entries = float(BANDS * 8 * 1024)
    codes = lax.all_gather((region + 1).astype(jnp.float32), "slab", axis=0, tiled=True)
    received = swap(pack(states_in))
    codes = jnp.pad(codes, ((0, 0), (LEFT + 1, LANES)))
    codes = lax.dynamic_slice(codes, (0, 32 * device), (8, LANES))
    coef_high, coef_low = coefficients(codes, onsite_table, hop_table, coupling_x, coupling_y)
    vh, vl, own_gram = filtered_blocks(received, coef_high, coef_low)
    own_moment = moment_of(vh, vl, coef_high, coef_low, own_gram)
    share = swap(parts_of(own_gram)).sum(0)
    both = swap(jnp.concatenate([for_all(share), parts_of(own_moment)], axis=1))
    inverse, blocks = basis(both[:, :8].reshape(256, 256), entries, vh, vl)
    moment = swap(for_all(both[:, 8:].sum(0))).reshape(256, 256)
    blocks, moment = lax.optimization_barrier((blocks, moment))
    states_out = unpack(swap(blocks))
    projected = project(moment, inverse, entries)
    return states_out, projected


DEGREE = 4


def extended(array, sides, width):
    for axis, dim in sides:
        size, length = (lax.axis_size(axis), array.shape[dim])
        up = [(i, (i + 1) % size) for i in range(size - 1)]
        down = [(j, i) for i, j in up]
        last = lax.slice_in_dim(array, length - width, length, axis=dim)
        leading = lax.slice_in_dim(array, 0, width, axis=dim)
        before = lax.ppermute(last, axis, up)
        after = lax.ppermute(leading, axis, down)
        array = jnp.concatenate([before, array, after], axis=dim)
    return array


def mixing(onsite_table, coupling_x, coupling_y):
    onsite = 0.5 * (onsite_table + jnp.swapaxes(onsite_table, 1, 2))
    blocks = [onsite[material] for material in range(onsite.shape[0])]
    return jnp.concatenate(
        blocks + [0.5 * (coupling_x - coupling_x.T), 0.5 * (coupling_y - coupling_y.T)], axis=1
    )


def masks_of(region):
    codes = jnp.arange(MATERIALS, dtype=jnp.int32)
    return (region[None] == codes[:, None, None]).astype(jnp.float32)


def apply_padded(padded, hop_padded, material_masks, mixing_matrix):
    centre = padded[:, :, 1:-1, 1:-1]
    hop_centre = hop_padded[:, 1:-1, 1:-1]
    kinetic = jnp.zeros_like(centre)
    sides = (
        (padded[:, :, 2:, 1:-1], hop_padded[:, 2:, 1:-1]),
        (padded[:, :, :-2, 1:-1], hop_padded[:, :-2, 1:-1]),
        (padded[:, :, 1:-1, 2:], hop_padded[:, 1:-1, 2:]),
        (padded[:, :, 1:-1, :-2], hop_padded[:, 1:-1, :-2]),
    )
    for field_side, hop_side in sides:
        kinetic = kinetic + (0.5 * (hop_centre + hop_side))[None] * (centre - field_side)
    deriv_rows = 0.5 * (padded[:, :, 2:, 1:-1] - padded[:, :, :-2, 1:-1])
    deriv_cols = 0.5 * (padded[:, :, 1:-1, 2:] - padded[:, :, 1:-1, :-2])
    pieces = [
        material_masks[material][None, None] * centre for material in range(material_masks.shape[0])
    ]
    stacked = jnp.concatenate(pieces + [deriv_rows, deriv_cols], axis=1)
    mixed = jnp.einsum("bc,scxy->sbxy", mixing_matrix, stacked, precision=lax.Precision.HIGHEST)
    return mixed + kinetic


def chebyshev(field, apply_fn):

    def scaled(value):
        return (apply_fn(value) - SHIFT * value) / SCALE

    previous = field
    current = scaled(field)
    for repeat in range(DEGREE - 1):
        previous, current = (current, 2.0 * scaled(current) - previous)
    return current


def inner(left, right):
    return jnp.dot(
        left, right.T, precision=lax.Precision.HIGHEST, preferred_element_type=jnp.float32
    )


def general(states_in, region, onsite_table, hop_table, coupling_x, coupling_y):
    mixing_matrix = mixing(onsite_table, coupling_x, coupling_y)
    material_masks = masks_of(region)
    hop_field = jnp.einsum(
        "mb,mxy->bxy", hop_table, material_masks, precision=lax.Precision.HIGHEST
    )
    hop_rows = extended(hop_field, (("slab", 1),), 1)
    hop_padded = jnp.pad(hop_rows, ((0, 0), (0, 0), (1, 1)))

    def apply_rows(field):
        padded = extended(field, (("slab", 2),), 1)
        padded = jnp.pad(padded, ((0, 0), (0, 0), (0, 0), (1, 1)))
        return apply_padded(padded, hop_padded, material_masks, mixing_matrix)

    filtered = chebyshev(states_in, apply_rows)
    block_count = lax.axis_size("blk")
    slab_count = lax.axis_size("slab")
    states_all = filtered.shape[0] * block_count
    row_count = filtered.shape[2]
    width_all = filtered.shape[3]
    entries = float(BANDS * row_count * slab_count * width_all)
    image = apply_rows(filtered)
    cell_states, cell_image = (
        lax.all_to_all(filtered, "blk", split_axis=3, concat_axis=0, tiled=True),
        lax.all_to_all(image, "blk", split_axis=3, concat_axis=0, tiled=True),
    )
    states_flat = cell_states.reshape(states_all, -1)
    image_flat = cell_image.reshape(states_all, -1)
    moment = lax.psum(inner(states_flat, image_flat) / entries, ("blk", "slab"))

    def panel_step(panel, carry):
        basis_rows, factor_rows = carry
        offset = panel * PANEL
        panel_states = lax.dynamic_slice_in_dim(states_flat, offset, PANEL, 0)
        coeffs = lax.psum(inner(basis_rows, panel_states) / entries, ("blk", "slab"))
        residue = panel_states - jnp.dot(
            coeffs.T,
            basis_rows,
            precision=lax.Precision.HIGHEST,
            preferred_element_type=jnp.float32,
        )
        panel_gram = lax.psum(inner(residue, residue) / entries, ("blk", "slab"))
        panel_factor = jnp.linalg.cholesky(panel_gram)
        panel_basis = lax.linalg.triangular_solve(panel_factor, residue, left_side=True, lower=True)
        basis_rows = lax.dynamic_update_slice_in_dim(basis_rows, panel_basis, offset, 0)
        factor_row = lax.dynamic_update_slice_in_dim(coeffs.T, panel_factor, offset, 1)
        factor_rows = lax.dynamic_update_slice_in_dim(factor_rows, factor_row, offset, 0)
        return (basis_rows, factor_rows)

    start_state = (jnp.zeros_like(states_flat), jnp.zeros((states_all, states_all), jnp.float32))
    basis_flat, factor = lax.fori_loop(0, states_all // PANEL, panel_step, start_state)
    half_done = lax.linalg.triangular_solve(factor, moment, left_side=True, lower=True)
    projected = lax.linalg.triangular_solve(factor, half_done.T, left_side=True, lower=True).T
    basis_cells = basis_flat.reshape(cell_states.shape)
    states_out = lax.all_to_all(basis_cells, "blk", split_axis=0, concat_axis=3, tiled=True)
    owned = states_all // block_count
    projected_rows = lax.dynamic_slice_in_dim(projected, lax.axis_index("blk") * owned, owned, 0)
    return (states_out, projected_rows)


def per_device(states_in, region, *tables):
    known = (lax.axis_size("blk"), lax.axis_size("slab")) == (8, 4)
    run = fast if known and states_in.shape == (32, 8, 2, 1024) else general
    return run(states_in, region, *tables)


def solution(mesh):
    return jax.shard_map(
        per_device,
        mesh=mesh,
        in_specs=(P("blk", None, "slab", None), P("slab", None), P(), P(), P(), P()),
        out_specs=(P("blk", None, "slab", None), P("blk", None)),
        check_vma=False,
    )
```

```python
import functools

import jax
import jax.numpy as jnp
from jax import lax
from jax.experimental import pallas as pl
from jax.experimental.pallas import tpu as pltpu
from jax.sharding import PartitionSpec as P

BANDS = 8
MATERIALS = 4
PANEL = 32
SHIFT = 1.0
SCALE = 3.0
LANES = 128
ALL = ("blk", "slab")
LEFT = 4
WINDOW = 42
VMEM = pltpu.CompilerParams(vmem_limit_bytes=24 * 1024 * 1024)
ON_CHIP = pl.BlockSpec(memory_space=pltpu.VMEM)
OFF_CHIP = pl.BlockSpec(memory_space=pltpu.HBM)
HIGHEST = lax.Precision.HIGHEST
UNROLL = 7
OWN = slice(2 * 128 + 64, 18 * 128 + 64)


def off_chip(*arrays):
    return [pltpu.with_memory_space_constraint(array, pltpu.HBM) for array in arrays]


def dot(left, right, dims=((1,), (0,)), precision=None):
    return lax.dot_general(
        left, right, (dims, ((), ())), precision=precision, preferred_element_type=jnp.float32
    )


def split(value):
    high = value.astype(jnp.bfloat16)
    return high, (value - high.astype(jnp.float32)).astype(jnp.bfloat16)


def exchange(pieces, unit):
    count = len(pieces)
    lane = lax.broadcasted_iota(jnp.int32, pieces[0].shape, 1) // unit
    step = count // 2
    while step:
        low = (lane // step) % 2 == 0
        out = list(pieces)
        for i in range(count):
            if (i // step) % 2 == 0:
                a, c = pieces[i], pieces[i + step]
                out[i] = jnp.where(low, a, pltpu.roll(c, step * unit, 1))
                out[i + step] = jnp.where(low, pltpu.roll(a, LANES - step * unit, 1), c)
        pieces = out
        step //= 2
    return pieces


def pack_kernel(x_ref, o_ref, buf, scr, in_sem, out_sem):
    loads = [
        pltpu.make_async_copy(x_ref.at[:, pl.ds(8 * part, 8), :], buf.at[part], in_sem.at[part])
        for part in range(2)
    ]
    for load in loads:
        load.start()
    scr[0 : LEFT * 4, :] = jnp.zeros((LEFT * 4, LANES), jnp.float32)
    tail = (LEFT + 1024) * 4
    scr[tail:, :] = jnp.zeros((scr.shape[0] - tail, LANES), jnp.float32)
    sends = [
        pltpu.make_async_copy(scr.at[pl.ds(128 * d, WINDOW * 4), :], o_ref.at[d], out_sem.at[d])
        for d in range(32)
    ]
    for part in range(2):
        loads[part].wait()
        rows = buf.at[part].reshape(2048, LANES)
        for tile in range(4):
            for r in range(4):
                row, high = r // 2, r % 2
                parts = [
                    rows[pl.ds((high * 4 + low) * 8 + tile * 2 + row, 32, stride=64), :]
                    for low in range(4)
                ]
                turned = jnp.concatenate(parts, axis=0).T
                scr[pl.ds((LEFT + 512 * part + 128 * tile) * 4 + r, 128, stride=4), :] = turned
        for send in sends[15 * part : 15 + 17 * part]:
            send.start()
    for send in sends:
        send.wait()


def pack(x):
    rows = x.reshape(32, 8, 2, 8, LANES).transpose(0, 1, 3, 2, 4).reshape(256, 16, LANES)
    return pl.pallas_call(
        pack_kernel,
        out_shape=pltpu.HBM((32, WINDOW * 4, LANES), jnp.float32),
        in_specs=[OFF_CHIP],
        out_specs=OFF_CHIP,
        scratch_shapes=[
            pltpu.VMEM((2, 256, 8, LANES), jnp.float32),
            pltpu.VMEM((4136, LANES), jnp.float32),
            pltpu.SemaphoreType.DMA((2,)),
            pltpu.SemaphoreType.DMA((32,)),
        ],
        compiler_params=VMEM,
        name="pack",
    )(*off_chip(rows))


def unpack_kernel(r_ref, o_ref, buf, sem):
    stores = []
    for high in range(2):
        rows = buf.at[high].reshape(2048, LANES)
        for tile in range(8):
            for row in range(2):
                turned = r_ref[pl.ds(tile * 512 + row * 2 + high, 128, stride=4), :].T
                for low in range(4):
                    rows[pl.ds((low * 8 + tile) * 2 + row, 32, stride=64), :] = turned[
                        32 * low : 32 * low + 32
                    ]
        stores.append(
            pltpu.make_async_copy(buf.at[high], o_ref.at[:, pl.ds(64 * high, 64), :], sem.at[high])
        )
        stores[high].start()
    for store in stores:
        store.wait()


def unpack(blocks):
    rows = pl.pallas_call(
        unpack_kernel,
        out_shape=pltpu.HBM((32, 128, LANES), jnp.float32),
        in_specs=[ON_CHIP],
        out_specs=OFF_CHIP,
        scratch_shapes=[pltpu.VMEM((2, 32, 64, LANES), jnp.float32), pltpu.SemaphoreType.DMA((2,))],
        compiler_params=VMEM,
        name="unpack",
    )(blocks.reshape(4096, LANES))
    return rows.reshape(32, 8, 8, 2, LANES).transpose(0, 1, 3, 2, 4).reshape(32, 8, 2, 1024)


def coef_kernel(reg_ref, onsite_ref, hop_ref, kx_ref, ky_ref, ch_ref, cl_ref):
    def decode(index):
        band = (index % 2) * 4 + ((index // 32) % 2) * 2 + (index // 4) % 2
        x = ((index // 8) % 4) * 2 + (index // 2) % 2
        column = (index // 64) % 2
        return band, x, column

    def one_hot(values, shape, axis):
        return (values == lax.broadcasted_iota(jnp.int32, shape, axis)).astype(jnp.float32)

    b_r, x_r, y_r = decode(lax.broadcasted_iota(jnp.int32, (128, 8), 0))
    band_rows = one_hot(b_r, (128, 8), 1)
    b_c, _, _ = decode(lax.broadcasted_iota(jnp.int32, (8, 256), 1) + 64)
    band_cols = one_hot(b_c, (8, 256), 0)
    reg = reg_ref[...]
    hop = dot(band_rows, hop_ref[...], ((1,), (1,)), HIGHEST)

    def table_of(offset):
        return dot(one_hot(x_r + offset, (128, 8), 1), reg, precision=HIGHEST)

    def hops(codes):
        total = jnp.zeros_like(codes)
        for m in range(MATERIALS):
            total = total + jnp.where(codes == m + 1.0, hop[:, m : m + 1], 0.0)
        return total

    second = lax.broadcasted_iota(jnp.int32, (128, LANES), 0) >= 64

    def aligned(table):
        return jnp.where(second, pltpu.roll(table, LANES - 1, 1), table)

    codes = table_of(0)
    here, up, down = hops(codes), hops(table_of(-1)), hops(table_of(1))
    before, after = pltpu.roll(here, 1, 1), pltpu.roll(here, LANES - 1, 1)
    valid = (codes > 0.5).astype(jnp.float32)
    centre = (0.5 * (4.0 * here + up + down + before + after) - SHIFT) * valid
    fields = [aligned((codes == m + 1.0).astype(jnp.float32)) for m in range(MATERIALS)]
    fields += [aligned(valid), aligned(centre)]
    fields += [aligned(-0.5 * (here + side) * valid) for side in (up, down, before, after)]

    b_r, x_r, y_r = decode(lax.broadcasted_iota(jnp.int32, (128, 256), 0))
    k = lax.broadcasted_iota(jnp.int32, (128, 256), 1)
    b_c, x_c, _ = decode(k + 64)
    dy = k // 64 - 1 - y_r
    dx = x_c - x_r
    same = b_r == b_c

    def spread(matrix):
        return dot(dot(band_rows, matrix, precision=HIGHEST), band_cols, precision=HIGHEST)

    here_at, up_at, down_at = (dy == 0) & (dx == 0), (dy == 0) & (dx == -1), (dy == 0) & (dx == 1)
    before_at, after_at = (dy == -1) & (dx == 0), (dy == 1) & (dx == 0)
    onsite = [
        jnp.where(here_at, spread(0.5 * (onsite_ref[m] + onsite_ref[m].T)), 0.0) for m in range(MATERIALS)
    ]
    kx = spread(0.5 * (0.5 * (kx_ref[...] - kx_ref[...].T)))
    ky = spread(0.5 * (0.5 * (ky_ref[...] - ky_ref[...].T)))
    mixed = (
        jnp.where(down_at, kx, 0.0)
        - jnp.where(up_at, kx, 0.0)
        + jnp.where(after_at, ky, 0.0)
        - jnp.where(before_at, ky, 0.0)
    )
    places = [here_at & same, up_at & same, down_at & same, before_at & same, after_at & same]
    for pair in range(WINDOW // 2):
        lane = 2 * pair + 1
        scalar = [field[:, lane : lane + 1] for field in fields]
        value = scalar[4] * mixed
        for m in range(MATERIALS):
            value = value + scalar[m] * onsite[m]
        for place, weight in zip(places, scalar[5:]):
            value = value + jnp.where(place, weight, 0.0)
        high, low = split((2.0 / SCALE) * value)
        ch_ref[pair] = high
        cl_ref[pair] = low


def coefficients(reg, onsite_table, hop_table, coupling_x, coupling_y):
    shape = pltpu.HBM((WINDOW // 2, 128, 256), jnp.bfloat16)
    return pl.pallas_call(
        coef_kernel,
        out_shape=(shape, shape),
        compiler_params=VMEM,
        name="coefficients",
    )(reg, onsite_table, hop_table, coupling_x, coupling_y)


def halves(even, odd):
    even, odd = (value.reshape(-1, 8, LANES) for value in (even, odd))
    first = lax.broadcasted_iota(jnp.int32, (1, 8, LANES), 1) < 4
    return (
        jnp.where(first, even, pltpu.roll(odd, 4, 1)),
        jnp.where(first, pltpu.roll(even, 4, 1), odd),
    )


def filter_kernel(
    r_ref, ch_hbm, cl_hbm, vh_hbm, vl_hbm, g_ref, ch_ref, cl_ref, fa, fb, ah, al, bh, bl, sem
):
    loads = [
        pltpu.make_async_copy(ch_hbm, ch_ref, sem.at[0]),
        pltpu.make_async_copy(cl_hbm, cl_ref, sem.at[1]),
    ]
    for load in loads:
        load.start()
    pairs = WINDOW // 2
    block = 128
    edge = 64
    zero = jnp.zeros((edge, 256), jnp.bfloat16)
    for ref in (ah, al, bh, bl):
        ref[0:edge, :] = zero
        ref[pairs * block + edge :, :] = zero
    def ingest(pair, carry):
        at = pl.multiple_of(pair * block, block)
        source = pl.ds(pl.multiple_of(pair * 8, 8), 8)
        for half in range(2):
            lanes = slice(half * 128, half * 128 + 128)
            for slab in range(4):
                pieces = exchange([r_ref[(half * 4 + j) * 4 + slab, source, :] for j in range(4)], 32)
                for mid in range(2):
                    for column, piece in enumerate(halves(pieces[2 * mid], pieces[2 * mid + 1])):
                        fa[pl.ds(at + (column * 64 + mid * 32 + slab * 8), 8), lanes] = piece[0]
        rows = pl.ds(at + edge, block)
        ah[rows, :], al[rows, :] = split(fa[pl.ds(at, block), :])
        return carry

    lax.fori_loop(0, pairs, ingest, 0, unroll=3)
    for load in loads:
        load.wait()

    def product(pair, high, low):
        rows = pl.ds(pair * block, 256)
        vh, vl = high[rows, :], low[rows, :]
        c_high, c_low = ch_ref[pair], cl_ref[pair]
        return dot(
            jnp.concatenate([c_high, c_high, c_low], axis=1), jnp.concatenate([vh, vl, vh], axis=0)
        )

    def store(pair, value, field, high, low):
        field[pl.ds(pair * block, block), :] = value
        rows = pl.ds(pair * block + edge, block)
        high[rows, :], low[rows, :] = split(value)

    def first(pair, carry):
        store(pair, 0.5 * product(pair, ah, al), fb, bh, bl)
        return carry

    lax.fori_loop(0, pairs, first, 0, unroll=UNROLL)

    def later(source_high, source_low, old, high, low):
        def body(pair, carry):
            rows = pl.ds(pair * block, block)
            store(pair, product(pair, source_high, source_low) - old[rows, :], old, high, low)
            return carry

        return body

    lax.fori_loop(1, pairs - 1, later(bh, bl, fa, ah, al), 0, unroll=UNROLL)
    lax.fori_loop(1, pairs - 1, later(ah, al, fb, bh, bl), 0, unroll=UNROLL)
    lax.fori_loop(2, pairs - 2, later(bh, bl, fa, ah, al), 0, unroll=UNROLL)
    stores = [
        pltpu.make_async_copy(ah, vh_hbm, sem.at[2]),
        pltpu.make_async_copy(al, vl_hbm, sem.at[3]),
    ]
    for store_out in stores:
        store_out.start()
    dims = ((0,), (0,))
    cross = dot(ah[OWN, :], al[OWN, :], dims)
    g_ref[...] = dot(ah[OWN, :], ah[OWN, :], dims) + (cross + cross.T)
    for store_out in stores:
        store_out.wait()


def filtered_blocks(received, coef_high, coef_low):
    rows = (WINDOW // 2) * 128
    half = pltpu.HBM((rows + 128, 256), jnp.bfloat16)
    square = jax.ShapeDtypeStruct((256, 256), jnp.float32)
    return pl.pallas_call(
        filter_kernel,
        out_shape=(half, half, square),
        scratch_shapes=[pltpu.VMEM((WINDOW // 2, 128, 256), jnp.bfloat16)] * 2
        + [pltpu.VMEM((rows, 256), jnp.float32)] * 2
        + [pltpu.VMEM((rows + 128, 256), jnp.bfloat16)] * 4
        + [pltpu.SemaphoreType.DMA((4,))],
        in_specs=[ON_CHIP, OFF_CHIP, OFF_CHIP],
        out_specs=(OFF_CHIP, OFF_CHIP, ON_CHIP),
        compiler_params=VMEM,
        name="filtered",
    )(received, *off_chip(coef_high, coef_low))


def moment_kernel(vh_ref, vl_ref, ch_ref, cl_ref, g_ref, m_ref, bh, bl):
    block, edge = 128, 64

    def image(pair, rows, drop=0):
        vh, vl = vh_ref[rows, :], vl_ref[rows, :]
        c_high, c_low = ch_ref[pair, :, drop:], cl_ref[pair, :, drop:]
        value = dot(
            jnp.concatenate([c_high, c_high, c_low], axis=1), jnp.concatenate([vh, vl, vh], axis=0)
        )
        at = pl.ds((pair - 2) * block, block)
        bh[at, :], bl[at, :] = split(value)

    def body(pair, carry):
        image(pair, pl.ds(pair * block, 256))
        return carry

    image(2, slice(2 * block + edge, 4 * block), edge)
    lax.fori_loop(3, 18, body, 0, unroll=3)
    rows = slice(18 * block, 18 * block + edge)
    c_high, c_low = ch_ref[18, 0:edge, 0:edge], cl_ref[18, 0:edge, 0:edge]
    value = dot(c_high, vh_ref[rows, :]) + (dot(c_high, vl_ref[rows, :]) + dot(c_low, vh_ref[rows, :]))
    bh[16 * block :, :], bl[16 * block :, :] = split(value)
    dims = ((0,), (0,))
    top = slice(OWN.start, OWN.stop + edge)
    high = vh_ref[top, :]
    moment = dot(high, bh[...], dims) + (dot(high, bl[...], dims) + dot(vl_ref[top, :], bh[...], dims))
    m_ref[...] = (0.5 * SCALE) * moment + SHIFT * g_ref[...]


def moment_of(vh, vl, coef_high, coef_low, gram):
    return pl.pallas_call(
        moment_kernel,
        out_shape=jax.ShapeDtypeStruct((256, 256), jnp.float32),
        scratch_shapes=[pltpu.VMEM((16 * 128 + 64, 256), jnp.bfloat16)] * 2,
        compiler_params=VMEM,
        cost_estimate=pl.CostEstimate(flops=int(4e9), transcendentals=0, bytes_accessed=int(1e7)),
        name="moment",
    )(*off_chip(vh, vl, coef_high, coef_low), gram)


def panel_inverse(block):
    row = lax.broadcasted_iota(jnp.int32, (8, LANES), 0)
    lane = lax.broadcasted_iota(jnp.int32, (8, LANES), 1)

    def spread(tile, k):
        return jnp.broadcast_to(tile[k % 8 : k % 8 + 1], (8, LANES))

    cols = [
        [jnp.broadcast_to(block[8 * t : 8 * t + 8, j : j + 1], (8, LANES)) for t in range(4)]
        for j in range(32)
    ]
    inverse = [(lane == row + 8 * t).astype(jnp.float32) for t in range(4)]
    pivots = [jnp.ones((8, LANES), jnp.float32) for t in range(4)]
    for k in range(32):
        own = k // 8
        pivot = spread(cols[k][own], k)
        pivots[own] = jnp.where(row == k % 8, pivot, pivots[own])
        scale = 1.0 / pivot
        ratio = {t: cols[k][t] * scale for t in range(own, 4)}
        ratio[own] = jnp.where(row > k % 8, ratio[own], 0.0)
        line = spread(inverse[own], k)
        for j in range(k + 1, 32):
            weight = spread(ratio[j // 8], j)
            for t in range(j // 8, 4):
                cols[j][t] = cols[j][t] - cols[k][t] * weight
        for t in range(own, 4):
            inverse[t] = inverse[t] - ratio[t] * line
    return jnp.concatenate([inverse[t] * lax.rsqrt(pivots[t]) for t in range(4)], axis=0)


def half_inverse(aug):
    def panel(p, carry):
        rows = pl.ds(pl.multiple_of(32 * p, 32), 32)
        lines = aug[rows, :]
        inverse = panel_inverse(pltpu.roll(lines[:, :LANES], LANES - 32 * p, 1))
        lines = dot(inverse[:, :32], lines, precision=HIGHEST)
        aug[rows, :] = lines
        lane = lax.broadcasted_iota(jnp.int32, (32, LANES), 1)
        upper = jnp.where(lane >= 32 * (p + 1), lines[:, :LANES], 0.0)
        aug[...] = aug[...] - dot(upper, lines, ((0,), (0,)), HIGHEST)
        return carry

    lax.fori_loop(0, 4, panel, 0)


def basis_kernel(entries, both_ref, vh_hbm, vl_hbm, w_ref, o_hbm, gram, aug, vh, vl, scr, out, sem, out_sem):
    loads = [
        pltpu.make_async_copy(vh_hbm.at[OWN, :], vh, sem.at[0]),
        pltpu.make_async_copy(vl_hbm.at[OWN, :], vl, sem.at[1]),
    ]
    for load in loads:
        load.start()
    row = lax.broadcasted_iota(jnp.int32, (LANES, LANES), 0)
    eye = (row == lax.broadcasted_iota(jnp.int32, (LANES, LANES), 1)).astype(jnp.float32)
    gram[...] = both_ref[:, 0:8, :].reshape(256, 256) * (1.0 / entries)
    aug[:, :LANES] = gram[:LANES, :LANES]
    aug[:, LANES:] = eye
    half_inverse(aug)
    first = aug[:, LANES:]
    upper = dot(first, gram[:LANES, LANES:], precision=HIGHEST)
    aug[:, :LANES] = gram[LANES:, LANES:] - dot(upper, upper, ((0,), (0,)), HIGHEST)
    aug[:, LANES:] = eye
    corner = dot(upper, first, ((0,), (0,)), HIGHEST)
    half_inverse(aug)
    second = aug[:, LANES:]
    w_ref[:LANES, :LANES] = first
    w_ref[:LANES, LANES:] = jnp.zeros((LANES, LANES), jnp.float32)
    w_ref[LANES:, :LANES] = -dot(second, corner, precision=HIGHEST)
    w_ref[LANES:, LANES:] = second
    for load in loads:
        load.wait()
    sends = [pltpu.make_async_copy(out.at[d], o_hbm.at[d], out_sem.at[d]) for d in range(32)]
    for half in range(2):
        used = LANES * (half + 1)
        wh, wl = split(w_ref[LANES * half : used, :used])
        values = [vh[:, :used], vl[:, :used], vh[:, :used]]
        scr[...] = dot(
            jnp.concatenate(values, axis=1), jnp.concatenate([wh, wh, wl], axis=1), ((1,), (1,))
        )
        for slab in range(4):
            pieces = []
            for mid in range(2):
                columns = []
                for column in range(2):
                    at = column * 64 + mid * 32 + slab * 8
                    columns.append(
                        jnp.concatenate(
                            [scr[pair * 128 + at : pair * 128 + at + 8, :] for pair in range(16)], axis=0
                        )
                    )
                pieces += [value.reshape(128, LANES) for value in halves(*columns)]
            for j, piece in enumerate(exchange(pieces, 32)):
                d = (half * 4 + j) * 4 + slab
                out[d] = piece
                sends[d].start()
    for send in sends:
        send.wait()


def basis(both, entries, vh, vl):
    return pl.pallas_call(
        functools.partial(basis_kernel, entries),
        out_shape=(
            jax.ShapeDtypeStruct((256, 256), jnp.float32),
            pltpu.HBM((32, 128, LANES), jnp.float32),
        ),
        in_specs=[ON_CHIP, OFF_CHIP, OFF_CHIP],
        out_specs=(ON_CHIP, OFF_CHIP),
        scratch_shapes=[
            pltpu.VMEM((256, 256), jnp.float32),
            pltpu.VMEM((LANES, 256), jnp.float32),
            pltpu.VMEM((2048, 256), jnp.bfloat16),
            pltpu.VMEM((2048, 256), jnp.bfloat16),
            pltpu.VMEM((2048, LANES), jnp.float32),
            pltpu.VMEM((32, LANES, LANES), jnp.float32),
            pltpu.SemaphoreType.DMA((2,)),
            pltpu.SemaphoreType.DMA((32,)),
        ],
        compiler_params=VMEM,
        cost_estimate=pl.CostEstimate(flops=int(4e9), transcendentals=0, bytes_accessed=int(2e7)),
        name="basis",
    )(both, *off_chip(vh, vl))


def parts_of(square):
    count = lax.axis_size(ALL)
    return square.reshape(count, -1, square.shape[1])


def swap(parts):
    return lax.all_to_all(parts, ALL, 0, 0, tiled=True)


def for_all(share):
    return jnp.broadcast_to(share[None], (lax.axis_size(ALL),) + share.shape)


def project_kernel(entries, moment_ref, w_ref, p_ref):
    first = pl.multiple_of(32 * lax.axis_index("blk"), 32)
    half_done = dot(w_ref[pl.ds(first, 32), :], moment_ref[...], precision=HIGHEST) * (1.0 / entries)
    p_ref[...] = dot(half_done, w_ref[...], ((1,), (1,)), HIGHEST)


def project(moment, inverse, entries):
    return pl.pallas_call(
        functools.partial(project_kernel, entries),
        out_shape=jax.ShapeDtypeStruct((32, 256), jnp.float32),
        in_specs=[ON_CHIP] * 2,
        out_specs=ON_CHIP,
        compiler_params=VMEM,
        name="project",
    )(moment, inverse)


def fast(states_in, region, onsite_table, hop_table, coupling_x, coupling_y):
    device = lax.axis_index("blk") * lax.axis_size("slab") + lax.axis_index("slab")
    entries = float(BANDS * 8 * 1024)
    codes = lax.all_gather((region + 1).astype(jnp.float32), "slab", axis=0, tiled=True)
    received = swap(pack(states_in))
    codes = jnp.pad(codes, ((0, 0), (LEFT + 1, LANES)))
    codes = lax.dynamic_slice(codes, (0, 32 * device), (8, LANES))
    coef_high, coef_low = coefficients(codes, onsite_table, hop_table, coupling_x, coupling_y)
    vh, vl, own_gram = filtered_blocks(received, coef_high, coef_low)
    own_moment = moment_of(vh, vl, coef_high, coef_low, own_gram)
    share = swap(parts_of(own_gram)).sum(0)
    both = swap(jnp.concatenate([for_all(share), parts_of(own_moment)], axis=1))
    inverse, blocks = basis(both, entries, vh, vl)
    moment = swap(for_all(both[:, 8:].sum(0))).reshape(256, 256)
    blocks, moment = lax.optimization_barrier((blocks, moment))
    states_out = unpack(swap(blocks))
    projected = project(moment, inverse, entries)
    return states_out, projected


DEGREE = 4


def extended(array, sides, width):
    for axis, dim in sides:
        size, length = (lax.axis_size(axis), array.shape[dim])
        up = [(i, (i + 1) % size) for i in range(size - 1)]
        down = [(j, i) for i, j in up]
        last = lax.slice_in_dim(array, length - width, length, axis=dim)
        leading = lax.slice_in_dim(array, 0, width, axis=dim)
        before = lax.ppermute(last, axis, up)
        after = lax.ppermute(leading, axis, down)
        array = jnp.concatenate([before, array, after], axis=dim)
    return array


def mixing(onsite_table, coupling_x, coupling_y):
    onsite = 0.5 * (onsite_table + jnp.swapaxes(onsite_table, 1, 2))
    blocks = [onsite[material] for material in range(onsite.shape[0])]
    return jnp.concatenate(
        blocks + [0.5 * (coupling_x - coupling_x.T), 0.5 * (coupling_y - coupling_y.T)], axis=1
    )


def masks_of(region):
    codes = jnp.arange(MATERIALS, dtype=jnp.int32)
    return (region[None] == codes[:, None, None]).astype(jnp.float32)


def apply_padded(padded, hop_padded, material_masks, mixing_matrix):
    centre = padded[:, :, 1:-1, 1:-1]
    hop_centre = hop_padded[:, 1:-1, 1:-1]
    kinetic = jnp.zeros_like(centre)
    sides = (
        (padded[:, :, 2:, 1:-1], hop_padded[:, 2:, 1:-1]),
        (padded[:, :, :-2, 1:-1], hop_padded[:, :-2, 1:-1]),
        (padded[:, :, 1:-1, 2:], hop_padded[:, 1:-1, 2:]),
        (padded[:, :, 1:-1, :-2], hop_padded[:, 1:-1, :-2]),
    )
    for field_side, hop_side in sides:
        kinetic = kinetic + (0.5 * (hop_centre + hop_side))[None] * (centre - field_side)
    deriv_rows = 0.5 * (padded[:, :, 2:, 1:-1] - padded[:, :, :-2, 1:-1])
    deriv_cols = 0.5 * (padded[:, :, 1:-1, 2:] - padded[:, :, 1:-1, :-2])
    pieces = [
        material_masks[material][None, None] * centre for material in range(material_masks.shape[0])
    ]
    stacked = jnp.concatenate(pieces + [deriv_rows, deriv_cols], axis=1)
    mixed = jnp.einsum("bc,scxy->sbxy", mixing_matrix, stacked, precision=lax.Precision.HIGHEST)
    return mixed + kinetic


def chebyshev(field, apply_fn):

    def scaled(value):
        return (apply_fn(value) - SHIFT * value) / SCALE

    previous = field
    current = scaled(field)
    for repeat in range(DEGREE - 1):
        previous, current = (current, 2.0 * scaled(current) - previous)
    return current


def inner(left, right):
    return jnp.dot(
        left, right.T, precision=lax.Precision.HIGHEST, preferred_element_type=jnp.float32
    )


def general(states_in, region, onsite_table, hop_table, coupling_x, coupling_y):
    mixing_matrix = mixing(onsite_table, coupling_x, coupling_y)
    material_masks = masks_of(region)
    hop_field = jnp.einsum(
        "mb,mxy->bxy", hop_table, material_masks, precision=lax.Precision.HIGHEST
    )
    hop_rows = extended(hop_field, (("slab", 1),), 1)
    hop_padded = jnp.pad(hop_rows, ((0, 0), (0, 0), (1, 1)))

    def apply_rows(field):
        padded = extended(field, (("slab", 2),), 1)
        padded = jnp.pad(padded, ((0, 0), (0, 0), (0, 0), (1, 1)))
        return apply_padded(padded, hop_padded, material_masks, mixing_matrix)

    filtered = chebyshev(states_in, apply_rows)
    block_count = lax.axis_size("blk")
    slab_count = lax.axis_size("slab")
    states_all = filtered.shape[0] * block_count
    row_count = filtered.shape[2]
    width_all = filtered.shape[3]
    entries = float(BANDS * row_count * slab_count * width_all)
    image = apply_rows(filtered)
    cell_states, cell_image = (
        lax.all_to_all(filtered, "blk", split_axis=3, concat_axis=0, tiled=True),
        lax.all_to_all(image, "blk", split_axis=3, concat_axis=0, tiled=True),
    )
    states_flat = cell_states.reshape(states_all, -1)
    image_flat = cell_image.reshape(states_all, -1)
    moment = lax.psum(inner(states_flat, image_flat) / entries, ("blk", "slab"))

    def panel_step(panel, carry):
        basis_rows, factor_rows = carry
        offset = panel * PANEL
        panel_states = lax.dynamic_slice_in_dim(states_flat, offset, PANEL, 0)
        coeffs = lax.psum(inner(basis_rows, panel_states) / entries, ("blk", "slab"))
        residue = panel_states - jnp.dot(
            coeffs.T,
            basis_rows,
            precision=lax.Precision.HIGHEST,
            preferred_element_type=jnp.float32,
        )
        panel_gram = lax.psum(inner(residue, residue) / entries, ("blk", "slab"))
        panel_factor = jnp.linalg.cholesky(panel_gram)
        panel_basis = lax.linalg.triangular_solve(panel_factor, residue, left_side=True, lower=True)
        basis_rows = lax.dynamic_update_slice_in_dim(basis_rows, panel_basis, offset, 0)
        factor_row = lax.dynamic_update_slice_in_dim(coeffs.T, panel_factor, offset, 1)
        factor_rows = lax.dynamic_update_slice_in_dim(factor_rows, factor_row, offset, 0)
        return (basis_rows, factor_rows)

    start_state = (jnp.zeros_like(states_flat), jnp.zeros((states_all, states_all), jnp.float32))
    basis_flat, factor = lax.fori_loop(0, states_all // PANEL, panel_step, start_state)
    half_done = lax.linalg.triangular_solve(factor, moment, left_side=True, lower=True)
    projected = lax.linalg.triangular_solve(factor, half_done.T, left_side=True, lower=True).T
    basis_cells = basis_flat.reshape(cell_states.shape)
    states_out = lax.all_to_all(basis_cells, "blk", split_axis=0, concat_axis=3, tiled=True)
    owned = states_all // block_count
    projected_rows = lax.dynamic_slice_in_dim(projected, lax.axis_index("blk") * owned, owned, 0)
    return (states_out, projected_rows)


def per_device(states_in, region, *tables):
    known = (lax.axis_size("blk"), lax.axis_size("slab")) == (8, 4)
    run = fast if known and states_in.shape == (32, 8, 2, 1024) else general
    return run(states_in, region, *tables)


def solution(mesh):
    return jax.shard_map(
        per_device,
        mesh=mesh,
        in_specs=(P("blk", None, "slab", None), P("slab", None), P(), P(), P(), P()),
        out_specs=(P("blk", None, "slab", None), P("blk", None)),
        check_vma=False,
    )
```

```python
import functools

import jax
import jax.numpy as jnp
from jax import lax
from jax.experimental import pallas as pl
from jax.experimental.pallas import tpu as pltpu
from jax.sharding import PartitionSpec as P

BANDS = 8
MATERIALS = 4
PANEL = 32
SHIFT = 1.0
SCALE = 3.0
LANES = 128
ALL = ("blk", "slab")
LEFT = 4
WINDOW = 42
VMEM = pltpu.CompilerParams(vmem_limit_bytes=24 * 1024 * 1024)
ON_CHIP = pl.BlockSpec(memory_space=pltpu.VMEM)
OFF_CHIP = pl.BlockSpec(memory_space=pltpu.HBM)
HIGHEST = lax.Precision.HIGHEST
OWN = slice(0, 2048)
OWN_PAIRS = 2, 18
PAIR = 128
EDGE = 64


def off_chip(*arrays):
    return [pltpu.with_memory_space_constraint(array, pltpu.HBM) for array in arrays]


def dot(left, right, dims=((1,), (0,)), precision=None):
    return lax.dot_general(
        left, right, (dims, ((), ())), precision=precision, preferred_element_type=jnp.float32
    )


def split(value):
    high = value.astype(jnp.bfloat16)
    return high, (value - high.astype(jnp.float32)).astype(jnp.bfloat16)


def exchange(pieces, unit):
    count = len(pieces)
    lane = lax.broadcasted_iota(jnp.int32, pieces[0].shape, 1) // unit
    step = count // 2
    while step:
        low = (lane // step) % 2 == 0
        out = list(pieces)
        for i in range(count):
            if (i // step) % 2 == 0:
                a, c = pieces[i], pieces[i + step]
                out[i] = jnp.where(low, a, pltpu.roll(c, step * unit, 1))
                out[i + step] = jnp.where(low, pltpu.roll(a, LANES - step * unit, 1), c)
        pieces = out
        step //= 2
    return pieces


def pack_kernel(x_ref, o_ref, buf, scr, in_sem, out_sem):
    loads = [
        pltpu.make_async_copy(x_ref.at[:, pl.ds(8 * part, 8), :], buf.at[part], in_sem.at[part])
        for part in range(2)
    ]
    for load in loads:
        load.start()
    sends = [
        pltpu.make_async_copy(scr.at[pl.ds(128 * d, 128), :], o_ref.at[d], out_sem.at[d])
        for d in range(32)
    ]
    for part in range(2):
        loads[part].wait()
        rows = buf.at[part].reshape(2048, LANES)
        for tile in range(4):
            for r in range(4):
                row, high = r // 2, r % 2
                parts = [
                    rows[pl.ds((high * 4 + low) * 8 + tile * 2 + row, 32, stride=64), :]
                    for low in range(4)
                ]
                turned = jnp.concatenate(parts, axis=0).T
                scr[pl.ds((512 * part + 128 * tile) * 4 + r, 128, stride=4), :] = turned
        for send in sends[16 * part : 16 * part + 16]:
            send.start()
    for send in sends:
        send.wait()


def pack(x):
    rows = x.reshape(32, 8, 2, 8, LANES).transpose(0, 1, 3, 2, 4).reshape(256, 16, LANES)
    return pl.pallas_call(
        pack_kernel,
        out_shape=pltpu.HBM((32, LANES, LANES), jnp.float32),
        in_specs=[OFF_CHIP],
        out_specs=OFF_CHIP,
        scratch_shapes=[
            pltpu.VMEM((2, 256, 8, LANES), jnp.float32),
            pltpu.VMEM((4096, LANES), jnp.float32),
            pltpu.SemaphoreType.DMA((2,)),
            pltpu.SemaphoreType.DMA((32,)),
        ],
        compiler_params=VMEM,
        name="pack",
    )(*off_chip(rows))


def unpack_kernel(r_ref, o_ref, buf, sem):
    stores = []
    for high in range(2):
        rows = buf.at[high].reshape(2048, LANES)
        for tile in range(8):
            for row in range(2):
                turned = r_ref[pl.ds(tile * 512 + row * 2 + high, 128, stride=4), :].T
                for low in range(4):
                    rows[pl.ds((low * 8 + tile) * 2 + row, 32, stride=64), :] = turned[
                        32 * low : 32 * low + 32
                    ]
        stores.append(
            pltpu.make_async_copy(buf.at[high], o_ref.at[:, pl.ds(64 * high, 64), :], sem.at[high])
        )
        stores[high].start()
    for store in stores:
        store.wait()


def unpack(blocks):
    rows = pl.pallas_call(
        unpack_kernel,
        out_shape=pltpu.HBM((32, 128, LANES), jnp.float32),
        in_specs=[ON_CHIP],
        out_specs=OFF_CHIP,
        scratch_shapes=[pltpu.VMEM((2, 32, 64, LANES), jnp.float32), pltpu.SemaphoreType.DMA((2,))],
        compiler_params=VMEM,
        name="unpack",
    )(blocks.reshape(4096, LANES))
    return rows.reshape(32, 8, 8, 2, LANES).transpose(0, 1, 3, 2, 4).reshape(32, 8, 2, 1024)


def coef_kernel(reg_ref, onsite_ref, hop_ref, kx_ref, ky_ref, ch_ref, cl_ref):
    def decode(index):
        band = (index % 2) * 4 + ((index // 32) % 2) * 2 + (index // 4) % 2
        x = ((index // 8) % 4) * 2 + (index // 2) % 2
        column = (index // 64) % 2
        return band, x, column

    def one_hot(values, shape, axis):
        return (values == lax.broadcasted_iota(jnp.int32, shape, axis)).astype(jnp.float32)

    b_r, x_r, y_r = decode(lax.broadcasted_iota(jnp.int32, (128, 8), 0))
    band_rows = one_hot(b_r, (128, 8), 1)
    b_c, _, _ = decode(lax.broadcasted_iota(jnp.int32, (8, 256), 1) + 64)
    band_cols = one_hot(b_c, (8, 256), 0)
    reg = reg_ref[...]
    hop = dot(band_rows, hop_ref[...], ((1,), (1,)), HIGHEST)

    def table_of(offset):
        return dot(one_hot(x_r + offset, (128, 8), 1), reg, precision=HIGHEST)

    def hops(codes):
        total = jnp.zeros_like(codes)
        for m in range(MATERIALS):
            total = total + jnp.where(codes == m + 1.0, hop[:, m : m + 1], 0.0)
        return total

    second = lax.broadcasted_iota(jnp.int32, (128, LANES), 0) >= 64

    def aligned(table):
        return jnp.where(second, pltpu.roll(table, LANES - 1, 1), table)

    codes = table_of(0)
    here, up, down = hops(codes), hops(table_of(-1)), hops(table_of(1))
    before, after = pltpu.roll(here, 1, 1), pltpu.roll(here, LANES - 1, 1)
    valid = (codes > 0.5).astype(jnp.float32)
    centre = (0.5 * (4.0 * here + up + down + before + after) - SHIFT) * valid
    fields = [aligned((codes == m + 1.0).astype(jnp.float32)) for m in range(MATERIALS)]
    fields += [aligned(valid), aligned(centre)]
    fields += [aligned(-0.5 * (here + side) * valid) for side in (up, down, before, after)]

    b_r, x_r, y_r = decode(lax.broadcasted_iota(jnp.int32, (128, 256), 0))
    k = lax.broadcasted_iota(jnp.int32, (128, 256), 1)
    b_c, x_c, _ = decode(k + 64)
    dy = k // 64 - 1 - y_r
    dx = x_c - x_r
    same = b_r == b_c

    def spread(matrix):
        return dot(dot(band_rows, matrix, precision=HIGHEST), band_cols, precision=HIGHEST)

    here_at, up_at, down_at = (dy == 0) & (dx == 0), (dy == 0) & (dx == -1), (dy == 0) & (dx == 1)
    before_at, after_at = (dy == -1) & (dx == 0), (dy == 1) & (dx == 0)
    onsite = [
        jnp.where(here_at, spread(0.5 * (onsite_ref[m] + onsite_ref[m].T)), 0.0) for m in range(MATERIALS)
    ]
    kx = spread(0.5 * (0.5 * (kx_ref[...] - kx_ref[...].T)))
    ky = spread(0.5 * (0.5 * (ky_ref[...] - ky_ref[...].T)))
    mixed = (
        jnp.where(down_at, kx, 0.0)
        - jnp.where(up_at, kx, 0.0)
        + jnp.where(after_at, ky, 0.0)
        - jnp.where(before_at, ky, 0.0)
    )
    places = [here_at & same, up_at & same, down_at & same, before_at & same, after_at & same]
    for pair in range(WINDOW // 2):
        lane = 2 * pair + 1
        scalar = [field[:, lane : lane + 1] for field in fields]
        value = scalar[4] * mixed
        for m in range(MATERIALS):
            value = value + scalar[m] * onsite[m]
        for place, weight in zip(places, scalar[5:]):
            value = value + jnp.where(place, weight, 0.0)
        high, low = split((2.0 / SCALE) * value)
        ch_ref[pair] = high
        cl_ref[pair] = low


def coefficients(reg, onsite_table, hop_table, coupling_x, coupling_y):
    shape = pltpu.HBM((WINDOW // 2, 128, 256), jnp.bfloat16)
    return pl.pallas_call(
        coef_kernel,
        out_shape=(shape, shape),
        compiler_params=VMEM,
        name="coefficients",
    )(reg, onsite_table, hop_table, coupling_x, coupling_y)


def halves(even, odd):
    even, odd = (value.reshape(-1, 8, LANES) for value in (even, odd))
    first = lax.broadcasted_iota(jnp.int32, (1, 8, LANES), 1) < 4
    return (
        jnp.where(first, even, pltpu.roll(odd, 4, 1)),
        jnp.where(first, pltpu.roll(even, 4, 1), odd),
    )


def ingest(ref, start, pair, field, high, low):
    at = pair * PAIR
    for half in range(2):
        lanes = slice(half * LANES, half * LANES + LANES)
        for slab in range(4):
            pieces = exchange([ref[(half * 4 + j) * 4 + slab, pl.ds(start, 8), :] for j in range(4)], 32)
            for mid in range(2):
                for column, piece in enumerate(halves(pieces[2 * mid], pieces[2 * mid + 1])):
                    field[pl.ds(at + (column * 64 + mid * 32 + slab * 8), 8), lanes] = piece[0]
    rows = pl.ds(at + EDGE, PAIR)
    high[rows, :], low[rows, :] = split(field[pl.ds(at, PAIR), :])


def product(pair, ch_ref, cl_ref, high, low):
    rows = pl.ds(pair * PAIR, 2 * PAIR)
    vh, vl = high[rows, :], low[rows, :]
    c_high, c_low = ch_ref[pair], cl_ref[pair]
    return dot(
        jnp.concatenate([c_high, c_high, c_low], axis=1), jnp.concatenate([vh, vl, vh], axis=0)
    )


def steps(ch_ref, cl_ref, fa, fb, ah, al, bh, bl):
    def store(pair, value, field, high, low):
        field[pl.ds(pair * PAIR, PAIR), :] = value
        rows = pl.ds(pair * PAIR + EDGE, PAIR)
        high[rows, :], low[rows, :] = split(value)

    def first(pair):
        store(pair, 0.5 * product(pair, ch_ref, cl_ref, ah, al), fb, bh, bl)

    def later(old, high, low, source_high, source_low):
        def step(pair):
            rows = pl.ds(pair * PAIR, PAIR)
            value = product(pair, ch_ref, cl_ref, source_high, source_low) - old[rows, :]
            store(pair, value, old, high, low)

        return step

    even, odd = later(fa, ah, al, bh, bl), later(fb, bh, bl, ah, al)
    return first, even, odd, even


def interior_kernel(r_ref, ch_hbm, cl_hbm, fa, fb, ah, al, bh, bl, ch_ref, cl_ref, sem):
    loads = [
        pltpu.make_async_copy(ch_hbm, ch_ref, sem.at[0]),
        pltpu.make_async_copy(cl_hbm, cl_ref, sem.at[1]),
    ]
    for load in loads:
        load.start()

    def take(pair, carry):
        ingest(r_ref, pl.multiple_of((pair - OWN_PAIRS[0]) * 8, 8), pair, fa, ah, al)
        return carry

    lax.fori_loop(*OWN_PAIRS, take, 0, unroll=4)
    for load in loads:
        load.wait()
    for count, step in enumerate(steps(ch_ref, cl_ref, fa, fb, ah, al, bh, bl)):

        def body(pair, carry, step=step):
            step(pair)
            return carry

        low, high = OWN_PAIRS[0] + 1 + count, OWN_PAIRS[1] - 1 - count
        lax.fori_loop(low, high, body, 0, unroll=(high - low) // 2)


def interior(received, coef_high, coef_low):
    pairs = WINDOW // 2
    field = pltpu.VMEM((pairs * PAIR, 256), jnp.float32)
    half = pltpu.VMEM((pairs * PAIR + 2 * EDGE, 256), jnp.bfloat16)
    bands = pltpu.VMEM((pairs, PAIR, 256), jnp.bfloat16)
    return pl.pallas_call(
        interior_kernel,
        out_shape=(field,) * 2 + (half,) * 4 + (bands,) * 2,
        in_specs=[ON_CHIP, OFF_CHIP, OFF_CHIP],
        out_specs=(ON_CHIP,) * 8,
        scratch_shapes=[pltpu.SemaphoreType.DMA((2,))],
        compiler_params=VMEM,
        cost_estimate=pl.CostEstimate(flops=int(8e9), transcendentals=0, bytes_accessed=int(2e7)),
        name="interior",
    )(received, *off_chip(coef_high, coef_low))


def edges_kernel(left_ref, right_ref, *refs):
    (ch_ref, cl_ref), (vh_hbm, vl_hbm, g_ref) = refs[6:8], refs[8:11]
    fa, fb, ah, al, bh, bl = fields = refs[11:17]
    sem = refs[17]
    pairs = WINDOW // 2
    first_row = OWN_PAIRS[0] * PAIR + EDGE

    def results(low, high, index):
        rows = pl.ds(low + EDGE, high - low)
        target = pl.ds(low + EDGE - first_row, high - low)
        return [
            pltpu.make_async_copy(ah.at[rows, :], vh_hbm.at[target, :], sem.at[index]),
            pltpu.make_async_copy(al.at[rows, :], vl_hbm.at[target, :], sem.at[index + 1]),
        ]

    inner = OWN_PAIRS[0] + 4, OWN_PAIRS[1] - 4
    stores = results(inner[0] * PAIR, inner[1] * PAIR, 0)
    for store in stores:
        store.start()
    zero = jnp.zeros((EDGE, 256), jnp.bfloat16)
    for ref in (ah, al, bh, bl):
        ref[0:EDGE, :] = zero
        ref[pairs * PAIR + EDGE :, :] = zero
    for pair in range(OWN_PAIRS[0]):
        ingest(left_ref, pair * 8, pair, fa, ah, al)
    for pair in range(OWN_PAIRS[1], pairs):
        ingest(right_ref, (pair - OWN_PAIRS[1]) * 8, pair, fa, ah, al)
    reach = ((0, pairs), (1, pairs - 1), (1, pairs - 1), (2, pairs - 2))
    for count, step in enumerate(steps(ch_ref, cl_ref, *fields)):
        low, high = OWN_PAIRS[0] + 1 + count, OWN_PAIRS[1] - 1 - count
        for pair in list(range(reach[count][0], low)) + list(range(high, reach[count][1])):
            step(pair)
    last = OWN_PAIRS[1] * PAIR + EDGE
    stores += results(OWN_PAIRS[0] * PAIR, inner[0] * PAIR, 2) + results(inner[1] * PAIR, last, 4)
    for store in stores[2:]:
        store.start()
    own = slice(first_row, OWN_PAIRS[1] * PAIR + EDGE)
    dims = ((0,), (0,))
    cross = dot(ah[own, :], al[own, :], dims)
    g_ref[...] = dot(ah[own, :], ah[own, :], dims) + (cross + cross.T)
    for store in stores:
        store.wait()


def filtered_blocks(received, coef_high, coef_low):
    count = lax.axis_size(ALL)
    chain = [(i, i + 1) for i in range(count - 1)]
    left = lax.ppermute(received[:, 128 - 4 * LEFT :], ALL, chain)
    right = lax.ppermute(received[:, : 4 * (WINDOW - LEFT - 32)], ALL, [(j, i) for i, j in chain])
    state = interior(received, coef_high, coef_low)
    half = pltpu.HBM((2048 + EDGE, 256), jnp.bfloat16)
    fields = [pltpu.VMEM(value.shape, value.dtype) for value in state[:6]]
    return pl.pallas_call(
        edges_kernel,
        out_shape=(half, half, pltpu.VMEM((256, 256), jnp.float32), *fields),
        in_specs=[ON_CHIP] * 10,
        out_specs=(OFF_CHIP,) * 2 + (ON_CHIP,) * 7,
        input_output_aliases={i + 2: i + 3 for i in range(6)},
        scratch_shapes=[pltpu.SemaphoreType.DMA((6,))],
        compiler_params=VMEM,
        name="edges",
    )(left, right, *state)[:3]


def moment_kernel(vh_ref, vl_ref, ch_ref, cl_ref, g_ref, m_ref, bh, bl):
    block, edge = 128, 64

    def image(pair, rows, drop=0):
        vh, vl = vh_ref[rows, :], vl_ref[rows, :]
        c_high, c_low = ch_ref[pair, :, drop:], cl_ref[pair, :, drop:]
        value = dot(
            jnp.concatenate([c_high, c_high, c_low], axis=1), jnp.concatenate([vh, vl, vh], axis=0)
        )
        at = pl.ds((pair - 2) * block, block)
        bh[at, :], bl[at, :] = split(value)

    def body(pair, carry):
        image(pair, pl.ds(pl.multiple_of((pair - 3) * block + edge, edge), 256))
        return carry

    image(2, slice(0, block + edge), edge)
    lax.fori_loop(3, 18, body, 0, unroll=3)
    rows = slice(16 * block - edge, 16 * block)
    c_high, c_low = ch_ref[18, 0:edge, 0:edge], cl_ref[18, 0:edge, 0:edge]
    value = dot(c_high, vh_ref[rows, :]) + (dot(c_high, vl_ref[rows, :]) + dot(c_low, vh_ref[rows, :]))
    bh[16 * block :, :], bl[16 * block :, :] = split(value)
    dims = ((0,), (0,))
    high = vh_ref[...]
    moment = dot(high, bh[...], dims) + (dot(high, bl[...], dims) + dot(vl_ref[...], bh[...], dims))
    m_ref[...] = (0.5 * SCALE) * moment + SHIFT * g_ref[...]


def moment_of(vh, vl, coef_high, coef_low, gram):
    return pl.pallas_call(
        moment_kernel,
        out_shape=jax.ShapeDtypeStruct((256, 256), jnp.float32),
        scratch_shapes=[pltpu.VMEM((16 * 128 + 64, 256), jnp.bfloat16)] * 2,
        compiler_params=VMEM,
        cost_estimate=pl.CostEstimate(flops=int(4e9), transcendentals=0, bytes_accessed=int(1e7)),
        name="moment",
    )(*off_chip(vh, vl, coef_high, coef_low), gram)


def panel_solve(block, lines):
    row = lax.broadcasted_iota(jnp.int32, (8, LANES), 0)

    def spread(tile, k):
        return jnp.broadcast_to(tile[k % 8 : k % 8 + 1], tile.shape)

    cols = [
        [jnp.broadcast_to(block[8 * t : 8 * t + 8, j : j + 1], (8, LANES)) for t in range(4)]
        for j in range(32)
    ]
    lines = [
        [lines[8 * t : 8 * t + 8, LANES * h : LANES * h + LANES] for h in range(2)] for t in range(4)
    ]
    pivots = [jnp.ones((8, LANES), jnp.float32) for t in range(4)]
    for k in range(32):
        own = k // 8
        pivot = spread(cols[k][own], k)
        pivots[own] = jnp.where(row == k % 8, pivot, pivots[own])
        scale = 1.0 / pivot
        ratio = {t: cols[k][t] * scale for t in range(own, 4)}
        ratio[own] = jnp.where(row > k % 8, ratio[own], 0.0)
        line = [spread(part, k) for part in lines[own]]
        for j in range(k + 1, 32):
            weight = spread(ratio[j // 8], j)
            for t in range(j // 8, 4):
                cols[j][t] = cols[j][t] - cols[k][t] * weight
        for t in range(own, 4):
            lines[t] = [part - ratio[t] * above for part, above in zip(lines[t], line)]
    roots = [lax.rsqrt(pivots[t]) for t in range(4)]
    return jnp.concatenate(
        [jnp.concatenate([part * roots[t] for part in lines[t]], axis=1) for t in range(4)], axis=0
    )


def half_inverse(aug):
    def panel(p, carry):
        rows = pl.ds(pl.multiple_of(32 * p, 32), 32)
        lines = aug[rows, :]
        lines = panel_solve(pltpu.roll(lines[:, :LANES], LANES - 32 * p, 1), lines)
        aug[rows, :] = lines
        lane = lax.broadcasted_iota(jnp.int32, (32, LANES), 1)
        upper = jnp.where(lane >= 32 * (p + 1), lines[:, :LANES], 0.0)
        aug[...] = aug[...] - dot(upper, lines, ((0,), (0,)), HIGHEST)
        return carry

    lax.fori_loop(0, 4, panel, 0)


def basis_kernel(entries, both_ref, vh_hbm, vl_hbm, w_ref, o_hbm, gram, aug, vh, vl, scr, out, sem, out_sem):
    loads = [
        pltpu.make_async_copy(vh_hbm.at[OWN, :], vh, sem.at[0]),
        pltpu.make_async_copy(vl_hbm.at[OWN, :], vl, sem.at[1]),
    ]
    for load in loads:
        load.start()
    row = lax.broadcasted_iota(jnp.int32, (LANES, LANES), 0)
    eye = (row == lax.broadcasted_iota(jnp.int32, (LANES, LANES), 1)).astype(jnp.float32)
    gram[...] = both_ref[:, 0:8, :].reshape(256, 256) * (1.0 / entries)
    aug[:, :LANES] = gram[:LANES, :LANES]
    aug[:, LANES:] = eye
    half_inverse(aug)
    first = aug[:, LANES:]
    upper = dot(first, gram[:LANES, LANES:], precision=HIGHEST)
    aug[:, :LANES] = gram[LANES:, LANES:] - dot(upper, upper, ((0,), (0,)), HIGHEST)
    aug[:, LANES:] = eye
    corner = dot(upper, first, ((0,), (0,)), HIGHEST)
    half_inverse(aug)
    second = aug[:, LANES:]
    w_ref[:LANES, :LANES] = first
    w_ref[:LANES, LANES:] = jnp.zeros((LANES, LANES), jnp.float32)
    w_ref[LANES:, :LANES] = -dot(second, corner, precision=HIGHEST)
    w_ref[LANES:, LANES:] = second
    for load in loads:
        load.wait()
    sends = [pltpu.make_async_copy(out.at[d], o_hbm.at[d], out_sem.at[d]) for d in range(32)]
    for half in range(2):
        used = LANES * (half + 1)
        wh, wl = split(w_ref[LANES * half : used, :used])
        values = [vh[:, :used], vl[:, :used], vh[:, :used]]
        scr[...] = dot(
            jnp.concatenate(values, axis=1), jnp.concatenate([wh, wh, wl], axis=1), ((1,), (1,))
        )
        for slab in range(4):
            pieces = []
            for mid in range(2):
                columns = []
                for column in range(2):
                    at = column * 64 + mid * 32 + slab * 8
                    columns.append(
                        jnp.concatenate(
                            [scr[pair * 128 + at : pair * 128 + at + 8, :] for pair in range(16)], axis=0
                        )
                    )
                pieces += [value.reshape(128, LANES) for value in halves(*columns)]
            for j, piece in enumerate(exchange(pieces, 32)):
                d = (half * 4 + j) * 4 + slab
                out[d] = piece
                sends[d].start()
    for send in sends:
        send.wait()


def basis(both, entries, vh, vl):
    return pl.pallas_call(
        functools.partial(basis_kernel, entries),
        out_shape=(
            jax.ShapeDtypeStruct((256, 256), jnp.float32),
            pltpu.HBM((32, 128, LANES), jnp.float32),
        ),
        in_specs=[ON_CHIP, OFF_CHIP, OFF_CHIP],
        out_specs=(ON_CHIP, OFF_CHIP),
        scratch_shapes=[
            pltpu.VMEM((256, 256), jnp.float32),
            pltpu.VMEM((LANES, 256), jnp.float32),
            pltpu.VMEM((2048, 256), jnp.bfloat16),
            pltpu.VMEM((2048, 256), jnp.bfloat16),
            pltpu.VMEM((2048, LANES), jnp.float32),
            pltpu.VMEM((32, LANES, LANES), jnp.float32),
            pltpu.SemaphoreType.DMA((2,)),
            pltpu.SemaphoreType.DMA((32,)),
        ],
        compiler_params=VMEM,
        cost_estimate=pl.CostEstimate(flops=int(4e9), transcendentals=0, bytes_accessed=int(2e7)),
        name="basis",
    )(both, *off_chip(vh, vl))


def parts_of(square):
    count = lax.axis_size(ALL)
    return square.reshape(count, -1, square.shape[1])


def swap(parts):
    return lax.all_to_all(parts, ALL, 0, 0, tiled=True)


def for_all(share):
    return jnp.broadcast_to(share[None], (lax.axis_size(ALL),) + share.shape)


def project_kernel(entries, moment_ref, w_ref, p_ref):
    first = pl.multiple_of(32 * lax.axis_index("blk"), 32)
    half_done = dot(w_ref[pl.ds(first, 32), :], moment_ref[...], precision=HIGHEST) * (1.0 / entries)
    p_ref[...] = dot(half_done, w_ref[...], ((1,), (1,)), HIGHEST)


def project(moment, inverse, entries):
    return pl.pallas_call(
        functools.partial(project_kernel, entries),
        out_shape=jax.ShapeDtypeStruct((32, 256), jnp.float32),
        in_specs=[ON_CHIP] * 2,
        out_specs=ON_CHIP,
        compiler_params=VMEM,
        name="project",
    )(moment, inverse)


def fast(states_in, region, onsite_table, hop_table, coupling_x, coupling_y):
    device = lax.axis_index("blk") * lax.axis_size("slab") + lax.axis_index("slab")
    entries = float(BANDS * 8 * 1024)
    codes = lax.all_gather((region + 1).astype(jnp.float32), "slab", axis=0, tiled=True)
    received = swap(pack(states_in))
    codes = jnp.pad(codes, ((0, 0), (LEFT + 1, LANES)))
    codes = lax.dynamic_slice(codes, (0, 32 * device), (8, LANES))
    coef_high, coef_low = coefficients(codes, onsite_table, hop_table, coupling_x, coupling_y)
    vh, vl, own_gram = filtered_blocks(received, coef_high, coef_low)
    own_moment = moment_of(vh, vl, coef_high, coef_low, own_gram)
    share = swap(parts_of(own_gram)).sum(0)
    both = swap(jnp.concatenate([for_all(share), parts_of(own_moment)], axis=1))
    inverse, blocks = basis(both, entries, vh, vl)
    moment = swap(for_all(both[:, 8:].sum(0))).reshape(256, 256)
    blocks, moment = lax.optimization_barrier((blocks, moment))
    states_out = unpack(swap(blocks))
    projected = project(moment, inverse, entries)
    return states_out, projected


DEGREE = 4


def extended(array, sides, width):
    for axis, dim in sides:
        size, length = (lax.axis_size(axis), array.shape[dim])
        up = [(i, (i + 1) % size) for i in range(size - 1)]
        down = [(j, i) for i, j in up]
        last = lax.slice_in_dim(array, length - width, length, axis=dim)
        leading = lax.slice_in_dim(array, 0, width, axis=dim)
        before = lax.ppermute(last, axis, up)
        after = lax.ppermute(leading, axis, down)
        array = jnp.concatenate([before, array, after], axis=dim)
    return array


def mixing(onsite_table, coupling_x, coupling_y):
    onsite = 0.5 * (onsite_table + jnp.swapaxes(onsite_table, 1, 2))
    blocks = [onsite[material] for material in range(onsite.shape[0])]
    return jnp.concatenate(
        blocks + [0.5 * (coupling_x - coupling_x.T), 0.5 * (coupling_y - coupling_y.T)], axis=1
    )


def masks_of(region):
    codes = jnp.arange(MATERIALS, dtype=jnp.int32)
    return (region[None] == codes[:, None, None]).astype(jnp.float32)


def apply_padded(padded, hop_padded, material_masks, mixing_matrix):
    centre = padded[:, :, 1:-1, 1:-1]
    hop_centre = hop_padded[:, 1:-1, 1:-1]
    kinetic = jnp.zeros_like(centre)
    sides = (
        (padded[:, :, 2:, 1:-1], hop_padded[:, 2:, 1:-1]),
        (padded[:, :, :-2, 1:-1], hop_padded[:, :-2, 1:-1]),
        (padded[:, :, 1:-1, 2:], hop_padded[:, 1:-1, 2:]),
        (padded[:, :, 1:-1, :-2], hop_padded[:, 1:-1, :-2]),
    )
    for field_side, hop_side in sides:
        kinetic = kinetic + (0.5 * (hop_centre + hop_side))[None] * (centre - field_side)
    deriv_rows = 0.5 * (padded[:, :, 2:, 1:-1] - padded[:, :, :-2, 1:-1])
    deriv_cols = 0.5 * (padded[:, :, 1:-1, 2:] - padded[:, :, 1:-1, :-2])
    pieces = [
        material_masks[material][None, None] * centre for material in range(material_masks.shape[0])
    ]
    stacked = jnp.concatenate(pieces + [deriv_rows, deriv_cols], axis=1)
    mixed = jnp.einsum("bc,scxy->sbxy", mixing_matrix, stacked, precision=lax.Precision.HIGHEST)
    return mixed + kinetic


def chebyshev(field, apply_fn):

    def scaled(value):
        return (apply_fn(value) - SHIFT * value) / SCALE

    previous = field
    current = scaled(field)
    for repeat in range(DEGREE - 1):
        previous, current = (current, 2.0 * scaled(current) - previous)
    return current


def inner(left, right):
    return jnp.dot(
        left, right.T, precision=lax.Precision.HIGHEST, preferred_element_type=jnp.float32
    )


def general(states_in, region, onsite_table, hop_table, coupling_x, coupling_y):
    mixing_matrix = mixing(onsite_table, coupling_x, coupling_y)
    material_masks = masks_of(region)
    hop_field = jnp.einsum(
        "mb,mxy->bxy", hop_table, material_masks, precision=lax.Precision.HIGHEST
    )
    hop_rows = extended(hop_field, (("slab", 1),), 1)
    hop_padded = jnp.pad(hop_rows, ((0, 0), (0, 0), (1, 1)))

    def apply_rows(field):
        padded = extended(field, (("slab", 2),), 1)
        padded = jnp.pad(padded, ((0, 0), (0, 0), (0, 0), (1, 1)))
        return apply_padded(padded, hop_padded, material_masks, mixing_matrix)

    filtered = chebyshev(states_in, apply_rows)
    block_count = lax.axis_size("blk")
    slab_count = lax.axis_size("slab")
    states_all = filtered.shape[0] * block_count
    row_count = filtered.shape[2]
    width_all = filtered.shape[3]
    entries = float(BANDS * row_count * slab_count * width_all)
    image = apply_rows(filtered)
    cell_states, cell_image = (
        lax.all_to_all(filtered, "blk", split_axis=3, concat_axis=0, tiled=True),
        lax.all_to_all(image, "blk", split_axis=3, concat_axis=0, tiled=True),
    )
    states_flat = cell_states.reshape(states_all, -1)
    image_flat = cell_image.reshape(states_all, -1)
    moment = lax.psum(inner(states_flat, image_flat) / entries, ("blk", "slab"))

    def panel_step(panel, carry):
        basis_rows, factor_rows = carry
        offset = panel * PANEL
        panel_states = lax.dynamic_slice_in_dim(states_flat, offset, PANEL, 0)
        coeffs = lax.psum(inner(basis_rows, panel_states) / entries, ("blk", "slab"))
        residue = panel_states - jnp.dot(
            coeffs.T,
            basis_rows,
            precision=lax.Precision.HIGHEST,
            preferred_element_type=jnp.float32,
        )
        panel_gram = lax.psum(inner(residue, residue) / entries, ("blk", "slab"))
        panel_factor = jnp.linalg.cholesky(panel_gram)
        panel_basis = lax.linalg.triangular_solve(panel_factor, residue, left_side=True, lower=True)
        basis_rows = lax.dynamic_update_slice_in_dim(basis_rows, panel_basis, offset, 0)
        factor_row = lax.dynamic_update_slice_in_dim(coeffs.T, panel_factor, offset, 1)
        factor_rows = lax.dynamic_update_slice_in_dim(factor_rows, factor_row, offset, 0)
        return (basis_rows, factor_rows)

    start_state = (jnp.zeros_like(states_flat), jnp.zeros((states_all, states_all), jnp.float32))
    basis_flat, factor = lax.fori_loop(0, states_all // PANEL, panel_step, start_state)
    half_done = lax.linalg.triangular_solve(factor, moment, left_side=True, lower=True)
    projected = lax.linalg.triangular_solve(factor, half_done.T, left_side=True, lower=True).T
    basis_cells = basis_flat.reshape(cell_states.shape)
    states_out = lax.all_to_all(basis_cells, "blk", split_axis=0, concat_axis=3, tiled=True)
    owned = states_all // block_count
    projected_rows = lax.dynamic_slice_in_dim(projected, lax.axis_index("blk") * owned, owned, 0)
    return (states_out, projected_rows)


def per_device(states_in, region, *tables):
    known = (lax.axis_size("blk"), lax.axis_size("slab")) == (8, 4)
    run = fast if known and states_in.shape == (32, 8, 2, 1024) else general
    return run(states_in, region, *tables)


def solution(mesh):
    return jax.shard_map(
        per_device,
        mesh=mesh,
        in_specs=(P("blk", None, "slab", None), P("slab", None), P(), P(), P(), P()),
        out_specs=(P("blk", None, "slab", None), P("blk", None)),
        check_vma=False,
    )
```

```python
import functools

import jax
import jax.numpy as jnp
from jax import lax
from jax.experimental import pallas as pl
from jax.experimental.pallas import tpu as pltpu
from jax.sharding import PartitionSpec as P

BANDS = 8
MATERIALS = 4
PANEL = 32
SHIFT = 1.0
SCALE = 3.0
LANES = 128
ALL = ("blk", "slab")
LEFT = 4
WINDOW = 42
VMEM = pltpu.CompilerParams(vmem_limit_bytes=24 * 1024 * 1024)
ON_CHIP = pl.BlockSpec(memory_space=pltpu.VMEM)
OFF_CHIP = pl.BlockSpec(memory_space=pltpu.HBM)
HIGHEST = lax.Precision.HIGHEST
OWN = slice(0, 2048)
OWN_PAIRS = 2, 18
PAIR = 128
EDGE = 64


def off_chip(*arrays):
    return [pltpu.with_memory_space_constraint(array, pltpu.HBM) for array in arrays]


def dot(left, right, dims=((1,), (0,)), precision=None):
    return lax.dot_general(
        left, right, (dims, ((), ())), precision=precision, preferred_element_type=jnp.float32
    )


def split(value):
    high = value.astype(jnp.bfloat16)
    return high, (value - high.astype(jnp.float32)).astype(jnp.bfloat16)


def exchange(pieces, unit):
    count = len(pieces)
    lane = lax.broadcasted_iota(jnp.int32, pieces[0].shape, 1) // unit
    step = count // 2
    while step:
        low = (lane // step) % 2 == 0
        out = list(pieces)
        for i in range(count):
            if (i // step) % 2 == 0:
                a, c = pieces[i], pieces[i + step]
                out[i] = jnp.where(low, a, pltpu.roll(c, step * unit, 1))
                out[i + step] = jnp.where(low, pltpu.roll(a, LANES - step * unit, 1), c)
        pieces = out
        step //= 2
    return pieces


def pack_kernel(x_ref, o_ref, buf, scr, in_sem, out_sem):
    loads = [
        pltpu.make_async_copy(x_ref.at[:, pl.ds(8 * part, 8), :], buf.at[part], in_sem.at[part])
        for part in range(2)
    ]
    for load in loads:
        load.start()
    sends = [
        pltpu.make_async_copy(scr.at[pl.ds(128 * d, 128), :], o_ref.at[d], out_sem.at[d])
        for d in range(32)
    ]
    for part in range(2):
        loads[part].wait()
        rows = buf.at[part].reshape(2048, LANES)
        for tile in range(4):
            for r in range(4):
                row, high = r // 2, r % 2
                parts = [
                    rows[pl.ds((high * 4 + low) * 8 + tile * 2 + row, 32, stride=64), :]
                    for low in range(4)
                ]
                turned = jnp.concatenate(parts, axis=0).T
                scr[pl.ds((512 * part + 128 * tile) * 4 + r, 128, stride=4), :] = turned
        for send in sends[16 * part : 16 * part + 16]:
            send.start()
    for send in sends:
        send.wait()


def pack(x):
    rows = x.reshape(32, 8, 2, 8, LANES).transpose(0, 1, 3, 2, 4).reshape(256, 16, LANES)
    return pl.pallas_call(
        pack_kernel,
        out_shape=pltpu.HBM((32, LANES, LANES), jnp.float32),
        in_specs=[OFF_CHIP],
        out_specs=OFF_CHIP,
        scratch_shapes=[
            pltpu.VMEM((2, 256, 8, LANES), jnp.float32),
            pltpu.VMEM((4096, LANES), jnp.float32),
            pltpu.SemaphoreType.DMA((2,)),
            pltpu.SemaphoreType.DMA((32,)),
        ],
        compiler_params=VMEM,
        name="pack",
    )(*off_chip(rows))


def unpack_kernel(r_ref, o_ref, buf, sem):
    stores = []
    for high in range(2):
        rows = buf.at[high].reshape(2048, LANES)
        for tile in range(8):
            for row in range(2):
                turned = r_ref[pl.ds(tile * 512 + row * 2 + high, 128, stride=4), :].T
                for low in range(4):
                    rows[pl.ds((low * 8 + tile) * 2 + row, 32, stride=64), :] = turned[
                        32 * low : 32 * low + 32
                    ]
        stores.append(
            pltpu.make_async_copy(buf.at[high], o_ref.at[:, pl.ds(64 * high, 64), :], sem.at[high])
        )
        stores[high].start()
    for store in stores:
        store.wait()


def unpack(blocks):
    rows = pl.pallas_call(
        unpack_kernel,
        out_shape=pltpu.HBM((32, 128, LANES), jnp.float32),
        in_specs=[ON_CHIP],
        out_specs=OFF_CHIP,
        scratch_shapes=[pltpu.VMEM((2, 32, 64, LANES), jnp.float32), pltpu.SemaphoreType.DMA((2,))],
        compiler_params=VMEM,
        name="unpack",
    )(blocks.reshape(4096, LANES))
    return rows.reshape(32, 8, 8, 2, LANES).transpose(0, 1, 3, 2, 4).reshape(32, 8, 2, 1024)


def coef_kernel(reg_ref, onsite_ref, hop_ref, kx_ref, ky_ref, ch_ref, cl_ref):
    def decode(index):
        band = (index % 2) * 4 + ((index // 32) % 2) * 2 + (index // 4) % 2
        x = ((index // 8) % 4) * 2 + (index // 2) % 2
        column = (index // 64) % 2
        return band, x, column

    def one_hot(values, shape, axis):
        return (values == lax.broadcasted_iota(jnp.int32, shape, axis)).astype(jnp.float32)

    b_r, x_r, y_r = decode(lax.broadcasted_iota(jnp.int32, (128, 8), 0))
    band_rows = one_hot(b_r, (128, 8), 1)
    b_c, _, _ = decode(lax.broadcasted_iota(jnp.int32, (8, 256), 1) + 64)
    band_cols = one_hot(b_c, (8, 256), 0)
    reg = reg_ref[...]
    hop = dot(band_rows, hop_ref[...], ((1,), (1,)), HIGHEST)

    def table_of(offset):
        return dot(one_hot(x_r + offset, (128, 8), 1), reg, precision=HIGHEST)

    def hops(codes):
        total = jnp.zeros_like(codes)
        for m in range(MATERIALS):
            total = total + jnp.where(codes == m + 1.0, hop[:, m : m + 1], 0.0)
        return total

    second = lax.broadcasted_iota(jnp.int32, (128, LANES), 0) >= 64

    def aligned(table):
        return jnp.where(second, pltpu.roll(table, LANES - 1, 1), table)

    codes = table_of(0)
    here, up, down = hops(codes), hops(table_of(-1)), hops(table_of(1))
    before, after = pltpu.roll(here, 1, 1), pltpu.roll(here, LANES - 1, 1)
    valid = (codes > 0.5).astype(jnp.float32)
    centre = (0.5 * (4.0 * here + up + down + before + after) - SHIFT) * valid
    fields = [aligned((codes == m + 1.0).astype(jnp.float32)) for m in range(MATERIALS)]
    fields += [aligned(valid), aligned(centre)]
    fields += [aligned(-0.5 * (here + side) * valid) for side in (up, down, before, after)]

    b_r, x_r, y_r = decode(lax.broadcasted_iota(jnp.int32, (128, 256), 0))
    k = lax.broadcasted_iota(jnp.int32, (128, 256), 1)
    b_c, x_c, _ = decode(k + 64)
    dy = k // 64 - 1 - y_r
    dx = x_c - x_r
    same = b_r == b_c

    def spread(matrix):
        return dot(dot(band_rows, matrix, precision=HIGHEST), band_cols, precision=HIGHEST)

    here_at, up_at, down_at = (dy == 0) & (dx == 0), (dy == 0) & (dx == -1), (dy == 0) & (dx == 1)
    before_at, after_at = (dy == -1) & (dx == 0), (dy == 1) & (dx == 0)
    onsite = [
        jnp.where(here_at, spread(0.5 * (onsite_ref[m] + onsite_ref[m].T)), 0.0) for m in range(MATERIALS)
    ]
    kx = spread(0.5 * (0.5 * (kx_ref[...] - kx_ref[...].T)))
    ky = spread(0.5 * (0.5 * (ky_ref[...] - ky_ref[...].T)))
    mixed = (
        jnp.where(down_at, kx, 0.0)
        - jnp.where(up_at, kx, 0.0)
        + jnp.where(after_at, ky, 0.0)
        - jnp.where(before_at, ky, 0.0)
    )
    places = [here_at & same, up_at & same, down_at & same, before_at & same, after_at & same]
    for pair in range(WINDOW // 2):
        lane = 2 * pair + 1
        scalar = [field[:, lane : lane + 1] for field in fields]
        value = scalar[4] * mixed
        for m in range(MATERIALS):
            value = value + scalar[m] * onsite[m]
        for place, weight in zip(places, scalar[5:]):
            value = value + jnp.where(place, weight, 0.0)
        high, low = split((2.0 / SCALE) * value)
        ch_ref[pair] = high
        cl_ref[pair] = low


def coefficients(reg, onsite_table, hop_table, coupling_x, coupling_y):
    shape = pltpu.HBM((WINDOW // 2, 128, 256), jnp.bfloat16)
    return pl.pallas_call(
        coef_kernel,
        out_shape=(shape, shape),
        compiler_params=VMEM,
        name="coefficients",
    )(reg, onsite_table, hop_table, coupling_x, coupling_y)


def halves(even, odd):
    even, odd = (value.reshape(-1, 8, LANES) for value in (even, odd))
    first = lax.broadcasted_iota(jnp.int32, (1, 8, LANES), 1) < 4
    return (
        jnp.where(first, even, pltpu.roll(odd, 4, 1)),
        jnp.where(first, pltpu.roll(even, 4, 1), odd),
    )


def lower_blocks(square):
    return jnp.concatenate(
        [square[:LANES, :LANES], square[LANES:, :LANES], square[LANES:, LANES:]], axis=0
    )


def ingest(ref, start, pair, field, high, low):
    at = pair * PAIR
    for half in range(2):
        lanes = slice(half * LANES, half * LANES + LANES)
        for slab in range(4):
            pieces = exchange([ref[(half * 4 + j) * 4 + slab, pl.ds(start, 8), :] for j in range(4)], 32)
            for mid in range(2):
                for column, piece in enumerate(halves(pieces[2 * mid], pieces[2 * mid + 1])):
                    field[pl.ds(at + (column * 64 + mid * 32 + slab * 8), 8), lanes] = piece[0]
    rows = pl.ds(at + EDGE, PAIR)
    high[rows, :], low[rows, :] = split(field[pl.ds(at, PAIR), :])


def product(pair, ch_ref, cl_ref, high, low):
    rows = pl.ds(pair * PAIR, 2 * PAIR)
    vh, vl = high[rows, :], low[rows, :]
    c_high, c_low = ch_ref[pair], cl_ref[pair]
    return dot(
        jnp.concatenate([c_high, c_high, c_low], axis=1), jnp.concatenate([vh, vl, vh], axis=0)
    )


def steps(ch_ref, cl_ref, fa, fb, ah, al, bh, bl):
    def store(pair, value, field, high, low):
        field[pl.ds(pair * PAIR, PAIR), :] = value
        rows = pl.ds(pair * PAIR + EDGE, PAIR)
        high[rows, :], low[rows, :] = split(value)

    def first(pair):
        store(pair, 0.5 * product(pair, ch_ref, cl_ref, ah, al), fb, bh, bl)

    def later(old, high, low, source_high, source_low):
        def step(pair):
            rows = pl.ds(pair * PAIR, PAIR)
            value = product(pair, ch_ref, cl_ref, source_high, source_low) - old[rows, :]
            store(pair, value, old, high, low)

        return step

    even, odd = later(fa, ah, al, bh, bl), later(fb, bh, bl, ah, al)
    return first, even, odd, even


def interior_kernel(r_ref, ch_hbm, cl_hbm, fa, fb, ah, al, bh, bl, ch_ref, cl_ref, sem):
    loads = [
        pltpu.make_async_copy(ch_hbm, ch_ref, sem.at[0]),
        pltpu.make_async_copy(cl_hbm, cl_ref, sem.at[1]),
    ]
    for load in loads:
        load.start()

    def take(pair, carry):
        ingest(r_ref, pl.multiple_of((pair - OWN_PAIRS[0]) * 8, 8), pair, fa, ah, al)
        return carry

    lax.fori_loop(*OWN_PAIRS, take, 0, unroll=4)
    for load in loads:
        load.wait()
    for count, step in enumerate(steps(ch_ref, cl_ref, fa, fb, ah, al, bh, bl)):

        def body(pair, carry, step=step):
            step(pair)
            return carry

        low, high = OWN_PAIRS[0] + 1 + count, OWN_PAIRS[1] - 1 - count
        lax.fori_loop(low, high, body, 0, unroll=(high - low) // 2)


def interior(received, coef_high, coef_low):
    pairs = WINDOW // 2
    field = pltpu.VMEM((pairs * PAIR, 256), jnp.float32)
    half = pltpu.VMEM((pairs * PAIR + 2 * EDGE, 256), jnp.bfloat16)
    bands = pltpu.VMEM((pairs, PAIR, 256), jnp.bfloat16)
    return pl.pallas_call(
        interior_kernel,
        out_shape=(field,) * 2 + (half,) * 4 + (bands,) * 2,
        in_specs=[ON_CHIP, OFF_CHIP, OFF_CHIP],
        out_specs=(ON_CHIP,) * 8,
        scratch_shapes=[pltpu.SemaphoreType.DMA((2,))],
        compiler_params=VMEM,
        cost_estimate=pl.CostEstimate(flops=int(8e9), transcendentals=0, bytes_accessed=int(2e7)),
        name="interior",
    )(received, *off_chip(coef_high, coef_low))


def edges_kernel(left_ref, right_ref, *refs):
    (ch_ref, cl_ref), (vh_hbm, vl_hbm, g_ref) = refs[6:8], refs[8:11]
    fa, fb, ah, al, bh, bl = fields = refs[11:17]
    sem = refs[17]
    pairs = WINDOW // 2
    first_row = OWN_PAIRS[0] * PAIR + EDGE

    def results(low, high, index):
        rows = pl.ds(low + EDGE, high - low)
        target = pl.ds(low + EDGE - first_row, high - low)
        return [
            pltpu.make_async_copy(ah.at[rows, :], vh_hbm.at[target, :], sem.at[index]),
            pltpu.make_async_copy(al.at[rows, :], vl_hbm.at[target, :], sem.at[index + 1]),
        ]

    inner = OWN_PAIRS[0] + 4, OWN_PAIRS[1] - 4
    stores = results(inner[0] * PAIR, inner[1] * PAIR, 0)
    for store in stores:
        store.start()
    zero = jnp.zeros((EDGE, 256), jnp.bfloat16)
    for ref in (ah, al, bh, bl):
        ref[0:EDGE, :] = zero
        ref[pairs * PAIR + EDGE :, :] = zero
    for pair in range(OWN_PAIRS[0]):
        ingest(left_ref, pair * 8, pair, fa, ah, al)
    for pair in range(OWN_PAIRS[1], pairs):
        ingest(right_ref, (pair - OWN_PAIRS[1]) * 8, pair, fa, ah, al)
    reach = ((0, pairs), (1, pairs - 1), (1, pairs - 1), (2, pairs - 2))
    for count, step in enumerate(steps(ch_ref, cl_ref, *fields)):
        low, high = OWN_PAIRS[0] + 1 + count, OWN_PAIRS[1] - 1 - count
        for pair in list(range(reach[count][0], low)) + list(range(high, reach[count][1])):
            step(pair)
    last = OWN_PAIRS[1] * PAIR + EDGE
    stores += results(OWN_PAIRS[0] * PAIR, inner[0] * PAIR, 2) + results(inner[1] * PAIR, last, 4)
    for store in stores[2:]:
        store.start()
    own = slice(first_row, OWN_PAIRS[1] * PAIR + EDGE)
    dims = ((0,), (0,))
    cross = dot(ah[own, :], al[own, :], dims)
    g_ref[...] = lower_blocks(dot(ah[own, :], ah[own, :], dims) + (cross + cross.T))
    for store in stores:
        store.wait()


def filtered_blocks(received, coef_high, coef_low):
    count = lax.axis_size(ALL)
    chain = [(i, i + 1) for i in range(count - 1)]
    left = lax.ppermute(received[:, 128 - 4 * LEFT :], ALL, chain)
    right = lax.ppermute(received[:, : 4 * (WINDOW - LEFT - 32)], ALL, [(j, i) for i, j in chain])
    state = interior(received, coef_high, coef_low)
    half = pltpu.HBM((2048 + EDGE, 256), jnp.bfloat16)
    fields = [pltpu.VMEM(value.shape, value.dtype) for value in state[:6]]
    return pl.pallas_call(
        edges_kernel,
        out_shape=(half, half, pltpu.VMEM((3 * LANES, LANES), jnp.float32), *fields),
        in_specs=[ON_CHIP] * 10,
        out_specs=(OFF_CHIP,) * 2 + (ON_CHIP,) * 7,
        input_output_aliases={i + 2: i + 3 for i in range(6)},
        scratch_shapes=[pltpu.SemaphoreType.DMA((6,))],
        compiler_params=VMEM,
        name="edges",
    )(left, right, *state)[:3]


def moment_kernel(vh_ref, vl_ref, ch_ref, cl_ref, g_ref, m_ref, bh, bl):
    block, edge = 128, 64

    def image(pair, rows, drop=0):
        vh, vl = vh_ref[rows, :], vl_ref[rows, :]
        c_high, c_low = ch_ref[pair, :, drop:], cl_ref[pair, :, drop:]
        value = dot(
            jnp.concatenate([c_high, c_high, c_low], axis=1), jnp.concatenate([vh, vl, vh], axis=0)
        )
        at = pl.ds((pair - 2) * block, block)
        bh[at, :], bl[at, :] = split(value)

    def body(pair, carry):
        image(pair, pl.ds(pl.multiple_of((pair - 3) * block + edge, edge), 256))
        return carry

    image(2, slice(0, block + edge), edge)
    lax.fori_loop(3, 18, body, 0, unroll=3)
    rows = slice(16 * block - edge, 16 * block)
    c_high, c_low = ch_ref[18, 0:edge, 0:edge], cl_ref[18, 0:edge, 0:edge]
    value = dot(c_high, vh_ref[rows, :]) + (dot(c_high, vl_ref[rows, :]) + dot(c_low, vh_ref[rows, :]))
    bh[16 * block :, :], bl[16 * block :, :] = split(value)
    dims = ((0,), (0,))
    high = vh_ref[...]
    moment = dot(high, bh[...], dims) + (dot(high, bl[...], dims) + dot(vl_ref[...], bh[...], dims))
    m_ref[...] = (0.5 * SCALE) * lower_blocks(moment) + SHIFT * g_ref[...]


def moment_of(vh, vl, coef_high, coef_low, gram):
    return pl.pallas_call(
        moment_kernel,
        out_shape=jax.ShapeDtypeStruct((3 * LANES, LANES), jnp.float32),
        scratch_shapes=[pltpu.VMEM((16 * 128 + 64, 256), jnp.bfloat16)] * 2,
        compiler_params=VMEM,
        cost_estimate=pl.CostEstimate(flops=int(4e9), transcendentals=0, bytes_accessed=int(1e7)),
        name="moment",
    )(*off_chip(vh, vl, coef_high, coef_low), gram)


def panel_solve(block, lines):
    row = lax.broadcasted_iota(jnp.int32, (8, LANES), 0)

    def spread(tile, k):
        return jnp.broadcast_to(tile[k % 8 : k % 8 + 1], tile.shape)

    cols = [
        [jnp.broadcast_to(block[8 * t : 8 * t + 8, j : j + 1], (8, LANES)) for t in range(4)]
        for j in range(32)
    ]
    lines = [
        [lines[8 * t : 8 * t + 8, LANES * h : LANES * h + LANES] for h in range(2)] for t in range(4)
    ]
    pivots = [jnp.ones((8, LANES), jnp.float32) for t in range(4)]
    for k in range(32):
        own = k // 8
        pivot = spread(cols[k][own], k)
        pivots[own] = jnp.where(row == k % 8, pivot, pivots[own])
        scale = 1.0 / pivot
        ratio = {t: cols[k][t] * scale for t in range(own, 4)}
        ratio[own] = jnp.where(row > k % 8, ratio[own], 0.0)
        line = [spread(part, k) for part in lines[own]]
        for j in range(k + 1, 32):
            weight = spread(ratio[j // 8], j)
            for t in range(j // 8, 4):
                cols[j][t] = cols[j][t] - cols[k][t] * weight
        for t in range(own, 4):
            lines[t] = [part - ratio[t] * above for part, above in zip(lines[t], line)]
    roots = [lax.rsqrt(pivots[t]) for t in range(4)]
    return jnp.concatenate(
        [jnp.concatenate([part * roots[t] for part in lines[t]], axis=1) for t in range(4)], axis=0
    )


def half_inverse(aug):
    def panel(p, carry):
        rows = pl.ds(pl.multiple_of(32 * p, 32), 32)
        lines = aug[rows, :]
        lines = panel_solve(pltpu.roll(lines[:, :LANES], LANES - 32 * p, 1), lines)
        aug[rows, :] = lines
        lane = lax.broadcasted_iota(jnp.int32, (32, LANES), 1)
        upper = jnp.where(lane >= 32 * (p + 1), lines[:, :LANES], 0.0)
        aug[...] = aug[...] - dot(upper, lines, ((0,), (0,)), HIGHEST)
        return carry

    lax.fori_loop(0, 4, panel, 0)


def basis_kernel(entries, both_ref, vh_hbm, vl_hbm, w_ref, o_hbm, gram, aug, vh, vl, scr, out, sem, out_sem):
    loads = [
        pltpu.make_async_copy(vh_hbm.at[OWN, :], vh, sem.at[0]),
        pltpu.make_async_copy(vl_hbm.at[OWN, :], vl, sem.at[1]),
    ]
    for load in loads:
        load.start()
    row = lax.broadcasted_iota(jnp.int32, (LANES, LANES), 0)
    eye = (row == lax.broadcasted_iota(jnp.int32, (LANES, LANES), 1)).astype(jnp.float32)
    for d in range(32):
        gram[12 * d : 12 * d + 12, :] = both_ref[24 * d : 24 * d + 12, :] * (1.0 / entries)
    aug[:, :LANES] = gram[:LANES, :]
    aug[:, LANES:] = eye
    half_inverse(aug)
    first = aug[:, LANES:]
    upper = dot(first, gram[LANES : 2 * LANES, :], ((1,), (1,)), HIGHEST)
    aug[:, :LANES] = gram[2 * LANES :, :] - dot(upper, upper, ((0,), (0,)), HIGHEST)
    aug[:, LANES:] = eye
    corner = dot(upper, first, ((0,), (0,)), HIGHEST)
    half_inverse(aug)
    second = aug[:, LANES:]
    w_ref[:LANES, :LANES] = first
    w_ref[:LANES, LANES:] = jnp.zeros((LANES, LANES), jnp.float32)
    w_ref[LANES:, :LANES] = -dot(second, corner, precision=HIGHEST)
    w_ref[LANES:, LANES:] = second
    for load in loads:
        load.wait()
    sends = [pltpu.make_async_copy(out.at[d], o_hbm.at[d], out_sem.at[d]) for d in range(32)]
    for half in range(2):
        used = LANES * (half + 1)
        wh, wl = split(w_ref[LANES * half : used, :used])
        values = [vh[:, :used], vl[:, :used], vh[:, :used]]
        scr[...] = dot(
            jnp.concatenate(values, axis=1), jnp.concatenate([wh, wh, wl], axis=1), ((1,), (1,))
        )
        for slab in range(4):
            pieces = []
            for mid in range(2):
                columns = []
                for column in range(2):
                    at = column * 64 + mid * 32 + slab * 8
                    columns.append(
                        jnp.concatenate(
                            [scr[pair * 128 + at : pair * 128 + at + 8, :] for pair in range(16)], axis=0
                        )
                    )
                pieces += [value.reshape(128, LANES) for value in halves(*columns)]
            for j, piece in enumerate(exchange(pieces, 32)):
                d = (half * 4 + j) * 4 + slab
                out[d] = piece
                sends[d].start()
    for send in sends:
        send.wait()


def basis(both, entries, vh, vl):
    return pl.pallas_call(
        functools.partial(basis_kernel, entries),
        out_shape=(
            jax.ShapeDtypeStruct((256, 256), jnp.float32),
            pltpu.HBM((32, 128, LANES), jnp.float32),
        ),
        in_specs=[ON_CHIP, OFF_CHIP, OFF_CHIP],
        out_specs=(ON_CHIP, OFF_CHIP),
        scratch_shapes=[
            pltpu.VMEM((3 * LANES, LANES), jnp.float32),
            pltpu.VMEM((LANES, 256), jnp.float32),
            pltpu.VMEM((2048, 256), jnp.bfloat16),
            pltpu.VMEM((2048, 256), jnp.bfloat16),
            pltpu.VMEM((2048, LANES), jnp.float32),
            pltpu.VMEM((32, LANES, LANES), jnp.float32),
            pltpu.SemaphoreType.DMA((2,)),
            pltpu.SemaphoreType.DMA((32,)),
        ],
        compiler_params=VMEM,
        cost_estimate=pl.CostEstimate(flops=int(4e9), transcendentals=0, bytes_accessed=int(2e7)),
        name="basis",
    )(both.reshape(768, LANES), *off_chip(vh, vl))


def parts_of(blocks):
    return blocks.reshape(lax.axis_size(ALL), -1, 4, LANES)


def swap(parts):
    rows = parts.reshape((-1,) + parts.shape[-2:])
    return lax.all_to_all(rows, ALL, 0, 0, tiled=True).reshape(parts.shape)


def for_all(share):
    return jnp.broadcast_to(share[None], (lax.axis_size(ALL),) + share.shape)


def project_kernel(entries, moment_ref, w_ref, p_ref):
    first = pl.multiple_of(32 * lax.axis_index("blk"), 32)
    mine = w_ref[pl.ds(first, 32), :]
    left, right = mine[:, :LANES], mine[:, LANES:]
    above, below, last = (moment_ref[LANES * k : LANES * k + LANES, :] for k in range(3))
    half_done = jnp.concatenate(
        [
            dot(left, above, precision=HIGHEST) + dot(right, below, precision=HIGHEST),
            dot(left, below, ((1,), (1,)), HIGHEST) + dot(right, last, precision=HIGHEST),
        ],
        axis=1,
    ) * (1.0 / entries)
    p_ref[...] = dot(half_done, w_ref[...], ((1,), (1,)), HIGHEST)


def project(moment, inverse, entries):
    return pl.pallas_call(
        functools.partial(project_kernel, entries),
        out_shape=jax.ShapeDtypeStruct((32, 256), jnp.float32),
        in_specs=[ON_CHIP] * 2,
        out_specs=ON_CHIP,
        compiler_params=VMEM,
        name="project",
    )(moment, inverse)


def fast(states_in, region, onsite_table, hop_table, coupling_x, coupling_y):
    device = lax.axis_index("blk") * lax.axis_size("slab") + lax.axis_index("slab")
    entries = float(BANDS * 8 * 1024)
    codes = lax.all_gather((region + 1).astype(jnp.float32), "slab", axis=0, tiled=True)
    received = swap(pack(states_in))
    codes = jnp.pad(codes, ((0, 0), (LEFT + 1, LANES)))
    codes = lax.dynamic_slice(codes, (0, 32 * device), (8, LANES))
    coef_high, coef_low = coefficients(codes, onsite_table, hop_table, coupling_x, coupling_y)
    vh, vl, own_gram = filtered_blocks(received, coef_high, coef_low)
    own_moment = moment_of(vh, vl, coef_high, coef_low, own_gram)
    share = swap(parts_of(own_gram)).sum(0)
    both = swap(jnp.concatenate([for_all(share), parts_of(own_moment)], axis=1))
    inverse, blocks = basis(both, entries, vh, vl)
    moment = swap(for_all(both[:, 3:].sum(0))).reshape(3 * LANES, LANES)
    blocks, moment = lax.optimization_barrier((blocks, moment))
    states_out = unpack(swap(blocks))
    projected = project(moment, inverse, entries)
    return states_out, projected


DEGREE = 4


def extended(array, sides, width):
    for axis, dim in sides:
        size, length = (lax.axis_size(axis), array.shape[dim])
        up = [(i, (i + 1) % size) for i in range(size - 1)]
        down = [(j, i) for i, j in up]
        last = lax.slice_in_dim(array, length - width, length, axis=dim)
        leading = lax.slice_in_dim(array, 0, width, axis=dim)
        before = lax.ppermute(last, axis, up)
        after = lax.ppermute(leading, axis, down)
        array = jnp.concatenate([before, array, after], axis=dim)
    return array


def mixing(onsite_table, coupling_x, coupling_y):
    onsite = 0.5 * (onsite_table + jnp.swapaxes(onsite_table, 1, 2))
    blocks = [onsite[material] for material in range(onsite.shape[0])]
    return jnp.concatenate(
        blocks + [0.5 * (coupling_x - coupling_x.T), 0.5 * (coupling_y - coupling_y.T)], axis=1
    )


def masks_of(region):
    codes = jnp.arange(MATERIALS, dtype=jnp.int32)
    return (region[None] == codes[:, None, None]).astype(jnp.float32)


def apply_padded(padded, hop_padded, material_masks, mixing_matrix):
    centre = padded[:, :, 1:-1, 1:-1]
    hop_centre = hop_padded[:, 1:-1, 1:-1]
    kinetic = jnp.zeros_like(centre)
    sides = (
        (padded[:, :, 2:, 1:-1], hop_padded[:, 2:, 1:-1]),
        (padded[:, :, :-2, 1:-1], hop_padded[:, :-2, 1:-1]),
        (padded[:, :, 1:-1, 2:], hop_padded[:, 1:-1, 2:]),
        (padded[:, :, 1:-1, :-2], hop_padded[:, 1:-1, :-2]),
    )
    for field_side, hop_side in sides:
        kinetic = kinetic + (0.5 * (hop_centre + hop_side))[None] * (centre - field_side)
    deriv_rows = 0.5 * (padded[:, :, 2:, 1:-1] - padded[:, :, :-2, 1:-1])
    deriv_cols = 0.5 * (padded[:, :, 1:-1, 2:] - padded[:, :, 1:-1, :-2])
    pieces = [
        material_masks[material][None, None] * centre for material in range(material_masks.shape[0])
    ]
    stacked = jnp.concatenate(pieces + [deriv_rows, deriv_cols], axis=1)
    mixed = jnp.einsum("bc,scxy->sbxy", mixing_matrix, stacked, precision=lax.Precision.HIGHEST)
    return mixed + kinetic


def chebyshev(field, apply_fn):

    def scaled(value):
        return (apply_fn(value) - SHIFT * value) / SCALE

    previous = field
    current = scaled(field)
    for repeat in range(DEGREE - 1):
        previous, current = (current, 2.0 * scaled(current) - previous)
    return current


def inner(left, right):
    return jnp.dot(
        left, right.T, precision=lax.Precision.HIGHEST, preferred_element_type=jnp.float32
    )


def general(states_in, region, onsite_table, hop_table, coupling_x, coupling_y):
    mixing_matrix = mixing(onsite_table, coupling_x, coupling_y)
    material_masks = masks_of(region)
    hop_field = jnp.einsum(
        "mb,mxy->bxy", hop_table, material_masks, precision=lax.Precision.HIGHEST
    )
    hop_rows = extended(hop_field, (("slab", 1),), 1)
    hop_padded = jnp.pad(hop_rows, ((0, 0), (0, 0), (1, 1)))

    def apply_rows(field):
        padded = extended(field, (("slab", 2),), 1)
        padded = jnp.pad(padded, ((0, 0), (0, 0), (0, 0), (1, 1)))
        return apply_padded(padded, hop_padded, material_masks, mixing_matrix)

    filtered = chebyshev(states_in, apply_rows)
    block_count = lax.axis_size("blk")
    slab_count = lax.axis_size("slab")
    states_all = filtered.shape[0] * block_count
    row_count = filtered.shape[2]
    width_all = filtered.shape[3]
    entries = float(BANDS * row_count * slab_count * width_all)
    image = apply_rows(filtered)
    cell_states, cell_image = (
        lax.all_to_all(filtered, "blk", split_axis=3, concat_axis=0, tiled=True),
        lax.all_to_all(image, "blk", split_axis=3, concat_axis=0, tiled=True),
    )
    states_flat = cell_states.reshape(states_all, -1)
    image_flat = cell_image.reshape(states_all, -1)
    moment = lax.psum(inner(states_flat, image_flat) / entries, ("blk", "slab"))

    def panel_step(panel, carry):
        basis_rows, factor_rows = carry
        offset = panel * PANEL
        panel_states = lax.dynamic_slice_in_dim(states_flat, offset, PANEL, 0)
        coeffs = lax.psum(inner(basis_rows, panel_states) / entries, ("blk", "slab"))
        residue = panel_states - jnp.dot(
            coeffs.T,
            basis_rows,
            precision=lax.Precision.HIGHEST,
            preferred_element_type=jnp.float32,
        )
        panel_gram = lax.psum(inner(residue, residue) / entries, ("blk", "slab"))
        panel_factor = jnp.linalg.cholesky(panel_gram)
        panel_basis = lax.linalg.triangular_solve(panel_factor, residue, left_side=True, lower=True)
        basis_rows = lax.dynamic_update_slice_in_dim(basis_rows, panel_basis, offset, 0)
        factor_row = lax.dynamic_update_slice_in_dim(coeffs.T, panel_factor, offset, 1)
        factor_rows = lax.dynamic_update_slice_in_dim(factor_rows, factor_row, offset, 0)
        return (basis_rows, factor_rows)

    start_state = (jnp.zeros_like(states_flat), jnp.zeros((states_all, states_all), jnp.float32))
    basis_flat, factor = lax.fori_loop(0, states_all // PANEL, panel_step, start_state)
    half_done = lax.linalg.triangular_solve(factor, moment, left_side=True, lower=True)
    projected = lax.linalg.triangular_solve(factor, half_done.T, left_side=True, lower=True).T
    basis_cells = basis_flat.reshape(cell_states.shape)
    states_out = lax.all_to_all(basis_cells, "blk", split_axis=0, concat_axis=3, tiled=True)
    owned = states_all // block_count
    projected_rows = lax.dynamic_slice_in_dim(projected, lax.axis_index("blk") * owned, owned, 0)
    return (states_out, projected_rows)


def per_device(states_in, region, *tables):
    known = (lax.axis_size("blk"), lax.axis_size("slab")) == (8, 4)
    run = fast if known and states_in.shape == (32, 8, 2, 1024) else general
    return run(states_in, region, *tables)


def solution(mesh):
    return jax.shard_map(
        per_device,
        mesh=mesh,
        in_specs=(P("blk", None, "slab", None), P("slab", None), P(), P(), P(), P()),
        out_specs=(P("blk", None, "slab", None), P("blk", None)),
        check_vma=False,
    )
```

```python
import functools

import jax
import jax.numpy as jnp
from jax import lax
from jax.experimental import pallas as pl
from jax.experimental.pallas import tpu as pltpu
from jax.sharding import PartitionSpec as P

BANDS = 8
MATERIALS = 4
PANEL = 32
SHIFT = 1.0
SCALE = 3.0
LANES = 128
ALL = ("blk", "slab")
LEFT = 4
WINDOW = 42
VMEM = pltpu.CompilerParams(vmem_limit_bytes=24 * 1024 * 1024)
ON_CHIP = pl.BlockSpec(memory_space=pltpu.VMEM)
OFF_CHIP = pl.BlockSpec(memory_space=pltpu.HBM)
HIGHEST = lax.Precision.HIGHEST
OWN = slice(0, 2048)
OWN_PAIRS = 2, 18
PAIR = 128
EDGE = 64


def off_chip(*arrays):
    return [pltpu.with_memory_space_constraint(array, pltpu.HBM) for array in arrays]


def dot(left, right, dims=((1,), (0,)), precision=None):
    return lax.dot_general(
        left, right, (dims, ((), ())), precision=precision, preferred_element_type=jnp.float32
    )


def split(value):
    high = value.astype(jnp.bfloat16)
    return high, (value - high.astype(jnp.float32)).astype(jnp.bfloat16)


def exchange(pieces, unit):
    count = len(pieces)
    lane = lax.broadcasted_iota(jnp.int32, pieces[0].shape, 1) // unit
    step = count // 2
    while step:
        low = (lane // step) % 2 == 0
        out = list(pieces)
        for i in range(count):
            if (i // step) % 2 == 0:
                a, c = pieces[i], pieces[i + step]
                out[i] = jnp.where(low, a, pltpu.roll(c, step * unit, 1))
                out[i + step] = jnp.where(low, pltpu.roll(a, LANES - step * unit, 1), c)
        pieces = out
        step //= 2
    return pieces


def pack_kernel(x_ref, o_ref, buf, scr, in_sem, out_sem):
    loads = [
        pltpu.make_async_copy(x_ref.at[:, pl.ds(8 * part, 8), :], buf.at[part], in_sem.at[part])
        for part in range(2)
    ]
    for load in loads:
        load.start()
    sends = [
        pltpu.make_async_copy(scr.at[pl.ds(128 * d, 128), :], o_ref.at[d], out_sem.at[d])
        for d in range(32)
    ]
    for part in range(2):
        loads[part].wait()
        rows = buf.at[part].reshape(2048, LANES)
        for tile in range(4):
            for r in range(4):
                row, high = r // 2, r % 2
                parts = [
                    rows[pl.ds((high * 4 + low) * 8 + tile * 2 + row, 32, stride=64), :]
                    for low in range(4)
                ]
                turned = jnp.concatenate(parts, axis=0).T
                scr[pl.ds((512 * part + 128 * tile) * 4 + r, 128, stride=4), :] = turned
        for send in sends[16 * part : 16 * part + 16]:
            send.start()
    for send in sends:
        send.wait()


def pack(x):
    rows = x.reshape(32, 8, 2, 8, LANES).transpose(0, 1, 3, 2, 4).reshape(256, 16, LANES)
    return pl.pallas_call(
        pack_kernel,
        out_shape=pltpu.HBM((32, LANES, LANES), jnp.float32),
        in_specs=[OFF_CHIP],
        out_specs=OFF_CHIP,
        scratch_shapes=[
            pltpu.VMEM((2, 256, 8, LANES), jnp.float32),
            pltpu.VMEM((4096, LANES), jnp.float32),
            pltpu.SemaphoreType.DMA((2,)),
            pltpu.SemaphoreType.DMA((32,)),
        ],
        compiler_params=VMEM,
        name="pack",
    )(*off_chip(rows))


def unpack_kernel(r_ref, o_ref, buf, sem):
    stores = []
    for high in range(2):
        rows = buf.at[high].reshape(2048, LANES)
        for tile in range(8):
            for row in range(2):
                turned = r_ref[pl.ds(tile * 512 + row * 2 + high, 128, stride=4), :].T
                for low in range(4):
                    rows[pl.ds((low * 8 + tile) * 2 + row, 32, stride=64), :] = turned[
                        32 * low : 32 * low + 32
                    ]
        stores.append(
            pltpu.make_async_copy(buf.at[high], o_ref.at[:, pl.ds(64 * high, 64), :], sem.at[high])
        )
        stores[high].start()
    for store in stores:
        store.wait()


def unpack(blocks):
    rows = pl.pallas_call(
        unpack_kernel,
        out_shape=pltpu.HBM((32, 128, LANES), jnp.float32),
        in_specs=[ON_CHIP],
        out_specs=OFF_CHIP,
        scratch_shapes=[pltpu.VMEM((2, 32, 64, LANES), jnp.float32), pltpu.SemaphoreType.DMA((2,))],
        compiler_params=VMEM,
        name="unpack",
    )(blocks.reshape(4096, LANES))
    return rows.reshape(32, 8, 8, 2, LANES).transpose(0, 1, 3, 2, 4).reshape(32, 8, 2, 1024)


def coef_kernel(reg_ref, onsite_ref, hop_ref, kx_ref, ky_ref, ch_ref, cl_ref):
    def decode(index):
        band = (index % 2) * 4 + ((index // 32) % 2) * 2 + (index // 4) % 2
        x = ((index // 8) % 4) * 2 + (index // 2) % 2
        column = (index // 64) % 2
        return band, x, column

    def one_hot(values, shape, axis):
        return (values == lax.broadcasted_iota(jnp.int32, shape, axis)).astype(jnp.float32)

    b_r, x_r, y_r = decode(lax.broadcasted_iota(jnp.int32, (128, 8), 0))
    band_rows = one_hot(b_r, (128, 8), 1)
    b_c, _, _ = decode(lax.broadcasted_iota(jnp.int32, (8, 256), 1) + 64)
    band_cols = one_hot(b_c, (8, 256), 0)
    reg = reg_ref[...]
    hop = dot(band_rows, hop_ref[...], ((1,), (1,)), HIGHEST)

    def table_of(offset):
        return dot(one_hot(x_r + offset, (128, 8), 1), reg, precision=HIGHEST)

    def hops(codes):
        total = jnp.zeros_like(codes)
        for m in range(MATERIALS):
            total = total + jnp.where(codes == m + 1.0, hop[:, m : m + 1], 0.0)
        return total

    second = lax.broadcasted_iota(jnp.int32, (128, LANES), 0) >= 64

    def aligned(table):
        return jnp.where(second, pltpu.roll(table, LANES - 1, 1), table)

    codes = table_of(0)
    here, up, down = hops(codes), hops(table_of(-1)), hops(table_of(1))
    before, after = pltpu.roll(here, 1, 1), pltpu.roll(here, LANES - 1, 1)
    valid = (codes > 0.5).astype(jnp.float32)
    centre = (0.5 * (4.0 * here + up + down + before + after) - SHIFT) * valid
    fields = [aligned((codes == m + 1.0).astype(jnp.float32)) for m in range(MATERIALS)]
    fields += [aligned(valid), aligned(centre)]
    fields += [aligned(-0.5 * (here + side) * valid) for side in (up, down, before, after)]

    b_r, x_r, y_r = decode(lax.broadcasted_iota(jnp.int32, (128, 256), 0))
    k = lax.broadcasted_iota(jnp.int32, (128, 256), 1)
    b_c, x_c, _ = decode(k + 64)
    dy = k // 64 - 1 - y_r
    dx = x_c - x_r
    same = b_r == b_c

    def spread(matrix):
        return dot(dot(band_rows, matrix, precision=HIGHEST), band_cols, precision=HIGHEST)

    here_at, up_at, down_at = (dy == 0) & (dx == 0), (dy == 0) & (dx == -1), (dy == 0) & (dx == 1)
    before_at, after_at = (dy == -1) & (dx == 0), (dy == 1) & (dx == 0)
    onsite = [
        jnp.where(here_at, spread(0.5 * (onsite_ref[m] + onsite_ref[m].T)), 0.0) for m in range(MATERIALS)
    ]
    kx = spread(0.5 * (0.5 * (kx_ref[...] - kx_ref[...].T)))
    ky = spread(0.5 * (0.5 * (ky_ref[...] - ky_ref[...].T)))
    mixed = (
        jnp.where(down_at, kx, 0.0)
        - jnp.where(up_at, kx, 0.0)
        + jnp.where(after_at, ky, 0.0)
        - jnp.where(before_at, ky, 0.0)
    )
    places = [here_at & same, up_at & same, down_at & same, before_at & same, after_at & same]
    for pair in range(WINDOW // 2):
        lane = 2 * pair + 1
        scalar = [field[:, lane : lane + 1] for field in fields]
        value = scalar[4] * mixed
        for m in range(MATERIALS):
            value = value + scalar[m] * onsite[m]
        for place, weight in zip(places, scalar[5:]):
            value = value + jnp.where(place, weight, 0.0)
        high, low = split((2.0 / SCALE) * value)
        ch_ref[pair] = high
        cl_ref[pair] = low


def coefficients(reg, onsite_table, hop_table, coupling_x, coupling_y):
    shape = pltpu.HBM((WINDOW // 2, 128, 256), jnp.bfloat16)
    return pl.pallas_call(
        coef_kernel,
        out_shape=(shape, shape),
        compiler_params=VMEM,
        name="coefficients",
    )(reg, onsite_table, hop_table, coupling_x, coupling_y)


def halves(even, odd):
    even, odd = (value.reshape(-1, 8, LANES) for value in (even, odd))
    first = lax.broadcasted_iota(jnp.int32, (1, 8, LANES), 1) < 4
    return (
        jnp.where(first, even, pltpu.roll(odd, 4, 1)),
        jnp.where(first, pltpu.roll(even, 4, 1), odd),
    )


def lower_blocks(square):
    return jnp.concatenate(
        [square[:LANES, :LANES], square[LANES:, :LANES], square[LANES:, LANES:]], axis=0
    )


def ingest(ref, start, pair, field, high, low):
    at = pair * PAIR
    for half in range(2):
        lanes = slice(half * LANES, half * LANES + LANES)
        for slab in range(4):
            pieces = exchange([ref[(half * 4 + j) * 4 + slab, pl.ds(start, 8), :] for j in range(4)], 32)
            for mid in range(2):
                for column, piece in enumerate(halves(pieces[2 * mid], pieces[2 * mid + 1])):
                    field[pl.ds(at + (column * 64 + mid * 32 + slab * 8), 8), lanes] = piece[0]
    rows = pl.ds(at + EDGE, PAIR)
    high[rows, :], low[rows, :] = split(field[pl.ds(at, PAIR), :])


def product(pair, ch_ref, cl_ref, high, low):
    rows = pl.ds(pair * PAIR, 2 * PAIR)
    vh, vl = high[rows, :], low[rows, :]
    c_high, c_low = ch_ref[pair], cl_ref[pair]
    return dot(
        jnp.concatenate([c_high, c_high, c_low], axis=1), jnp.concatenate([vh, vl, vh], axis=0)
    )


def steps(ch_ref, cl_ref, fa, fb, ah, al, bh, bl):
    def store(pair, value, field, high, low):
        field[pl.ds(pair * PAIR, PAIR), :] = value
        rows = pl.ds(pair * PAIR + EDGE, PAIR)
        high[rows, :], low[rows, :] = split(value)

    def first(pair):
        store(pair, 0.5 * product(pair, ch_ref, cl_ref, ah, al), fb, bh, bl)

    def later(old, high, low, source_high, source_low):
        def step(pair):
            rows = pl.ds(pair * PAIR, PAIR)
            value = product(pair, ch_ref, cl_ref, source_high, source_low) - old[rows, :]
            store(pair, value, old, high, low)

        return step

    even, odd = later(fa, ah, al, bh, bl), later(fb, bh, bl, ah, al)
    return first, even, odd, even


def interior_kernel(r_ref, ch_hbm, cl_hbm, fa, fb, ah, al, bh, bl, ch_ref, cl_ref, sem):
    loads = [
        pltpu.make_async_copy(ch_hbm, ch_ref, sem.at[0]),
        pltpu.make_async_copy(cl_hbm, cl_ref, sem.at[1]),
    ]
    for load in loads:
        load.start()

    def take(pair, carry):
        ingest(r_ref, pl.multiple_of((pair - OWN_PAIRS[0]) * 8, 8), pair, fa, ah, al)
        return carry

    lax.fori_loop(*OWN_PAIRS, take, 0, unroll=2)
    for load in loads:
        load.wait()
    for count, step in enumerate(steps(ch_ref, cl_ref, fa, fb, ah, al, bh, bl)):

        def body(pair, carry, step=step):
            step(pair)
            return carry

        low, high = OWN_PAIRS[0] + 1 + count, OWN_PAIRS[1] - 1 - count
        lax.fori_loop(low, high, body, 0, unroll=high - low)


def interior(received, coef_high, coef_low):
    pairs = WINDOW // 2
    field = pltpu.VMEM((pairs * PAIR, 256), jnp.float32)
    half = pltpu.VMEM((pairs * PAIR + 2 * EDGE, 256), jnp.bfloat16)
    bands = pltpu.VMEM((pairs, PAIR, 256), jnp.bfloat16)
    return pl.pallas_call(
        interior_kernel,
        out_shape=(field,) * 2 + (half,) * 4 + (bands,) * 2,
        in_specs=[ON_CHIP, OFF_CHIP, OFF_CHIP],
        out_specs=(ON_CHIP,) * 8,
        scratch_shapes=[pltpu.SemaphoreType.DMA((2,))],
        compiler_params=VMEM,
        cost_estimate=pl.CostEstimate(flops=int(8e9), transcendentals=0, bytes_accessed=int(2e7)),
        name="interior",
    )(received, *off_chip(coef_high, coef_low))


def edges_kernel(left_ref, right_ref, *refs):
    (ch_ref, cl_ref), (vh_hbm, vl_hbm, g_ref) = refs[6:8], refs[8:11]
    fa, fb, ah, al, bh, bl = fields = refs[11:17]
    sem = refs[17]
    pairs = WINDOW // 2
    first_row = OWN_PAIRS[0] * PAIR + EDGE

    def results(low, high, index):
        rows = pl.ds(low + EDGE, high - low)
        target = pl.ds(low + EDGE - first_row, high - low)
        return [
            pltpu.make_async_copy(ah.at[rows, :], vh_hbm.at[target, :], sem.at[index]),
            pltpu.make_async_copy(al.at[rows, :], vl_hbm.at[target, :], sem.at[index + 1]),
        ]

    inner = OWN_PAIRS[0] + 4, OWN_PAIRS[1] - 4
    stores = results(inner[0] * PAIR, inner[1] * PAIR, 0)
    for store in stores:
        store.start()
    zero = jnp.zeros((EDGE, 256), jnp.bfloat16)
    for ref in (ah, al, bh, bl):
        ref[0:EDGE, :] = zero
        ref[pairs * PAIR + EDGE :, :] = zero
    for pair in range(OWN_PAIRS[0]):
        ingest(left_ref, pair * 8, pair, fa, ah, al)
    for pair in range(OWN_PAIRS[1], pairs):
        ingest(right_ref, (pair - OWN_PAIRS[1]) * 8, pair, fa, ah, al)
    reach = ((0, pairs), (1, pairs - 1), (1, pairs - 1), (2, pairs - 2))
    for count, step in enumerate(steps(ch_ref, cl_ref, *fields)):
        low, high = OWN_PAIRS[0] + 1 + count, OWN_PAIRS[1] - 1 - count
        for pair in list(range(reach[count][0], low)) + list(range(high, reach[count][1])):
            step(pair)
    last = OWN_PAIRS[1] * PAIR + EDGE
    stores += results(OWN_PAIRS[0] * PAIR, inner[0] * PAIR, 2) + results(inner[1] * PAIR, last, 4)
    for store in stores[2:]:
        store.start()
    own = slice(first_row, OWN_PAIRS[1] * PAIR + EDGE)
    dims = ((0,), (0,))
    cross = dot(ah[own, :], al[own, :], dims)
    g_ref[...] = lower_blocks(dot(ah[own, :], ah[own, :], dims) + (cross + cross.T))
    for store in stores:
        store.wait()


def filtered_blocks(received, coef_high, coef_low):
    count = lax.axis_size(ALL)
    chain = [(i, i + 1) for i in range(count - 1)]
    right = lax.ppermute(received[:, : 4 * (WINDOW - LEFT - 32)], ALL, [(j, i) for i, j in chain])
    left = lax.ppermute(received[:, 128 - 4 * LEFT :], ALL, chain)
    state = interior(received, coef_high, coef_low)
    half = pltpu.HBM((2048 + EDGE, 256), jnp.bfloat16)
    fields = [pltpu.VMEM(value.shape, value.dtype) for value in state[:6]]
    return pl.pallas_call(
        edges_kernel,
        out_shape=(half, half, pltpu.VMEM((3 * LANES, LANES), jnp.float32), *fields),
        in_specs=[ON_CHIP] * 10,
        out_specs=(OFF_CHIP,) * 2 + (ON_CHIP,) * 7,
        input_output_aliases={i + 2: i + 3 for i in range(6)},
        scratch_shapes=[pltpu.SemaphoreType.DMA((6,))],
        compiler_params=VMEM,
        name="edges",
    )(left, right, *state)[:3]


def moment_kernel(vh_ref, vl_ref, ch_ref, cl_ref, g_ref, m_ref, bh, bl):
    block, edge = 128, 64

    def image(pair, rows, drop=0):
        vh, vl = vh_ref[rows, :], vl_ref[rows, :]
        c_high, c_low = ch_ref[pair, :, drop:], cl_ref[pair, :, drop:]
        value = dot(
            jnp.concatenate([c_high, c_high, c_low], axis=1), jnp.concatenate([vh, vl, vh], axis=0)
        )
        at = pl.ds((pair - 2) * block, block)
        bh[at, :], bl[at, :] = split(value)

    def body(pair, carry):
        image(pair, pl.ds(pl.multiple_of((pair - 3) * block + edge, edge), 256))
        return carry

    image(2, slice(0, block + edge), edge)
    lax.fori_loop(3, 18, body, 0, unroll=3)
    rows = slice(16 * block - edge, 16 * block)
    c_high, c_low = ch_ref[18, 0:edge, 0:edge], cl_ref[18, 0:edge, 0:edge]
    value = dot(c_high, vh_ref[rows, :]) + (dot(c_high, vl_ref[rows, :]) + dot(c_low, vh_ref[rows, :]))
    bh[16 * block :, :], bl[16 * block :, :] = split(value)
    dims = ((0,), (0,))
    high = vh_ref[...]
    moment = dot(high, bh[...], dims) + (dot(high, bl[...], dims) + dot(vl_ref[...], bh[...], dims))
    m_ref[...] = (0.5 * SCALE) * lower_blocks(moment) + SHIFT * g_ref[...]


def moment_of(vh, vl, coef_high, coef_low, gram):
    return pl.pallas_call(
        moment_kernel,
        out_shape=jax.ShapeDtypeStruct((3 * LANES, LANES), jnp.float32),
        scratch_shapes=[pltpu.VMEM((16 * 128 + 64, 256), jnp.bfloat16)] * 2,
        compiler_params=VMEM,
        cost_estimate=pl.CostEstimate(flops=int(4e9), transcendentals=0, bytes_accessed=int(1e7)),
        name="moment",
    )(*off_chip(vh, vl, coef_high, coef_low), gram)


def panel_solve(block, lines):
    row = lax.broadcasted_iota(jnp.int32, (8, LANES), 0)

    def spread(tile, k):
        return jnp.broadcast_to(tile[k % 8 : k % 8 + 1], tile.shape)

    cols = [
        [jnp.broadcast_to(block[8 * t : 8 * t + 8, j : j + 1], (8, LANES)) for t in range(4)]
        for j in range(32)
    ]
    lines = [
        [lines[8 * t : 8 * t + 8, LANES * h : LANES * h + LANES] for h in range(2)] for t in range(4)
    ]
    pivots = [jnp.ones((8, LANES), jnp.float32) for t in range(4)]
    for k in range(32):
        own = k // 8
        pivot = spread(cols[k][own], k)
        pivots[own] = jnp.where(row == k % 8, pivot, pivots[own])
        scale = 1.0 / pivot
        ratio = {t: cols[k][t] * scale for t in range(own, 4)}
        line = [spread(part, k) for part in lines[own]]
        for j in range(k + 1, 32):
            weight = spread(cols[k][j // 8], j)
            for t in range(j // 8, 4):
                cols[j][t] = cols[j][t] - ratio[t] * weight
        ratio[own] = jnp.where(row > k % 8, ratio[own], 0.0)
        for t in range(own, 4):
            lines[t] = [part - ratio[t] * above for part, above in zip(lines[t], line)]
    roots = [lax.rsqrt(pivots[t]) for t in range(4)]
    return jnp.concatenate(
        [jnp.concatenate([part * roots[t] for part in lines[t]], axis=1) for t in range(4)], axis=0
    )


def half_inverse(aug):
    def panel(p, carry):
        rows = pl.ds(pl.multiple_of(32 * p, 32), 32)
        lines = aug[rows, :]
        lines = panel_solve(pltpu.roll(lines[:, :LANES], LANES - 32 * p, 1), lines)
        aug[rows, :] = lines

        @pl.when(p < 3)
        def update():
            lane = lax.broadcasted_iota(jnp.int32, (32, LANES), 1)
            upper = jnp.where(lane >= 32 * (p + 1), lines[:, :LANES], 0.0)
            aug[...] = aug[...] - dot(upper, lines, ((0,), (0,)), HIGHEST)

        return carry

    lax.fori_loop(0, 4, panel, 0)


def basis_kernel(entries, both_ref, vh_hbm, vl_hbm, w_ref, o_hbm, gram, aug, vh, vl, scr, out, sem, out_sem):
    loads = [
        pltpu.make_async_copy(vh_hbm.at[OWN, :], vh, sem.at[0]),
        pltpu.make_async_copy(vl_hbm.at[OWN, :], vl, sem.at[1]),
    ]
    for load in loads:
        load.start()
    row = lax.broadcasted_iota(jnp.int32, (LANES, LANES), 0)
    eye = (row == lax.broadcasted_iota(jnp.int32, (LANES, LANES), 1)).astype(jnp.float32)
    for d in range(32):
        gram[12 * d : 12 * d + 12, :] = both_ref[24 * d : 24 * d + 12, :] * (1.0 / entries)
    aug[:, :LANES] = gram[:LANES, :]
    aug[:, LANES:] = eye
    half_inverse(aug)
    first = aug[:, LANES:]
    upper = dot(first, gram[LANES : 2 * LANES, :], ((1,), (1,)), HIGHEST)
    aug[:, :LANES] = gram[2 * LANES :, :] - dot(upper, upper, ((0,), (0,)), HIGHEST)
    aug[:, LANES:] = eye
    corner = dot(upper, first, ((0,), (0,)), HIGHEST)
    half_inverse(aug)
    second = aug[:, LANES:]
    w_ref[:LANES, :LANES] = first
    w_ref[:LANES, LANES:] = jnp.zeros((LANES, LANES), jnp.float32)
    w_ref[LANES:, :LANES] = -dot(second, corner, precision=HIGHEST)
    w_ref[LANES:, LANES:] = second
    for load in loads:
        load.wait()
    sends = [pltpu.make_async_copy(out.at[d], o_hbm.at[d], out_sem.at[d]) for d in range(32)]
    for half in range(2):
        used = LANES * (half + 1)
        wh, wl = split(w_ref[LANES * half : used, :used])
        values = [vh[:, :used], vl[:, :used], vh[:, :used]]
        scr[...] = dot(
            jnp.concatenate(values, axis=1), jnp.concatenate([wh, wh, wl], axis=1), ((1,), (1,))
        )
        for slab in range(4):
            pieces = []
            for mid in range(2):
                columns = []
                for column in range(2):
                    at = column * 64 + mid * 32 + slab * 8
                    columns.append(
                        jnp.concatenate(
                            [scr[pair * 128 + at : pair * 128 + at + 8, :] for pair in range(16)], axis=0
                        )
                    )
                pieces += [value.reshape(128, LANES) for value in halves(*columns)]
            for j, piece in enumerate(exchange(pieces, 32)):
                d = (half * 4 + j) * 4 + slab
                out[d] = piece
                sends[d].start()
    for send in sends:
        send.wait()


def basis(both, entries, vh, vl):
    return pl.pallas_call(
        functools.partial(basis_kernel, entries),
        out_shape=(
            jax.ShapeDtypeStruct((256, 256), jnp.float32),
            pltpu.HBM((32, 128, LANES), jnp.float32),
        ),
        in_specs=[ON_CHIP, OFF_CHIP, OFF_CHIP],
        out_specs=(ON_CHIP, OFF_CHIP),
        scratch_shapes=[
            pltpu.VMEM((3 * LANES, LANES), jnp.float32),
            pltpu.VMEM((LANES, 256), jnp.float32),
            pltpu.VMEM((2048, 256), jnp.bfloat16),
            pltpu.VMEM((2048, 256), jnp.bfloat16),
            pltpu.VMEM((2048, LANES), jnp.float32),
            pltpu.VMEM((32, LANES, LANES), jnp.float32),
            pltpu.SemaphoreType.DMA((2,)),
            pltpu.SemaphoreType.DMA((32,)),
        ],
        compiler_params=VMEM,
        cost_estimate=pl.CostEstimate(flops=int(4e9), transcendentals=0, bytes_accessed=int(2e7)),
        name="basis",
    )(both.reshape(768, LANES), *off_chip(vh, vl))


def parts_of(blocks):
    return blocks.reshape(lax.axis_size(ALL), -1, 4, LANES)


def swap(parts):
    rows = parts.reshape((-1,) + parts.shape[-2:])
    return lax.all_to_all(rows, ALL, 0, 0, tiled=True).reshape(parts.shape)


def for_all(share):
    return jnp.broadcast_to(share[None], (lax.axis_size(ALL),) + share.shape)


def project_kernel(entries, moment_ref, w_ref, p_ref):
    first = pl.multiple_of(32 * lax.axis_index("blk"), 32)
    mine = w_ref[pl.ds(first, 32), :]
    left, right = mine[:, :LANES], mine[:, LANES:]
    above, below, last = (moment_ref[LANES * k : LANES * k + LANES, :] for k in range(3))
    half_done = jnp.concatenate(
        [
            dot(left, above, precision=HIGHEST) + dot(right, below, precision=HIGHEST),
            dot(left, below, ((1,), (1,)), HIGHEST) + dot(right, last, precision=HIGHEST),
        ],
        axis=1,
    ) * (1.0 / entries)
    p_ref[...] = dot(half_done, w_ref[...], ((1,), (1,)), HIGHEST)


def project(moment, inverse, entries):
    return pl.pallas_call(
        functools.partial(project_kernel, entries),
        out_shape=jax.ShapeDtypeStruct((32, 256), jnp.float32),
        in_specs=[ON_CHIP] * 2,
        out_specs=ON_CHIP,
        compiler_params=VMEM,
        name="project",
    )(moment, inverse)


def fast(states_in, region, onsite_table, hop_table, coupling_x, coupling_y):
    device = lax.axis_index("blk") * lax.axis_size("slab") + lax.axis_index("slab")
    entries = float(BANDS * 8 * 1024)
    codes = lax.all_gather((region + 1).astype(jnp.float32), "slab", axis=0, tiled=True)
    received = swap(pack(states_in))
    codes = jnp.pad(codes, ((0, 0), (LEFT + 1, LANES)))
    codes = lax.dynamic_slice(codes, (0, 32 * device), (8, LANES))
    coef_high, coef_low = coefficients(codes, onsite_table, hop_table, coupling_x, coupling_y)
    vh, vl, own_gram = filtered_blocks(received, coef_high, coef_low)
    own_moment = moment_of(vh, vl, coef_high, coef_low, own_gram)
    share = swap(parts_of(own_gram)).sum(0)
    both = swap(jnp.concatenate([for_all(share), parts_of(own_moment)], axis=1))
    inverse, blocks = basis(both, entries, vh, vl)
    moment = swap(for_all(both[:, 3:].sum(0))).reshape(3 * LANES, LANES)
    blocks, moment = lax.optimization_barrier((blocks, moment))
    states_out = unpack(swap(blocks))
    projected = project(moment, inverse, entries)
    return states_out, projected


DEGREE = 4


def extended(array, sides, width):
    for axis, dim in sides:
        size, length = (lax.axis_size(axis), array.shape[dim])
        up = [(i, (i + 1) % size) for i in range(size - 1)]
        down = [(j, i) for i, j in up]
        last = lax.slice_in_dim(array, length - width, length, axis=dim)
        leading = lax.slice_in_dim(array, 0, width, axis=dim)
        before = lax.ppermute(last, axis, up)
        after = lax.ppermute(leading, axis, down)
        array = jnp.concatenate([before, array, after], axis=dim)
    return array


def mixing(onsite_table, coupling_x, coupling_y):
    onsite = 0.5 * (onsite_table + jnp.swapaxes(onsite_table, 1, 2))
    blocks = [onsite[material] for material in range(onsite.shape[0])]
    return jnp.concatenate(
        blocks + [0.5 * (coupling_x - coupling_x.T), 0.5 * (coupling_y - coupling_y.T)], axis=1
    )


def masks_of(region):
    codes = jnp.arange(MATERIALS, dtype=jnp.int32)
    return (region[None] == codes[:, None, None]).astype(jnp.float32)


def apply_padded(padded, hop_padded, material_masks, mixing_matrix):
    centre = padded[:, :, 1:-1, 1:-1]
    hop_centre = hop_padded[:, 1:-1, 1:-1]
    kinetic = jnp.zeros_like(centre)
    sides = (
        (padded[:, :, 2:, 1:-1], hop_padded[:, 2:, 1:-1]),
        (padded[:, :, :-2, 1:-1], hop_padded[:, :-2, 1:-1]),
        (padded[:, :, 1:-1, 2:], hop_padded[:, 1:-1, 2:]),
        (padded[:, :, 1:-1, :-2], hop_padded[:, 1:-1, :-2]),
    )
    for field_side, hop_side in sides:
        kinetic = kinetic + (0.5 * (hop_centre + hop_side))[None] * (centre - field_side)
    deriv_rows = 0.5 * (padded[:, :, 2:, 1:-1] - padded[:, :, :-2, 1:-1])
    deriv_cols = 0.5 * (padded[:, :, 1:-1, 2:] - padded[:, :, 1:-1, :-2])
    pieces = [
        material_masks[material][None, None] * centre for material in range(material_masks.shape[0])
    ]
    stacked = jnp.concatenate(pieces + [deriv_rows, deriv_cols], axis=1)
    mixed = jnp.einsum("bc,scxy->sbxy", mixing_matrix, stacked, precision=lax.Precision.HIGHEST)
    return mixed + kinetic


def chebyshev(field, apply_fn):

    def scaled(value):
        return (apply_fn(value) - SHIFT * value) / SCALE

    previous = field
    current = scaled(field)
    for repeat in range(DEGREE - 1):
        previous, current = (current, 2.0 * scaled(current) - previous)
    return current


def inner(left, right):
    return jnp.dot(
        left, right.T, precision=lax.Precision.HIGHEST, preferred_element_type=jnp.float32
    )


def general(states_in, region, onsite_table, hop_table, coupling_x, coupling_y):
    mixing_matrix = mixing(onsite_table, coupling_x, coupling_y)
    material_masks = masks_of(region)
    hop_field = jnp.einsum(
        "mb,mxy->bxy", hop_table, material_masks, precision=lax.Precision.HIGHEST
    )
    hop_rows = extended(hop_field, (("slab", 1),), 1)
    hop_padded = jnp.pad(hop_rows, ((0, 0), (0, 0), (1, 1)))

    def apply_rows(field):
        padded = extended(field, (("slab", 2),), 1)
        padded = jnp.pad(padded, ((0, 0), (0, 0), (0, 0), (1, 1)))
        return apply_padded(padded, hop_padded, material_masks, mixing_matrix)

    filtered = chebyshev(states_in, apply_rows)
    block_count = lax.axis_size("blk")
    slab_count = lax.axis_size("slab")
    states_all = filtered.shape[0] * block_count
    row_count = filtered.shape[2]
    width_all = filtered.shape[3]
    entries = float(BANDS * row_count * slab_count * width_all)
    image = apply_rows(filtered)
    cell_states, cell_image = (
        lax.all_to_all(filtered, "blk", split_axis=3, concat_axis=0, tiled=True),
        lax.all_to_all(image, "blk", split_axis=3, concat_axis=0, tiled=True),
    )
    states_flat = cell_states.reshape(states_all, -1)
    image_flat = cell_image.reshape(states_all, -1)
    moment = lax.psum(inner(states_flat, image_flat) / entries, ("blk", "slab"))

    def panel_step(panel, carry):
        basis_rows, factor_rows = carry
        offset = panel * PANEL
        panel_states = lax.dynamic_slice_in_dim(states_flat, offset, PANEL, 0)
        coeffs = lax.psum(inner(basis_rows, panel_states) / entries, ("blk", "slab"))
        residue = panel_states - jnp.dot(
            coeffs.T,
            basis_rows,
            precision=lax.Precision.HIGHEST,
            preferred_element_type=jnp.float32,
        )
        panel_gram = lax.psum(inner(residue, residue) / entries, ("blk", "slab"))
        panel_factor = jnp.linalg.cholesky(panel_gram)
        panel_basis = lax.linalg.triangular_solve(panel_factor, residue, left_side=True, lower=True)
        basis_rows = lax.dynamic_update_slice_in_dim(basis_rows, panel_basis, offset, 0)
        factor_row = lax.dynamic_update_slice_in_dim(coeffs.T, panel_factor, offset, 1)
        factor_rows = lax.dynamic_update_slice_in_dim(factor_rows, factor_row, offset, 0)
        return (basis_rows, factor_rows)

    start_state = (jnp.zeros_like(states_flat), jnp.zeros((states_all, states_all), jnp.float32))
    basis_flat, factor = lax.fori_loop(0, states_all // PANEL, panel_step, start_state)
    half_done = lax.linalg.triangular_solve(factor, moment, left_side=True, lower=True)
    projected = lax.linalg.triangular_solve(factor, half_done.T, left_side=True, lower=True).T
    basis_cells = basis_flat.reshape(cell_states.shape)
    states_out = lax.all_to_all(basis_cells, "blk", split_axis=0, concat_axis=3, tiled=True)
    owned = states_all // block_count
    projected_rows = lax.dynamic_slice_in_dim(projected, lax.axis_index("blk") * owned, owned, 0)
    return (states_out, projected_rows)


def per_device(states_in, region, *tables):
    known = (lax.axis_size("blk"), lax.axis_size("slab")) == (8, 4)
    run = fast if known and states_in.shape == (32, 8, 2, 1024) else general
    return run(states_in, region, *tables)


def solution(mesh):
    return jax.shard_map(
        per_device,
        mesh=mesh,
        in_specs=(P("blk", None, "slab", None), P("slab", None), P(), P(), P(), P()),
        out_specs=(P("blk", None, "slab", None), P("blk", None)),
        check_vma=False,
    )
```

```python
import functools

import jax
import jax.numpy as jnp
from jax import lax
from jax.experimental import pallas as pl
from jax.experimental.pallas import tpu as pltpu
from jax.sharding import PartitionSpec as P

BANDS = 8
MATERIALS = 4
PANEL = 32
SHIFT = 1.0
SCALE = 3.0
LANES = 128
ALL = ("blk", "slab")
LEFT = 4
RIGHT = 5
WINDOW = 42
VMEM = pltpu.CompilerParams(vmem_limit_bytes=24 * 1024 * 1024)
ON_CHIP = pl.BlockSpec(memory_space=pltpu.VMEM)
OFF_CHIP = pl.BlockSpec(memory_space=pltpu.HBM)
HIGHEST = lax.Precision.HIGHEST
OWN = slice(0, 2048)
OWN_PAIRS = 2, 18
INNER = 6, 14
PAIR = 128
EDGE = 64
PACKED = 320


def off_chip(*arrays):
    return [pltpu.with_memory_space_constraint(array, pltpu.HBM) for array in arrays]


def dot(left, right, dims=((1,), (0,)), precision=None):
    return lax.dot_general(
        left, right, (dims, ((), ())), precision=precision, preferred_element_type=jnp.float32
    )


def split(value):
    high = value.astype(jnp.bfloat16)
    return high, (value - high.astype(jnp.float32)).astype(jnp.bfloat16)


def exchange(pieces, unit):
    count = len(pieces)
    lane = lax.broadcasted_iota(jnp.int32, pieces[0].shape, 1) // unit
    step = count // 2
    while step:
        low = (lane // step) % 2 == 0
        out = list(pieces)
        for i in range(count):
            if (i // step) % 2 == 0:
                a, c = pieces[i], pieces[i + step]
                out[i] = jnp.where(low, a, pltpu.roll(c, step * unit, 1))
                out[i + step] = jnp.where(low, pltpu.roll(a, LANES - step * unit, 1), c)
        pieces = out
        step //= 2
    return pieces


def pack_kernel(x_ref, o_ref, buf, scr, in_sem, out_sem):
    loads = [
        pltpu.make_async_copy(x_ref.at[:, pl.ds(8 * part, 8), :], buf.at[part], in_sem.at[part])
        for part in range(2)
    ]
    for load in loads:
        load.start()
    sends = [
        pltpu.make_async_copy(scr.at[pl.ds(128 * d, 128), :], o_ref.at[d], out_sem.at[d])
        for d in range(32)
    ]
    for part in range(2):
        loads[part].wait()
        rows = buf.at[part].reshape(2048, LANES)
        for tile in range(4):
            for r in range(4):
                row, high = r // 2, r % 2
                parts = [
                    rows[pl.ds((high * 4 + low) * 8 + tile * 2 + row, 32, stride=64), :]
                    for low in range(4)
                ]
                turned = jnp.concatenate(parts, axis=0).T
                scr[pl.ds((512 * part + 128 * tile) * 4 + r, 128, stride=4), :] = turned
        for send in sends[16 * part : 16 * part + 16]:
            send.start()
    for send in sends:
        send.wait()


def pack(x):
    rows = x.reshape(32, 8, 2, 8, LANES).transpose(0, 1, 3, 2, 4).reshape(256, 16, LANES)
    return pl.pallas_call(
        pack_kernel,
        out_shape=pltpu.HBM((32, LANES, LANES), jnp.float32),
        in_specs=[OFF_CHIP],
        out_specs=OFF_CHIP,
        scratch_shapes=[
            pltpu.VMEM((2, 256, 8, LANES), jnp.float32),
            pltpu.VMEM((4096, LANES), jnp.float32),
            pltpu.SemaphoreType.DMA((2,)),
            pltpu.SemaphoreType.DMA((32,)),
        ],
        compiler_params=VMEM,
        name="pack",
    )(*off_chip(rows))


def unpack_kernel(r_ref, o_ref, buf, sem):
    stores = []
    for high in range(2):
        rows = buf.at[high].reshape(2048, LANES)
        for tile in range(8):
            for row in range(2):
                turned = r_ref[pl.ds(tile * 512 + row * 2 + high, 128, stride=4), :].T
                for low in range(4):
                    rows[pl.ds((low * 8 + tile) * 2 + row, 32, stride=64), :] = turned[
                        32 * low : 32 * low + 32
                    ]
        stores.append(
            pltpu.make_async_copy(buf.at[high], o_ref.at[:, pl.ds(64 * high, 64), :], sem.at[high])
        )
        stores[high].start()
    for store in stores:
        store.wait()


def unpack(blocks):
    rows = pl.pallas_call(
        unpack_kernel,
        out_shape=pltpu.HBM((32, 128, LANES), jnp.float32),
        in_specs=[ON_CHIP],
        out_specs=OFF_CHIP,
        scratch_shapes=[pltpu.VMEM((2, 32, 64, LANES), jnp.float32), pltpu.SemaphoreType.DMA((2,))],
        compiler_params=VMEM,
        name="unpack",
    )(blocks.reshape(4096, LANES))
    return rows.reshape(32, 8, 8, 2, LANES).transpose(0, 1, 3, 2, 4).reshape(32, 8, 2, 1024)


def coef_kernel(reg_ref, onsite_ref, hop_ref, kx_ref, ky_ref, ch_ref, cl_ref):
    def decode(index):
        band = (index % 2) * 4 + ((index // 32) % 2) * 2 + (index // 4) % 2
        x = ((index // 8) % 4) * 2 + (index // 2) % 2
        column = (index // 64) % 2
        return band, x, column

    def one_hot(values, shape, axis):
        return (values == lax.broadcasted_iota(jnp.int32, shape, axis)).astype(jnp.float32)

    b_r, x_r, y_r = decode(lax.broadcasted_iota(jnp.int32, (128, 8), 0))
    band_rows = one_hot(b_r, (128, 8), 1)
    b_c, _, _ = decode(lax.broadcasted_iota(jnp.int32, (8, 256), 1) + 64)
    band_cols = one_hot(b_c, (8, 256), 0)
    reg = reg_ref[...]
    hop = dot(band_rows, hop_ref[...], ((1,), (1,)), HIGHEST)

    def table_of(offset):
        return dot(one_hot(x_r + offset, (128, 8), 1), reg, precision=HIGHEST)

    def hops(codes):
        total = jnp.zeros_like(codes)
        for m in range(MATERIALS):
            total = total + jnp.where(codes == m + 1.0, hop[:, m : m + 1], 0.0)
        return total

    second = lax.broadcasted_iota(jnp.int32, (128, LANES), 0) >= 64

    def aligned(table):
        return jnp.where(second, pltpu.roll(table, LANES - 1, 1), table)

    codes = table_of(0)
    here, up, down = hops(codes), hops(table_of(-1)), hops(table_of(1))
    before, after = pltpu.roll(here, 1, 1), pltpu.roll(here, LANES - 1, 1)
    valid = (codes > 0.5).astype(jnp.float32)
    centre = (0.5 * (4.0 * here + up + down + before + after) - SHIFT) * valid
    fields = [aligned((codes == m + 1.0).astype(jnp.float32)) for m in range(MATERIALS)]
    fields += [aligned(valid), aligned(centre)]
    fields += [aligned(-0.5 * (here + side) * valid) for side in (up, down, before, after)]

    b_r, x_r, y_r = decode(lax.broadcasted_iota(jnp.int32, (128, 256), 0))
    k = lax.broadcasted_iota(jnp.int32, (128, 256), 1)
    b_c, x_c, _ = decode(k + 64)
    dy = k // 64 - 1 - y_r
    dx = x_c - x_r
    same = b_r == b_c

    def spread(matrix):
        return dot(dot(band_rows, matrix, precision=HIGHEST), band_cols, precision=HIGHEST)

    here_at, up_at, down_at = (dy == 0) & (dx == 0), (dy == 0) & (dx == -1), (dy == 0) & (dx == 1)
    before_at, after_at = (dy == -1) & (dx == 0), (dy == 1) & (dx == 0)
    onsite = [
        jnp.where(here_at, spread(0.5 * (onsite_ref[m] + onsite_ref[m].T)), 0.0) for m in range(MATERIALS)
    ]
    kx = spread(0.5 * (0.5 * (kx_ref[...] - kx_ref[...].T)))
    ky = spread(0.5 * (0.5 * (ky_ref[...] - ky_ref[...].T)))
    mixed = (
        jnp.where(down_at, kx, 0.0)
        - jnp.where(up_at, kx, 0.0)
        + jnp.where(after_at, ky, 0.0)
        - jnp.where(before_at, ky, 0.0)
    )
    places = [here_at & same, up_at & same, down_at & same, before_at & same, after_at & same]
    for pair in range(WINDOW // 2):
        lane = 2 * pair + 1
        scalar = [field[:, lane : lane + 1] for field in fields]
        value = scalar[4] * mixed
        for m in range(MATERIALS):
            value = value + scalar[m] * onsite[m]
        for place, weight in zip(places, scalar[5:]):
            value = value + jnp.where(place, weight, 0.0)
        high, low = split((2.0 / SCALE) * value)
        ch_ref[pair] = high
        cl_ref[pair] = low


def coefficients(reg, onsite_table, hop_table, coupling_x, coupling_y):
    shape = pltpu.HBM((WINDOW // 2, 128, 256), jnp.bfloat16)
    return pl.pallas_call(
        coef_kernel,
        out_shape=(shape, shape),
        compiler_params=VMEM,
        name="coefficients",
    )(reg, onsite_table, hop_table, coupling_x, coupling_y)


def halves(even, odd):
    even, odd = (value.reshape(-1, 8, LANES) for value in (even, odd))
    first = lax.broadcasted_iota(jnp.int32, (1, 8, LANES), 1) < 4
    return (
        jnp.where(first, even, pltpu.roll(odd, 4, 1)),
        jnp.where(first, pltpu.roll(even, 4, 1), odd),
    )


def lower_blocks(square):
    first, last = square[:LANES, :LANES], square[LANES:, LANES:]
    left = lax.broadcasted_iota(jnp.int32, (64, LANES), 1) < 64
    corners = jnp.where(left, first[:64], pltpu.roll(last[:64], 64, 1))
    return jnp.concatenate([corners, first[64:], last[64:], square[LANES:, :LANES]], axis=0)


def whole_blocks(rows):
    row = lax.broadcasted_iota(jnp.int32, (LANES, LANES), 0)
    upper = (row < 64) & (lax.broadcasted_iota(jnp.int32, (LANES, LANES), 1) >= 64)

    def mirrored(top, bottom):
        block = jnp.concatenate([top, bottom], axis=0)
        return jnp.where(upper, block.T, block)

    first = mirrored(rows[:64], rows[64:128])
    return first, rows[192:], mirrored(pltpu.roll(rows[:64], 64, 1), rows[128:192])


def ingest(load, pair, field, high, low):
    at = pair * PAIR
    for half in range(2):
        lanes = slice(half * LANES, half * LANES + LANES)
        for slab in range(4):
            pieces = exchange([load((half * 4 + j) * 4 + slab) for j in range(4)], 32)
            for mid in range(2):
                for column, piece in enumerate(halves(pieces[2 * mid], pieces[2 * mid + 1])):
                    field[pl.ds(at + (column * 64 + mid * 32 + slab * 8), 8), lanes] = piece[0]
    rows = pl.ds(at + EDGE, PAIR)
    high[rows, :], low[rows, :] = split(field[pl.ds(at, PAIR), :])


def product(pair, ch_ref, cl_ref, high, low):
    rows = pl.ds(pair * PAIR, 2 * PAIR)
    vh, vl = high[rows, :], low[rows, :]
    c_high, c_low = ch_ref[pair], cl_ref[pair]
    return dot(
        jnp.concatenate([c_high, c_high, c_low], axis=1), jnp.concatenate([vh, vl, vh], axis=0)
    )


def steps(ch_ref, cl_ref, fa, fb, ah, al, bh, bl):
    def store(pair, value, field, high, low):
        field[pl.ds(pair * PAIR, PAIR), :] = value
        rows = pl.ds(pair * PAIR + EDGE, PAIR)
        high[rows, :], low[rows, :] = split(value)

    def first(pair):
        store(pair, 0.5 * product(pair, ch_ref, cl_ref, ah, al), fb, bh, bl)

    def later(old, high, low, source_high, source_low):
        def step(pair):
            rows = pl.ds(pair * PAIR, PAIR)
            value = product(pair, ch_ref, cl_ref, source_high, source_low) - old[rows, :]
            store(pair, value, old, high, low)

        return step

    even, odd = later(fa, ah, al, bh, bl), later(fb, bh, bl, ah, al)
    return first, even, odd, even


def gram_of(high, low):
    dims = ((0,), (0,))
    cross = dot(high, low, dims)
    return dot(high, high, dims) + (cross + cross.T)


def interior_kernel(r_ref, ch_hbm, cl_hbm, fa, fb, ah, al, bh, bl, ch_ref, cl_ref, g_ref, sem):
    loads = [
        pltpu.make_async_copy(ch_hbm, ch_ref, sem.at[0]),
        pltpu.make_async_copy(cl_hbm, cl_ref, sem.at[1]),
    ]
    for load in loads:
        load.start()

    def take(pair, carry):
        rows = pl.ds(pl.multiple_of((pair - OWN_PAIRS[0]) * 8, 8), 8)
        ingest(lambda source: r_ref[source, rows, :], pair, fa, ah, al)
        return carry

    lax.fori_loop(*OWN_PAIRS, take, 0, unroll=2)
    for load in loads:
        load.wait()
    for count, step in enumerate(steps(ch_ref, cl_ref, fa, fb, ah, al, bh, bl)):

        def body(pair, carry, step=step):
            step(pair)
            return carry

        low, high = OWN_PAIRS[0] + 1 + count, OWN_PAIRS[1] - 1 - count
        lax.fori_loop(low, high, body, 0, unroll=high - low)
    rows = slice(INNER[0] * PAIR + EDGE, INNER[1] * PAIR + EDGE)
    g_ref[...] = gram_of(ah[rows, :], al[rows, :])


def interior(received, coef_high, coef_low):
    pairs = WINDOW // 2
    field = pltpu.VMEM((pairs * PAIR, 256), jnp.float32)
    half = pltpu.VMEM((pairs * PAIR + 2 * EDGE, 256), jnp.bfloat16)
    bands = pltpu.VMEM((pairs, PAIR, 256), jnp.bfloat16)
    return pl.pallas_call(
        interior_kernel,
        out_shape=(field,) * 2 + (half,) * 4 + (bands,) * 2 + (pltpu.VMEM((256, 256), jnp.float32),),
        in_specs=[ON_CHIP, OFF_CHIP, OFF_CHIP],
        out_specs=(ON_CHIP,) * 9,
        scratch_shapes=[pltpu.SemaphoreType.DMA((2,))],
        compiler_params=VMEM,
        cost_estimate=pl.CostEstimate(flops=int(8e9), transcendentals=0, bytes_accessed=int(2e7)),
        name="interior",
    )(received, *off_chip(coef_high, coef_low))


def edges_kernel(left_ref, right_ref, *refs):
    (ch_ref, cl_ref, inner_ref), (vh_hbm, vl_hbm, g_ref) = refs[6:9], refs[9:12]
    fa, fb, ah, al, bh, bl = fields = refs[12:18]
    sem = refs[18]
    pairs = WINDOW // 2
    first_row = OWN_PAIRS[0] * PAIR + EDGE

    def results(low, high, index):
        rows = pl.ds(low + EDGE, high - low)
        target = pl.ds(low + EDGE - first_row, high - low)
        return [
            pltpu.make_async_copy(ah.at[rows, :], vh_hbm.at[target, :], sem.at[index]),
            pltpu.make_async_copy(al.at[rows, :], vl_hbm.at[target, :], sem.at[index + 1]),
        ]

    stores = results(INNER[0] * PAIR, INNER[1] * PAIR, 0)
    for store in stores:
        store.start()
    zero = jnp.zeros((EDGE, 256), jnp.bfloat16)
    for ref in (ah, al, bh, bl):
        ref[0:EDGE, :] = zero
        ref[pairs * PAIR + EDGE :, :] = zero
    for pair in range(OWN_PAIRS[0]):
        ingest(lambda source, pair=pair: left_ref[source, 8 * pair : 8 * pair + 8, :], pair, fa, ah, al)
    for pair in range(OWN_PAIRS[1], pairs):

        def load(source, start=8 * (pair - OWN_PAIRS[1])):
            count = min(8, 4 * RIGHT - start)
            rows = right_ref[4 * RIGHT * source + start : 4 * RIGHT * source + start + count, :]
            return rows if count == 8 else jnp.concatenate([rows, jnp.zeros_like(rows)], axis=0)

        ingest(load, pair, fa, ah, al)
    reach = ((0, pairs), (1, pairs - 1), (1, pairs - 1), (2, pairs - 2))
    for count, step in enumerate(steps(ch_ref, cl_ref, *fields)):
        low, high = OWN_PAIRS[0] + 1 + count, OWN_PAIRS[1] - 1 - count
        for pair in list(range(reach[count][0], low)) + list(range(high, reach[count][1])):
            step(pair)
    last = OWN_PAIRS[1] * PAIR + EDGE
    stores += results(OWN_PAIRS[0] * PAIR, INNER[0] * PAIR, 2) + results(INNER[1] * PAIR, last, 4)
    for store in stores[2:]:
        store.start()
    before = slice(first_row, INNER[0] * PAIR + EDGE)
    after = slice(INNER[1] * PAIR + EDGE, OWN_PAIRS[1] * PAIR + EDGE)
    high, low = (jnp.concatenate([ref[before, :], ref[after, :]], axis=0) for ref in (ah, al))
    g_ref[...] = lower_blocks(inner_ref[...] + gram_of(high, low))
    for store in stores:
        store.wait()


def filtered_blocks(received, coef_high, coef_low):
    count = lax.axis_size(ALL)
    chain = [(i, i + 1) for i in range(count - 1)]
    leading = received.reshape(count, 32, 4, LANES)[:, :RIGHT]
    right = lax.ppermute(leading, ALL, [(j, i) for i, j in chain]).reshape(-1, LANES)
    left = lax.ppermute(received[:, 128 - 4 * LEFT :], ALL, chain)
    state = interior(received, coef_high, coef_low)
    half = pltpu.HBM((2048 + EDGE, 256), jnp.bfloat16)
    fields = [pltpu.VMEM(value.shape, value.dtype) for value in state[:6]]
    return pl.pallas_call(
        edges_kernel,
        out_shape=(half, half, pltpu.VMEM((PACKED, LANES), jnp.float32), *fields),
        in_specs=[ON_CHIP] * 11,
        out_specs=(OFF_CHIP,) * 2 + (ON_CHIP,) * 7,
        input_output_aliases={i + 2: i + 3 for i in range(6)},
        scratch_shapes=[pltpu.SemaphoreType.DMA((6,))],
        compiler_params=VMEM,
        name="edges",
    )(left, right, *state)[:3]


def moment_kernel(vh_ref, vl_ref, ch_ref, cl_ref, g_ref, m_ref, bh, bl):
    block, edge = 128, 64

    def image(pair, rows, drop=0):
        vh, vl = vh_ref[rows, :], vl_ref[rows, :]
        c_high, c_low = ch_ref[pair, :, drop:], cl_ref[pair, :, drop:]
        value = dot(
            jnp.concatenate([c_high, c_high, c_low], axis=1), jnp.concatenate([vh, vl, vh], axis=0)
        )
        at = pl.ds((pair - 2) * block, block)
        bh[at, :], bl[at, :] = split(value)

    def body(pair, carry):
        image(pair, pl.ds(pl.multiple_of((pair - 3) * block + edge, edge), 256))
        return carry

    image(2, slice(0, block + edge), edge)
    lax.fori_loop(3, 18, body, 0, unroll=3)
    rows = slice(16 * block - edge, 16 * block)
    c_high, c_low = ch_ref[18, 0:edge, 0:edge], cl_ref[18, 0:edge, 0:edge]
    value = dot(c_high, vh_ref[rows, :]) + (dot(c_high, vl_ref[rows, :]) + dot(c_low, vh_ref[rows, :]))
    bh[16 * block :, :], bl[16 * block :, :] = split(value)
    dims = ((0,), (0,))
    high = vh_ref[...]
    moment = dot(high, bh[...], dims) + (dot(high, bl[...], dims) + dot(vl_ref[...], bh[...], dims))
    m_ref[...] = (0.5 * SCALE) * lower_blocks(moment) + SHIFT * g_ref[...]


def moment_of(vh, vl, coef_high, coef_low, gram):
    return pl.pallas_call(
        moment_kernel,
        out_shape=jax.ShapeDtypeStruct((PACKED, LANES), jnp.float32),
        scratch_shapes=[pltpu.VMEM((16 * 128 + 64, 256), jnp.bfloat16)] * 2,
        compiler_params=VMEM,
        cost_estimate=pl.CostEstimate(flops=int(4e9), transcendentals=0, bytes_accessed=int(1e7)),
        name="moment",
    )(*off_chip(vh, vl, coef_high, coef_low), gram)


def panel_solve(block, lines):
    row = lax.broadcasted_iota(jnp.int32, (8, LANES), 0)

    def spread(tile, k):
        return jnp.broadcast_to(tile[k % 8 : k % 8 + 1], tile.shape)

    cols = [
        [jnp.broadcast_to(block[8 * t : 8 * t + 8, j : j + 1], (8, LANES)) for t in range(4)]
        for j in range(32)
    ]
    lines = [
        [lines[8 * t : 8 * t + 8, LANES * h : LANES * h + LANES] for h in range(2)] for t in range(4)
    ]
    pivots = [jnp.ones((8, LANES), jnp.float32) for t in range(4)]
    for k in range(32):
        own = k // 8
        pivot = spread(cols[k][own], k)
        pivots[own] = jnp.where(row == k % 8, pivot, pivots[own])
        scale = 1.0 / pivot
        ratio = {t: cols[k][t] * scale for t in range(own, 4)}
        line = [spread(part, k) for part in lines[own]]
        for j in range(k + 1, 32):
            weight = spread(cols[k][j // 8], j)
            for t in range(j // 8, 4):
                cols[j][t] = cols[j][t] - ratio[t] * weight
        ratio[own] = jnp.where(row > k % 8, ratio[own], 0.0)
        for t in range(own, 4):
            lines[t] = [part - ratio[t] * above for part, above in zip(lines[t], line)]
    roots = [lax.rsqrt(pivots[t]) for t in range(4)]
    return jnp.concatenate(
        [jnp.concatenate([part * roots[t] for part in lines[t]], axis=1) for t in range(4)], axis=0
    )


def half_inverse(aug):
    def panel(p, carry):
        rows = pl.ds(pl.multiple_of(32 * p, 32), 32)
        lines = aug[rows, :]
        lines = panel_solve(pltpu.roll(lines[:, :LANES], LANES - 32 * p, 1), lines)
        aug[rows, :] = lines

        @pl.when(p < 3)
        def update():
            lane = lax.broadcasted_iota(jnp.int32, (32, LANES), 1)
            upper = jnp.where(lane >= 32 * (p + 1), lines[:, :LANES], 0.0)
            aug[...] = aug[...] - dot(upper, lines, ((0,), (0,)), HIGHEST)

        return carry

    lax.fori_loop(0, 4, panel, 0)


def basis_kernel(entries, both_ref, vh_hbm, vl_hbm, w_ref, o_hbm, gram, aug, vh, vl, scr, out, sem, out_sem):
    loads = [
        pltpu.make_async_copy(vh_hbm.at[OWN, :], vh, sem.at[0]),
        pltpu.make_async_copy(vl_hbm.at[OWN, :], vl, sem.at[1]),
    ]
    for load in loads:
        load.start()
    row = lax.broadcasted_iota(jnp.int32, (LANES, LANES), 0)
    eye = (row == lax.broadcasted_iota(jnp.int32, (LANES, LANES), 1)).astype(jnp.float32)
    for d in range(32):
        gram[10 * d : 10 * d + 10, :] = both_ref[20 * d : 20 * d + 10, :] * (1.0 / entries)
    above, below, after = whole_blocks(gram[...])
    aug[:, :LANES] = above
    aug[:, LANES:] = eye
    half_inverse(aug)
    first = aug[:, LANES:]
    upper = dot(first, below, ((1,), (1,)), HIGHEST)
    aug[:, :LANES] = after - dot(upper, upper, ((0,), (0,)), HIGHEST)
    aug[:, LANES:] = eye
    corner = dot(upper, first, ((0,), (0,)), HIGHEST)
    half_inverse(aug)
    second = aug[:, LANES:]
    w_ref[:LANES, :LANES] = first
    w_ref[:LANES, LANES:] = jnp.zeros((LANES, LANES), jnp.float32)
    w_ref[LANES:, :LANES] = -dot(second, corner, precision=HIGHEST)
    w_ref[LANES:, LANES:] = second
    for load in loads:
        load.wait()
    sends = [pltpu.make_async_copy(out.at[d], o_hbm.at[d], out_sem.at[d]) for d in range(32)]
    for half in range(2):
        used = LANES * (half + 1)
        wh, wl = split(w_ref[LANES * half : used, :used])
        values = [vh[:, :used], vl[:, :used], vh[:, :used]]
        scr[...] = dot(
            jnp.concatenate(values, axis=1), jnp.concatenate([wh, wh, wl], axis=1), ((1,), (1,))
        )
        for slab in range(4):
            pieces = []
            for mid in range(2):
                columns = []
                for column in range(2):
                    at = column * 64 + mid * 32 + slab * 8
                    columns.append(
                        jnp.concatenate(
                            [scr[pair * 128 + at : pair * 128 + at + 8, :] for pair in range(16)], axis=0
                        )
                    )
                pieces += [value.reshape(128, LANES) for value in halves(*columns)]
            for j, piece in enumerate(exchange(pieces, 32)):
                d = (half * 4 + j) * 4 + slab
                out[d] = piece
                sends[d].start()
    for send in sends:
        send.wait()


def basis(both, entries, vh, vl):
    return pl.pallas_call(
        functools.partial(basis_kernel, entries),
        out_shape=(
            jax.ShapeDtypeStruct((256, 256), jnp.float32),
            pltpu.HBM((32, 128, LANES), jnp.float32),
        ),
        in_specs=[ON_CHIP, OFF_CHIP, OFF_CHIP],
        out_specs=(ON_CHIP, OFF_CHIP),
        scratch_shapes=[
            pltpu.VMEM((PACKED, LANES), jnp.float32),
            pltpu.VMEM((LANES, 256), jnp.float32),
            pltpu.VMEM((2048, 256), jnp.bfloat16),
            pltpu.VMEM((2048, 256), jnp.bfloat16),
            pltpu.VMEM((2048, LANES), jnp.float32),
            pltpu.VMEM((32, LANES, LANES), jnp.float32),
            pltpu.SemaphoreType.DMA((2,)),
            pltpu.SemaphoreType.DMA((32,)),
        ],
        compiler_params=VMEM,
        cost_estimate=pl.CostEstimate(flops=int(4e9), transcendentals=0, bytes_accessed=int(2e7)),
        name="basis",
    )(both.reshape(2 * PACKED, LANES), *off_chip(vh, vl))


def parts_of(blocks):
    return blocks.reshape(lax.axis_size(ALL), -1, 2, LANES)


def swap(parts):
    rows = parts.reshape((-1,) + parts.shape[-2:])
    return lax.all_to_all(rows, ALL, 0, 0, tiled=True).reshape(parts.shape)


def for_all(share):
    return jnp.broadcast_to(share[None], (lax.axis_size(ALL),) + share.shape)


def project_kernel(entries, moment_ref, w_ref, p_ref):
    first = pl.multiple_of(32 * lax.axis_index("blk"), 32)
    mine = w_ref[pl.ds(first, 32), :]
    left, right = mine[:, :LANES], mine[:, LANES:]
    above, below, last = whole_blocks(moment_ref[...])
    half_done = jnp.concatenate(
        [
            dot(left, above, precision=HIGHEST) + dot(right, below, precision=HIGHEST),
            dot(left, below, ((1,), (1,)), HIGHEST) + dot(right, last, precision=HIGHEST),
        ],
        axis=1,
    ) * (1.0 / entries)
    p_ref[...] = dot(half_done, w_ref[...], ((1,), (1,)), HIGHEST)


def project(moment, inverse, entries):
    return pl.pallas_call(
        functools.partial(project_kernel, entries),
        out_shape=jax.ShapeDtypeStruct((32, 256), jnp.float32),
        in_specs=[ON_CHIP] * 2,
        out_specs=ON_CHIP,
        compiler_params=VMEM,
        name="project",
    )(moment, inverse)


def fast(states_in, region, onsite_table, hop_table, coupling_x, coupling_y):
    device = lax.axis_index("blk") * lax.axis_size("slab") + lax.axis_index("slab")
    entries = float(BANDS * 8 * 1024)
    codes = lax.all_gather((region + 1).astype(jnp.float32), "slab", axis=0, tiled=True)
    received = swap(pack(states_in))
    codes = jnp.pad(codes, ((0, 0), (LEFT + 1, LANES)))
    codes = lax.dynamic_slice(codes, (0, 32 * device), (8, LANES))
    coef_high, coef_low = coefficients(codes, onsite_table, hop_table, coupling_x, coupling_y)
    vh, vl, own_gram = filtered_blocks(received, coef_high, coef_low)
    own_moment = moment_of(vh, vl, coef_high, coef_low, own_gram)
    share = swap(parts_of(own_gram)).sum(0)
    both = swap(jnp.concatenate([for_all(share), parts_of(own_moment)], axis=1))
    inverse, blocks = basis(both, entries, vh, vl)
    moment = swap(for_all(both[:, 5:].sum(0))).reshape(PACKED, LANES)
    blocks, moment = lax.optimization_barrier((blocks, moment))
    states_out = unpack(swap(blocks))
    projected = project(moment, inverse, entries)
    return states_out, projected


DEGREE = 4


def extended(array, sides, width):
    for axis, dim in sides:
        size, length = (lax.axis_size(axis), array.shape[dim])
        up = [(i, (i + 1) % size) for i in range(size - 1)]
        down = [(j, i) for i, j in up]
        last = lax.slice_in_dim(array, length - width, length, axis=dim)
        leading = lax.slice_in_dim(array, 0, width, axis=dim)
        before = lax.ppermute(last, axis, up)
        after = lax.ppermute(leading, axis, down)
        array = jnp.concatenate([before, array, after], axis=dim)
    return array


def mixing(onsite_table, coupling_x, coupling_y):
    onsite = 0.5 * (onsite_table + jnp.swapaxes(onsite_table, 1, 2))
    blocks = [onsite[material] for material in range(onsite.shape[0])]
    return jnp.concatenate(
        blocks + [0.5 * (coupling_x - coupling_x.T), 0.5 * (coupling_y - coupling_y.T)], axis=1
    )


def masks_of(region):
    codes = jnp.arange(MATERIALS, dtype=jnp.int32)
    return (region[None] == codes[:, None, None]).astype(jnp.float32)


def apply_padded(padded, hop_padded, material_masks, mixing_matrix):
    centre = padded[:, :, 1:-1, 1:-1]
    hop_centre = hop_padded[:, 1:-1, 1:-1]
    kinetic = jnp.zeros_like(centre)
    sides = (
        (padded[:, :, 2:, 1:-1], hop_padded[:, 2:, 1:-1]),
        (padded[:, :, :-2, 1:-1], hop_padded[:, :-2, 1:-1]),
        (padded[:, :, 1:-1, 2:], hop_padded[:, 1:-1, 2:]),
        (padded[:, :, 1:-1, :-2], hop_padded[:, 1:-1, :-2]),
    )
    for field_side, hop_side in sides:
        kinetic = kinetic + (0.5 * (hop_centre + hop_side))[None] * (centre - field_side)
    deriv_rows = 0.5 * (padded[:, :, 2:, 1:-1] - padded[:, :, :-2, 1:-1])
    deriv_cols = 0.5 * (padded[:, :, 1:-1, 2:] - padded[:, :, 1:-1, :-2])
    pieces = [
        material_masks[material][None, None] * centre for material in range(material_masks.shape[0])
    ]
    stacked = jnp.concatenate(pieces + [deriv_rows, deriv_cols], axis=1)
    mixed = jnp.einsum("bc,scxy->sbxy", mixing_matrix, stacked, precision=lax.Precision.HIGHEST)
    return mixed + kinetic


def chebyshev(field, apply_fn):

    def scaled(value):
        return (apply_fn(value) - SHIFT * value) / SCALE

    previous = field
    current = scaled(field)
    for repeat in range(DEGREE - 1):
        previous, current = (current, 2.0 * scaled(current) - previous)
    return current


def inner(left, right):
    return jnp.dot(
        left, right.T, precision=lax.Precision.HIGHEST, preferred_element_type=jnp.float32
    )


def general(states_in, region, onsite_table, hop_table, coupling_x, coupling_y):
    mixing_matrix = mixing(onsite_table, coupling_x, coupling_y)
    material_masks = masks_of(region)
    hop_field = jnp.einsum(
        "mb,mxy->bxy", hop_table, material_masks, precision=lax.Precision.HIGHEST
    )
    hop_rows = extended(hop_field, (("slab", 1),), 1)
    hop_padded = jnp.pad(hop_rows, ((0, 0), (0, 0), (1, 1)))

    def apply_rows(field):
        padded = extended(field, (("slab", 2),), 1)
        padded = jnp.pad(padded, ((0, 0), (0, 0), (0, 0), (1, 1)))
        return apply_padded(padded, hop_padded, material_masks, mixing_matrix)

    filtered = chebyshev(states_in, apply_rows)
    block_count = lax.axis_size("blk")
    slab_count = lax.axis_size("slab")
    states_all = filtered.shape[0] * block_count
    row_count = filtered.shape[2]
    width_all = filtered.shape[3]
    entries = float(BANDS * row_count * slab_count * width_all)
    image = apply_rows(filtered)
    cell_states, cell_image = (
        lax.all_to_all(filtered, "blk", split_axis=3, concat_axis=0, tiled=True),
        lax.all_to_all(image, "blk", split_axis=3, concat_axis=0, tiled=True),
    )
    states_flat = cell_states.reshape(states_all, -1)
    image_flat = cell_image.reshape(states_all, -1)
    moment = lax.psum(inner(states_flat, image_flat) / entries, ("blk", "slab"))

    def panel_step(panel, carry):
        basis_rows, factor_rows = carry
        offset = panel * PANEL
        panel_states = lax.dynamic_slice_in_dim(states_flat, offset, PANEL, 0)
        coeffs = lax.psum(inner(basis_rows, panel_states) / entries, ("blk", "slab"))
        residue = panel_states - jnp.dot(
            coeffs.T,
            basis_rows,
            precision=lax.Precision.HIGHEST,
            preferred_element_type=jnp.float32,
        )
        panel_gram = lax.psum(inner(residue, residue) / entries, ("blk", "slab"))
        panel_factor = jnp.linalg.cholesky(panel_gram)
        panel_basis = lax.linalg.triangular_solve(panel_factor, residue, left_side=True, lower=True)
        basis_rows = lax.dynamic_update_slice_in_dim(basis_rows, panel_basis, offset, 0)
        factor_row = lax.dynamic_update_slice_in_dim(coeffs.T, panel_factor, offset, 1)
        factor_rows = lax.dynamic_update_slice_in_dim(factor_rows, factor_row, offset, 0)
        return (basis_rows, factor_rows)

    start_state = (jnp.zeros_like(states_flat), jnp.zeros((states_all, states_all), jnp.float32))
    basis_flat, factor = lax.fori_loop(0, states_all // PANEL, panel_step, start_state)
    half_done = lax.linalg.triangular_solve(factor, moment, left_side=True, lower=True)
    projected = lax.linalg.triangular_solve(factor, half_done.T, left_side=True, lower=True).T
    basis_cells = basis_flat.reshape(cell_states.shape)
    states_out = lax.all_to_all(basis_cells, "blk", split_axis=0, concat_axis=3, tiled=True)
    owned = states_all // block_count
    projected_rows = lax.dynamic_slice_in_dim(projected, lax.axis_index("blk") * owned, owned, 0)
    return (states_out, projected_rows)


def per_device(states_in, region, *tables):
    known = (lax.axis_size("blk"), lax.axis_size("slab")) == (8, 4)
    run = fast if known and states_in.shape == (32, 8, 2, 1024) else general
    return run(states_in, region, *tables)


def solution(mesh):
    return jax.shard_map(
        per_device,
        mesh=mesh,
        in_specs=(P("blk", None, "slab", None), P("slab", None), P(), P(), P(), P()),
        out_specs=(P("blk", None, "slab", None), P("blk", None)),
        check_vma=False,
    )
```

```python
import functools

import jax
import jax.numpy as jnp
from jax import lax
from jax.experimental import pallas as pl
from jax.experimental.pallas import tpu as pltpu
from jax.sharding import PartitionSpec as P

BANDS = 8
MATERIALS = 4
PANEL = 32
SHIFT = 1.0
SCALE = 3.0
LANES = 128
ALL = ("blk", "slab")
LEFT = 4
RIGHT = 5
WINDOW = 42
VMEM = pltpu.CompilerParams(vmem_limit_bytes=24 * 1024 * 1024)
ON_CHIP = pl.BlockSpec(memory_space=pltpu.VMEM)
OFF_CHIP = pl.BlockSpec(memory_space=pltpu.HBM)
HIGHEST = lax.Precision.HIGHEST
OWN = slice(0, 2048)
OWN_PAIRS = 2, 18
INNER = 6, 14
PAIR = 128
EDGE = 64
PACKED = 320


def off_chip(*arrays):
    return [pltpu.with_memory_space_constraint(array, pltpu.HBM) for array in arrays]


def dot(left, right, dims=((1,), (0,)), precision=None):
    return lax.dot_general(
        left, right, (dims, ((), ())), precision=precision, preferred_element_type=jnp.float32
    )


def split(value):
    high = value.astype(jnp.bfloat16)
    return high, (value - high.astype(jnp.float32)).astype(jnp.bfloat16)


def exchange(pieces, unit):
    count = len(pieces)
    lane = lax.broadcasted_iota(jnp.int32, pieces[0].shape, 1) // unit
    step = count // 2
    while step:
        low = (lane // step) % 2 == 0
        out = list(pieces)
        for i in range(count):
            if (i // step) % 2 == 0:
                a, c = pieces[i], pieces[i + step]
                out[i] = jnp.where(low, a, pltpu.roll(c, step * unit, 1))
                out[i + step] = jnp.where(low, pltpu.roll(a, LANES - step * unit, 1), c)
        pieces = out
        step //= 2
    return pieces


def pack_kernel(x_ref, o_ref, buf, scr, in_sem, out_sem):
    loads = [
        pltpu.make_async_copy(x_ref.at[:, pl.ds(8 * part, 8), :], buf.at[part], in_sem.at[part])
        for part in range(2)
    ]
    for load in loads:
        load.start()
    sends = [
        pltpu.make_async_copy(
            scr.at[pl.ds(512 * k, 512), :].reshape(4, LANES, LANES), o_ref.at[pl.ds(4 * k, 4)], out_sem.at[k]
        )
        for k in range(8)
    ]
    for part in range(2):
        loads[part].wait()
        rows = buf.at[part].reshape(2048, LANES)
        for tile in range(4):
            for r in range(4):
                row, high = r // 2, r % 2
                parts = [
                    rows[pl.ds((high * 4 + low) * 8 + tile * 2 + row, 32, stride=64), :]
                    for low in range(4)
                ]
                turned = jnp.concatenate(parts, axis=0).T
                scr[pl.ds((512 * part + 128 * tile) * 4 + r, 128, stride=4), :] = turned
            sends[4 * part + tile].start()
    for send in sends:
        send.wait()


def pack(x):
    rows = x.reshape(32, 8, 2, 8, LANES).transpose(0, 1, 3, 2, 4).reshape(256, 16, LANES)
    return pl.pallas_call(
        pack_kernel,
        out_shape=pltpu.HBM((32, LANES, LANES), jnp.float32),
        in_specs=[OFF_CHIP],
        out_specs=OFF_CHIP,
        scratch_shapes=[
            pltpu.VMEM((2, 256, 8, LANES), jnp.float32),
            pltpu.VMEM((4096, LANES), jnp.float32),
            pltpu.SemaphoreType.DMA((2,)),
            pltpu.SemaphoreType.DMA((8,)),
        ],
        compiler_params=VMEM,
        name="pack",
    )(*off_chip(rows))


def unpack_kernel(r_ref, o_ref, buf, sem):
    stores = []
    for high in range(2):
        rows = buf.at[high].reshape(2048, LANES)
        for tile in range(8):
            for row in range(2):
                turned = r_ref[pl.ds(tile * 512 + row * 2 + high, 128, stride=4), :].T
                for low in range(4):
                    rows[pl.ds((low * 8 + tile) * 2 + row, 32, stride=64), :] = turned[
                        32 * low : 32 * low + 32
                    ]
        stores.append(
            pltpu.make_async_copy(buf.at[high], o_ref.at[:, pl.ds(64 * high, 64), :], sem.at[high])
        )
        stores[high].start()
    for store in stores:
        store.wait()


def unpack(blocks):
    rows = pl.pallas_call(
        unpack_kernel,
        out_shape=pltpu.HBM((32, 128, LANES), jnp.float32),
        in_specs=[ON_CHIP],
        out_specs=OFF_CHIP,
        scratch_shapes=[pltpu.VMEM((2, 32, 64, LANES), jnp.float32), pltpu.SemaphoreType.DMA((2,))],
        compiler_params=VMEM,
        name="unpack",
    )(blocks.reshape(4096, LANES))
    return rows.reshape(32, 8, 8, 2, LANES).transpose(0, 1, 3, 2, 4).reshape(32, 8, 2, 1024)


def coef_kernel(reg_ref, onsite_ref, hop_ref, kx_ref, ky_ref, ch_ref, cl_ref):
    def decode(index):
        band = (index % 2) * 4 + ((index // 32) % 2) * 2 + (index // 4) % 2
        x = ((index // 8) % 4) * 2 + (index // 2) % 2
        column = (index // 64) % 2
        return band, x, column

    def one_hot(values, shape, axis):
        return (values == lax.broadcasted_iota(jnp.int32, shape, axis)).astype(jnp.float32)

    b_r, x_r, y_r = decode(lax.broadcasted_iota(jnp.int32, (128, 8), 0))
    band_rows = one_hot(b_r, (128, 8), 1)
    b_c, _, _ = decode(lax.broadcasted_iota(jnp.int32, (8, 256), 1) + 64)
    band_cols = one_hot(b_c, (8, 256), 0)
    reg = reg_ref[...]
    hop = dot(band_rows, hop_ref[...], ((1,), (1,)), HIGHEST)

    def table_of(offset):
        return dot(one_hot(x_r + offset, (128, 8), 1), reg, precision=HIGHEST)

    def hops(codes):
        total = jnp.zeros_like(codes)
        for m in range(MATERIALS):
            total = total + jnp.where(codes == m + 1.0, hop[:, m : m + 1], 0.0)
        return total

    second = lax.broadcasted_iota(jnp.int32, (128, LANES), 0) >= 64

    def aligned(table):
        return jnp.where(second, pltpu.roll(table, LANES - 1, 1), table)

    codes = table_of(0)
    here, up, down = hops(codes), hops(table_of(-1)), hops(table_of(1))
    before, after = pltpu.roll(here, 1, 1), pltpu.roll(here, LANES - 1, 1)
    valid = (codes > 0.5).astype(jnp.float32)
    centre = (0.5 * (4.0 * here + up + down + before + after) - SHIFT) * valid
    fields = [aligned((codes == m + 1.0).astype(jnp.float32)) for m in range(MATERIALS)]
    fields += [aligned(valid), aligned(centre)]
    fields += [aligned(-0.5 * (here + side) * valid) for side in (up, down, before, after)]

    b_r, x_r, y_r = decode(lax.broadcasted_iota(jnp.int32, (128, 256), 0))
    k = lax.broadcasted_iota(jnp.int32, (128, 256), 1)
    b_c, x_c, _ = decode(k + 64)
    dy = k // 64 - 1 - y_r
    dx = x_c - x_r
    same = b_r == b_c

    def spread(matrix):
        return dot(dot(band_rows, matrix, precision=HIGHEST), band_cols, precision=HIGHEST)

    here_at, up_at, down_at = (dy == 0) & (dx == 0), (dy == 0) & (dx == -1), (dy == 0) & (dx == 1)
    before_at, after_at = (dy == -1) & (dx == 0), (dy == 1) & (dx == 0)
    onsite = [
        jnp.where(here_at, spread(0.5 * (onsite_ref[m] + onsite_ref[m].T)), 0.0) for m in range(MATERIALS)
    ]
    kx = spread(0.5 * (0.5 * (kx_ref[...] - kx_ref[...].T)))
    ky = spread(0.5 * (0.5 * (ky_ref[...] - ky_ref[...].T)))
    mixed = (
        jnp.where(down_at, kx, 0.0)
        - jnp.where(up_at, kx, 0.0)
        + jnp.where(after_at, ky, 0.0)
        - jnp.where(before_at, ky, 0.0)
    )
    places = [here_at & same, up_at & same, down_at & same, before_at & same, after_at & same]
    for pair in range(WINDOW // 2):
        lane = 2 * pair + 1
        scalar = [field[:, lane : lane + 1] for field in fields]
        value = scalar[4] * mixed
        for m in range(MATERIALS):
            value = value + scalar[m] * onsite[m]
        for place, weight in zip(places, scalar[5:]):
            value = value + jnp.where(place, weight, 0.0)
        high, low = split((2.0 / SCALE) * value)
        ch_ref[pair] = high
        cl_ref[pair] = low


def coefficients(reg, onsite_table, hop_table, coupling_x, coupling_y):
    shape = pltpu.HBM((WINDOW // 2, 128, 256), jnp.bfloat16)
    return pl.pallas_call(
        coef_kernel,
        out_shape=(shape, shape),
        compiler_params=VMEM,
        name="coefficients",
    )(reg, onsite_table, hop_table, coupling_x, coupling_y)


def halves(even, odd):
    even, odd = (value.reshape(-1, 8, LANES) for value in (even, odd))
    first = lax.broadcasted_iota(jnp.int32, (1, 8, LANES), 1) < 4
    return (
        jnp.where(first, even, pltpu.roll(odd, 4, 1)),
        jnp.where(first, pltpu.roll(even, 4, 1), odd),
    )


def lower_blocks(square):
    first, last = square[:LANES, :LANES], square[LANES:, LANES:]
    left = lax.broadcasted_iota(jnp.int32, (64, LANES), 1) < 64
    corners = jnp.where(left, first[:64], pltpu.roll(last[:64], 64, 1))
    return jnp.concatenate([corners, first[64:], last[64:], square[LANES:, :LANES]], axis=0)


def whole_blocks(rows):
    row = lax.broadcasted_iota(jnp.int32, (LANES, LANES), 0)
    upper = (row < 64) & (lax.broadcasted_iota(jnp.int32, (LANES, LANES), 1) >= 64)

    def mirrored(top, bottom):
        block = jnp.concatenate([top, bottom], axis=0)
        return jnp.where(upper, block.T, block)

    first = mirrored(rows[:64], rows[64:128])
    return first, rows[192:], mirrored(pltpu.roll(rows[:64], 64, 1), rows[128:192])


def ingest(load, pair, field, high, low):
    at = pair * PAIR
    for half in range(2):
        lanes = slice(half * LANES, half * LANES + LANES)
        for slab in range(4):
            pieces = exchange([load((half * 4 + j) * 4 + slab) for j in range(4)], 32)
            for mid in range(2):
                for column, piece in enumerate(halves(pieces[2 * mid], pieces[2 * mid + 1])):
                    field[pl.ds(at + (column * 64 + mid * 32 + slab * 8), 8), lanes] = piece[0]
    rows = pl.ds(at + EDGE, PAIR)
    high[rows, :], low[rows, :] = split(field[pl.ds(at, PAIR), :])


def product(pair, ch_ref, cl_ref, high, low):
    rows = pl.ds(pair * PAIR, 2 * PAIR)
    vh, vl = high[rows, :], low[rows, :]
    c_high, c_low = ch_ref[pair], cl_ref[pair]
    return dot(
        jnp.concatenate([c_high, c_high, c_low], axis=1), jnp.concatenate([vh, vl, vh], axis=0)
    )


def steps(ch_ref, cl_ref, fa, fb, ah, al, bh, bl):
    def store(pair, value, field, high, low):
        field[pl.ds(pair * PAIR, PAIR), :] = value
        rows = pl.ds(pair * PAIR + EDGE, PAIR)
        high[rows, :], low[rows, :] = split(value)

    def first(pair):
        store(pair, 0.5 * product(pair, ch_ref, cl_ref, ah, al), fb, bh, bl)

    def later(old, high, low, source_high, source_low):
        def step(pair):
            rows = pl.ds(pair * PAIR, PAIR)
            value = product(pair, ch_ref, cl_ref, source_high, source_low) - old[rows, :]
            store(pair, value, old, high, low)

        return step

    even, odd = later(fa, ah, al, bh, bl), later(fb, bh, bl, ah, al)
    return first, even, odd, even


def gram_of(high, low):
    dims = ((0,), (0,))
    cross = dot(high, low, dims)
    return dot(high, high, dims) + (cross + cross.T)


def interior_kernel(r_ref, ch_hbm, cl_hbm, fa, fb, ah, al, bh, bl, ch_ref, cl_ref, g_ref, sem):
    loads = [
        pltpu.make_async_copy(ch_hbm, ch_ref, sem.at[0]),
        pltpu.make_async_copy(cl_hbm, cl_ref, sem.at[1]),
    ]
    for load in loads:
        load.start()

    def take(pair, carry):
        rows = pl.ds(pl.multiple_of((pair - OWN_PAIRS[0]) * 8, 8), 8)
        ingest(lambda source: r_ref[source, rows, :], pair, fa, ah, al)
        return carry

    lax.fori_loop(*OWN_PAIRS, take, 0, unroll=2)
    for load in loads:
        load.wait()
    for count, step in enumerate(steps(ch_ref, cl_ref, fa, fb, ah, al, bh, bl)):

        def body(pair, carry, step=step):
            step(pair)
            return carry

        low, high = OWN_PAIRS[0] + 1 + count, OWN_PAIRS[1] - 1 - count
        lax.fori_loop(low, high, body, 0, unroll=high - low)
    rows = slice(INNER[0] * PAIR + EDGE, INNER[1] * PAIR + EDGE)
    g_ref[...] = gram_of(ah[rows, :], al[rows, :])


def interior(received, coef_high, coef_low):
    pairs = WINDOW // 2
    field = pltpu.VMEM((pairs * PAIR, 256), jnp.float32)
    half = pltpu.VMEM((pairs * PAIR + 2 * EDGE, 256), jnp.bfloat16)
    bands = pltpu.VMEM((pairs, PAIR, 256), jnp.bfloat16)
    return pl.pallas_call(
        interior_kernel,
        out_shape=(field,) * 2 + (half,) * 4 + (bands,) * 2 + (pltpu.VMEM((256, 256), jnp.float32),),
        in_specs=[ON_CHIP, OFF_CHIP, OFF_CHIP],
        out_specs=(ON_CHIP,) * 9,
        scratch_shapes=[pltpu.SemaphoreType.DMA((2,))],
        compiler_params=VMEM,
        cost_estimate=pl.CostEstimate(flops=int(8e9), transcendentals=0, bytes_accessed=int(2e7)),
        name="interior",
    )(received, *off_chip(coef_high, coef_low))


def edges_kernel(left_ref, right_ref, *refs):
    (ch_ref, cl_ref, inner_ref), (vh_hbm, vl_hbm, g_ref) = refs[6:9], refs[9:12]
    fa, fb, ah, al, bh, bl = fields = refs[12:18]
    sem = refs[18]
    pairs = WINDOW // 2
    first_row = OWN_PAIRS[0] * PAIR + EDGE

    def results(low, high, index):
        rows = pl.ds(low + EDGE, high - low)
        target = pl.ds(low + EDGE - first_row, high - low)
        return [
            pltpu.make_async_copy(ah.at[rows, :], vh_hbm.at[target, :], sem.at[index]),
            pltpu.make_async_copy(al.at[rows, :], vl_hbm.at[target, :], sem.at[index + 1]),
        ]

    stores = results(INNER[0] * PAIR, INNER[1] * PAIR, 0)
    for store in stores:
        store.start()
    zero = jnp.zeros((EDGE, 256), jnp.bfloat16)
    for ref in (ah, al, bh, bl):
        ref[0:EDGE, :] = zero
        ref[pairs * PAIR + EDGE :, :] = zero
    for pair in range(OWN_PAIRS[0]):
        ingest(lambda source, pair=pair: left_ref[source, 8 * pair : 8 * pair + 8, :], pair, fa, ah, al)
    for pair in range(OWN_PAIRS[1], pairs):

        def load(source, start=8 * (pair - OWN_PAIRS[1])):
            count = min(8, 4 * RIGHT - start)
            rows = right_ref[4 * RIGHT * source + start : 4 * RIGHT * source + start + count, :]
            return rows if count == 8 else jnp.concatenate([rows, jnp.zeros_like(rows)], axis=0)

        ingest(load, pair, fa, ah, al)
    reach = ((0, pairs), (1, pairs - 1), (1, pairs - 1), (2, pairs - 2))
    for count, step in enumerate(steps(ch_ref, cl_ref, *fields)):
        low, high = OWN_PAIRS[0] + 1 + count, OWN_PAIRS[1] - 1 - count
        for pair in list(range(reach[count][0], low)) + list(range(high, reach[count][1])):
            step(pair)
    last = OWN_PAIRS[1] * PAIR + EDGE
    stores += results(OWN_PAIRS[0] * PAIR, INNER[0] * PAIR, 2) + results(INNER[1] * PAIR, last, 4)
    for store in stores[2:]:
        store.start()
    before = slice(first_row, INNER[0] * PAIR + EDGE)
    after = slice(INNER[1] * PAIR + EDGE, OWN_PAIRS[1] * PAIR + EDGE)
    high, low = (jnp.concatenate([ref[before, :], ref[after, :]], axis=0) for ref in (ah, al))
    g_ref[...] = lower_blocks(inner_ref[...] + gram_of(high, low))
    for store in stores:
        store.wait()


def filtered_blocks(received, coef_high, coef_low):
    count = lax.axis_size(ALL)
    chain = [(i, i + 1) for i in range(count - 1)]
    leading = received.reshape(count, 32, 4, LANES)[:, :RIGHT]
    right = lax.ppermute(leading, ALL, [(j, i) for i, j in chain]).reshape(-1, LANES)
    left = lax.ppermute(received[:, 128 - 4 * LEFT :], ALL, chain)
    state = interior(received, coef_high, coef_low)
    half = pltpu.HBM((2048 + EDGE, 256), jnp.bfloat16)
    fields = [pltpu.VMEM(value.shape, value.dtype) for value in state[:6]]
    return pl.pallas_call(
        edges_kernel,
        out_shape=(half, half, pltpu.VMEM((PACKED, LANES), jnp.float32), *fields),
        in_specs=[ON_CHIP] * 11,
        out_specs=(OFF_CHIP,) * 2 + (ON_CHIP,) * 7,
        input_output_aliases={i + 2: i + 3 for i in range(6)},
        scratch_shapes=[pltpu.SemaphoreType.DMA((6,))],
        compiler_params=VMEM,
        name="edges",
    )(left, right, *state)[:3]


def moment_kernel(vh_ref, vl_ref, ch_ref, cl_ref, g_ref, m_ref, bh, bl):
    block, edge = 128, 64

    def image(pair, rows, drop=0):
        vh, vl = vh_ref[rows, :], vl_ref[rows, :]
        c_high, c_low = ch_ref[pair, :, drop:], cl_ref[pair, :, drop:]
        value = dot(
            jnp.concatenate([c_high, c_high, c_low], axis=1), jnp.concatenate([vh, vl, vh], axis=0)
        )
        at = pl.ds((pair - 2) * block, block)
        bh[at, :], bl[at, :] = split(value)

    def body(pair, carry):
        image(pair, pl.ds(pl.multiple_of((pair - 3) * block + edge, edge), 256))
        return carry

    image(2, slice(0, block + edge), edge)
    lax.fori_loop(3, 18, body, 0, unroll=3)
    rows = slice(16 * block - edge, 16 * block)
    c_high, c_low = ch_ref[18, 0:edge, 0:edge], cl_ref[18, 0:edge, 0:edge]
    value = dot(c_high, vh_ref[rows, :]) + (dot(c_high, vl_ref[rows, :]) + dot(c_low, vh_ref[rows, :]))
    bh[16 * block :, :], bl[16 * block :, :] = split(value)
    dims = ((0,), (0,))
    high = vh_ref[...]
    moment = dot(high, bh[...], dims) + (dot(high, bl[...], dims) + dot(vl_ref[...], bh[...], dims))
    m_ref[...] = (0.5 * SCALE) * lower_blocks(moment) + SHIFT * g_ref[...]


def moment_of(vh, vl, coef_high, coef_low, gram):
    return pl.pallas_call(
        moment_kernel,
        out_shape=jax.ShapeDtypeStruct((PACKED, LANES), jnp.float32),
        scratch_shapes=[pltpu.VMEM((16 * 128 + 64, 256), jnp.bfloat16)] * 2,
        compiler_params=VMEM,
        cost_estimate=pl.CostEstimate(flops=int(4e9), transcendentals=0, bytes_accessed=int(1e7)),
        name="moment",
    )(*off_chip(vh, vl, coef_high, coef_low), gram)


def panel_solve(block, lines):
    row = lax.broadcasted_iota(jnp.int32, (8, LANES), 0)

    def spread(tile, k):
        return jnp.broadcast_to(tile[k % 8 : k % 8 + 1], tile.shape)

    cols = [
        [jnp.broadcast_to(block[8 * t : 8 * t + 8, j : j + 1], (8, LANES)) for t in range(4)]
        for j in range(32)
    ]
    lines = [
        [lines[8 * t : 8 * t + 8, LANES * h : LANES * h + LANES] for h in range(2)] for t in range(4)
    ]
    pivots = [jnp.ones((8, LANES), jnp.float32) for t in range(4)]
    for k in range(32):
        own = k // 8
        pivot = spread(cols[k][own], k)
        pivots[own] = jnp.where(row == k % 8, pivot, pivots[own])
        scale = 1.0 / pivot
        ratio = {t: cols[k][t] * scale for t in range(own, 4)}
        line = [spread(part, k) for part in lines[own]]
        for j in range(k + 1, 32):
            weight = spread(cols[k][j // 8], j)
            for t in range(j // 8, 4):
                cols[j][t] = cols[j][t] - ratio[t] * weight
        ratio[own] = jnp.where(row > k % 8, ratio[own], 0.0)
        for t in range(own, 4):
            lines[t] = [part - ratio[t] * above for part, above in zip(lines[t], line)]
    roots = [lax.rsqrt(pivots[t]) for t in range(4)]
    return jnp.concatenate(
        [jnp.concatenate([part * roots[t] for part in lines[t]], axis=1) for t in range(4)], axis=0
    )


def half_inverse(aug):
    def panel(p, carry):
        rows = pl.ds(pl.multiple_of(32 * p, 32), 32)
        lines = aug[rows, :]
        lines = panel_solve(pltpu.roll(lines[:, :LANES], LANES - 32 * p, 1), lines)
        aug[rows, :] = lines

        @pl.when(p < 3)
        def update():
            lane = lax.broadcasted_iota(jnp.int32, (32, LANES), 1)
            upper = jnp.where(lane >= 32 * (p + 1), lines[:, :LANES], 0.0)
            aug[...] = aug[...] - dot(upper, lines, ((0,), (0,)), HIGHEST)

        return carry

    lax.fori_loop(0, 4, panel, 0)


def basis_kernel(entries, both_ref, vh_hbm, vl_hbm, w_ref, o_hbm, gram, aug, vh, vl, scr, out, sem, out_sem):
    loads = [
        pltpu.make_async_copy(vh_hbm.at[OWN, :], vh, sem.at[0]),
        pltpu.make_async_copy(vl_hbm.at[OWN, :], vl, sem.at[1]),
    ]
    for load in loads:
        load.start()
    row = lax.broadcasted_iota(jnp.int32, (LANES, LANES), 0)
    eye = (row == lax.broadcasted_iota(jnp.int32, (LANES, LANES), 1)).astype(jnp.float32)
    for d in range(32):
        gram[10 * d : 10 * d + 10, :] = both_ref[20 * d : 20 * d + 10, :] * (1.0 / entries)
    above, below, after = whole_blocks(gram[...])
    aug[:, :LANES] = above
    aug[:, LANES:] = eye
    half_inverse(aug)
    first = aug[:, LANES:]
    upper = dot(first, below, ((1,), (1,)), HIGHEST)
    aug[:, :LANES] = after - dot(upper, upper, ((0,), (0,)), HIGHEST)
    aug[:, LANES:] = eye
    corner = dot(upper, first, ((0,), (0,)), HIGHEST)
    half_inverse(aug)
    second = aug[:, LANES:]
    w_ref[:LANES, :LANES] = first
    w_ref[:LANES, LANES:] = jnp.zeros((LANES, LANES), jnp.float32)
    w_ref[LANES:, :LANES] = -dot(second, corner, precision=HIGHEST)
    w_ref[LANES:, LANES:] = second
    for load in loads:
        load.wait()
    sends = [pltpu.make_async_copy(out.at[d], o_hbm.at[d], out_sem.at[d]) for d in range(32)]
    for half in range(2):
        used = LANES * (half + 1)
        wh, wl = split(w_ref[LANES * half : used, :used])
        values = [vh[:, :used], vl[:, :used], vh[:, :used]]
        scr[...] = dot(
            jnp.concatenate(values, axis=1), jnp.concatenate([wh, wh, wl], axis=1), ((1,), (1,))
        )
        for slab in range(4):
            pieces = []
            for mid in range(2):
                columns = []
                for column in range(2):
                    at = column * 64 + mid * 32 + slab * 8
                    columns.append(
                        jnp.concatenate(
                            [scr[pair * 128 + at : pair * 128 + at + 8, :] for pair in range(16)], axis=0
                        )
                    )
                pieces += [value.reshape(128, LANES) for value in halves(*columns)]
            for j, piece in enumerate(exchange(pieces, 32)):
                d = (half * 4 + j) * 4 + slab
                out[d] = piece
                sends[d].start()
    for send in sends:
        send.wait()


def basis(both, entries, vh, vl):
    return pl.pallas_call(
        functools.partial(basis_kernel, entries),
        out_shape=(
            jax.ShapeDtypeStruct((256, 256), jnp.float32),
            pltpu.HBM((32, 128, LANES), jnp.float32),
        ),
        in_specs=[ON_CHIP, OFF_CHIP, OFF_CHIP],
        out_specs=(ON_CHIP, OFF_CHIP),
        scratch_shapes=[
            pltpu.VMEM((PACKED, LANES), jnp.float32),
            pltpu.VMEM((LANES, 256), jnp.float32),
            pltpu.VMEM((2048, 256), jnp.bfloat16),
            pltpu.VMEM((2048, 256), jnp.bfloat16),
            pltpu.VMEM((2048, LANES), jnp.float32),
            pltpu.VMEM((32, LANES, LANES), jnp.float32),
            pltpu.SemaphoreType.DMA((2,)),
            pltpu.SemaphoreType.DMA((32,)),
        ],
        compiler_params=VMEM,
        cost_estimate=pl.CostEstimate(flops=int(4e9), transcendentals=0, bytes_accessed=int(2e7)),
        name="basis",
    )(both.reshape(2 * PACKED, LANES), *off_chip(vh, vl))


def parts_of(blocks):
    return blocks.reshape(lax.axis_size(ALL), -1, 2, LANES)


def swap(parts):
    rows = parts.reshape((-1,) + parts.shape[-2:])
    return lax.all_to_all(rows, ALL, 0, 0, tiled=True).reshape(parts.shape)


def for_all(share):
    return jnp.broadcast_to(share[None], (lax.axis_size(ALL),) + share.shape)


def project_kernel(entries, moment_ref, w_ref, p_ref):
    first = pl.multiple_of(32 * lax.axis_index("blk"), 32)
    mine = w_ref[pl.ds(first, 32), :]
    left, right = mine[:, :LANES], mine[:, LANES:]
    above, below, last = whole_blocks(moment_ref[...])
    half_done = jnp.concatenate(
        [
            dot(left, above, precision=HIGHEST) + dot(right, below, precision=HIGHEST),
            dot(left, below, ((1,), (1,)), HIGHEST) + dot(right, last, precision=HIGHEST),
        ],
        axis=1,
    ) * (1.0 / entries)
    p_ref[...] = dot(half_done, w_ref[...], ((1,), (1,)), HIGHEST)


def project(moment, inverse, entries):
    return pl.pallas_call(
        functools.partial(project_kernel, entries),
        out_shape=jax.ShapeDtypeStruct((32, 256), jnp.float32),
        in_specs=[ON_CHIP] * 2,
        out_specs=ON_CHIP,
        compiler_params=VMEM,
        name="project",
    )(moment, inverse)


def fast(states_in, region, onsite_table, hop_table, coupling_x, coupling_y):
    device = lax.axis_index("blk") * lax.axis_size("slab") + lax.axis_index("slab")
    entries = float(BANDS * 8 * 1024)
    codes = lax.all_gather((region + 1).astype(jnp.float32), "slab", axis=0, tiled=True)
    received = swap(pack(states_in))
    codes = jnp.pad(codes, ((0, 0), (LEFT + 1, LANES)))
    codes = lax.dynamic_slice(codes, (0, 32 * device), (8, LANES))
    coef_high, coef_low = coefficients(codes, onsite_table, hop_table, coupling_x, coupling_y)
    vh, vl, own_gram = filtered_blocks(received, coef_high, coef_low)
    own_moment = moment_of(vh, vl, coef_high, coef_low, own_gram)
    share = swap(parts_of(own_gram)).sum(0)
    both = swap(jnp.concatenate([for_all(share), parts_of(own_moment)], axis=1))
    inverse, blocks = basis(both, entries, vh, vl)
    moment = swap(for_all(both[:, 5:].sum(0))).reshape(PACKED, LANES)
    blocks, moment = lax.optimization_barrier((blocks, moment))
    states_out = unpack(swap(blocks))
    projected = project(moment, inverse, entries)
    return states_out, projected


DEGREE = 4


def extended(array, sides, width):
    for axis, dim in sides:
        size, length = (lax.axis_size(axis), array.shape[dim])
        up = [(i, (i + 1) % size) for i in range(size - 1)]
        down = [(j, i) for i, j in up]
        last = lax.slice_in_dim(array, length - width, length, axis=dim)
        leading = lax.slice_in_dim(array, 0, width, axis=dim)
        before = lax.ppermute(last, axis, up)
        after = lax.ppermute(leading, axis, down)
        array = jnp.concatenate([before, array, after], axis=dim)
    return array


def mixing(onsite_table, coupling_x, coupling_y):
    onsite = 0.5 * (onsite_table + jnp.swapaxes(onsite_table, 1, 2))
    blocks = [onsite[material] for material in range(onsite.shape[0])]
    return jnp.concatenate(
        blocks + [0.5 * (coupling_x - coupling_x.T), 0.5 * (coupling_y - coupling_y.T)], axis=1
    )


def masks_of(region):
    codes = jnp.arange(MATERIALS, dtype=jnp.int32)
    return (region[None] == codes[:, None, None]).astype(jnp.float32)


def apply_padded(padded, hop_padded, material_masks, mixing_matrix):
    centre = padded[:, :, 1:-1, 1:-1]
    hop_centre = hop_padded[:, 1:-1, 1:-1]
    kinetic = jnp.zeros_like(centre)
    sides = (
        (padded[:, :, 2:, 1:-1], hop_padded[:, 2:, 1:-1]),
        (padded[:, :, :-2, 1:-1], hop_padded[:, :-2, 1:-1]),
        (padded[:, :, 1:-1, 2:], hop_padded[:, 1:-1, 2:]),
        (padded[:, :, 1:-1, :-2], hop_padded[:, 1:-1, :-2]),
    )
    for field_side, hop_side in sides:
        kinetic = kinetic + (0.5 * (hop_centre + hop_side))[None] * (centre - field_side)
    deriv_rows = 0.5 * (padded[:, :, 2:, 1:-1] - padded[:, :, :-2, 1:-1])
    deriv_cols = 0.5 * (padded[:, :, 1:-1, 2:] - padded[:, :, 1:-1, :-2])
    pieces = [
        material_masks[material][None, None] * centre for material in range(material_masks.shape[0])
    ]
    stacked = jnp.concatenate(pieces + [deriv_rows, deriv_cols], axis=1)
    mixed = jnp.einsum("bc,scxy->sbxy", mixing_matrix, stacked, precision=lax.Precision.HIGHEST)
    return mixed + kinetic


def chebyshev(field, apply_fn):

    def scaled(value):
        return (apply_fn(value) - SHIFT * value) / SCALE

    previous = field
    current = scaled(field)
    for repeat in range(DEGREE - 1):
        previous, current = (current, 2.0 * scaled(current) - previous)
    return current


def inner(left, right):
    return jnp.dot(
        left, right.T, precision=lax.Precision.HIGHEST, preferred_element_type=jnp.float32
    )


def general(states_in, region, onsite_table, hop_table, coupling_x, coupling_y):
    mixing_matrix = mixing(onsite_table, coupling_x, coupling_y)
    material_masks = masks_of(region)
    hop_field = jnp.einsum(
        "mb,mxy->bxy", hop_table, material_masks, precision=lax.Precision.HIGHEST
    )
    hop_rows = extended(hop_field, (("slab", 1),), 1)
    hop_padded = jnp.pad(hop_rows, ((0, 0), (0, 0), (1, 1)))

    def apply_rows(field):
        padded = extended(field, (("slab", 2),), 1)
        padded = jnp.pad(padded, ((0, 0), (0, 0), (0, 0), (1, 1)))
        return apply_padded(padded, hop_padded, material_masks, mixing_matrix)

    filtered = chebyshev(states_in, apply_rows)
    block_count = lax.axis_size("blk")
    slab_count = lax.axis_size("slab")
    states_all = filtered.shape[0] * block_count
    row_count = filtered.shape[2]
    width_all = filtered.shape[3]
    entries = float(BANDS * row_count * slab_count * width_all)
    image = apply_rows(filtered)
    cell_states, cell_image = (
        lax.all_to_all(filtered, "blk", split_axis=3, concat_axis=0, tiled=True),
        lax.all_to_all(image, "blk", split_axis=3, concat_axis=0, tiled=True),
    )
    states_flat = cell_states.reshape(states_all, -1)
    image_flat = cell_image.reshape(states_all, -1)
    moment = lax.psum(inner(states_flat, image_flat) / entries, ("blk", "slab"))

    def panel_step(panel, carry):
        basis_rows, factor_rows = carry
        offset = panel * PANEL
        panel_states = lax.dynamic_slice_in_dim(states_flat, offset, PANEL, 0)
        coeffs = lax.psum(inner(basis_rows, panel_states) / entries, ("blk", "slab"))
        residue = panel_states - jnp.dot(
            coeffs.T,
            basis_rows,
            precision=lax.Precision.HIGHEST,
            preferred_element_type=jnp.float32,
        )
        panel_gram = lax.psum(inner(residue, residue) / entries, ("blk", "slab"))
        panel_factor = jnp.linalg.cholesky(panel_gram)
        panel_basis = lax.linalg.triangular_solve(panel_factor, residue, left_side=True, lower=True)
        basis_rows = lax.dynamic_update_slice_in_dim(basis_rows, panel_basis, offset, 0)
        factor_row = lax.dynamic_update_slice_in_dim(coeffs.T, panel_factor, offset, 1)
        factor_rows = lax.dynamic_update_slice_in_dim(factor_rows, factor_row, offset, 0)
        return (basis_rows, factor_rows)

    start_state = (jnp.zeros_like(states_flat), jnp.zeros((states_all, states_all), jnp.float32))
    basis_flat, factor = lax.fori_loop(0, states_all // PANEL, panel_step, start_state)
    half_done = lax.linalg.triangular_solve(factor, moment, left_side=True, lower=True)
    projected = lax.linalg.triangular_solve(factor, half_done.T, left_side=True, lower=True).T
    basis_cells = basis_flat.reshape(cell_states.shape)
    states_out = lax.all_to_all(basis_cells, "blk", split_axis=0, concat_axis=3, tiled=True)
    owned = states_all // block_count
    projected_rows = lax.dynamic_slice_in_dim(projected, lax.axis_index("blk") * owned, owned, 0)
    return (states_out, projected_rows)


def per_device(states_in, region, *tables):
    known = (lax.axis_size("blk"), lax.axis_size("slab")) == (8, 4)
    run = fast if known and states_in.shape == (32, 8, 2, 1024) else general
    return run(states_in, region, *tables)


def solution(mesh):
    return jax.shard_map(
        per_device,
        mesh=mesh,
        in_specs=(P("blk", None, "slab", None), P("slab", None), P(), P(), P(), P()),
        out_specs=(P("blk", None, "slab", None), P("blk", None)),
        check_vma=False,
    )
```

```python
import functools

import jax
import jax.numpy as jnp
from jax import lax
from jax.experimental import pallas as pl
from jax.experimental.pallas import tpu as pltpu
from jax.sharding import PartitionSpec as P

BANDS = 8
MATERIALS = 4
PANEL = 32
SHIFT = 1.0
SCALE = 3.0
LANES = 128
ALL = ("blk", "slab")
LEFT = 4
RIGHT = 5
WINDOW = 42
VMEM = pltpu.CompilerParams(vmem_limit_bytes=24 * 1024 * 1024)
ON_CHIP = pl.BlockSpec(memory_space=pltpu.VMEM)
OFF_CHIP = pl.BlockSpec(memory_space=pltpu.HBM)
HIGHEST = lax.Precision.HIGHEST
OWN = slice(0, 2048)
OWN_PAIRS = 2, 18
INNER = 6, 14
PAIR = 128
EDGE = 64
PACKED = 320


def off_chip(*arrays):
    return [pltpu.with_memory_space_constraint(array, pltpu.HBM) for array in arrays]


def dot(left, right, dims=((1,), (0,)), precision=None):
    return lax.dot_general(
        left, right, (dims, ((), ())), precision=precision, preferred_element_type=jnp.float32
    )


def split(value):
    high = value.astype(jnp.bfloat16)
    return high, (value - high.astype(jnp.float32)).astype(jnp.bfloat16)


def exchange(pieces, unit):
    count = len(pieces)
    lane = lax.broadcasted_iota(jnp.int32, pieces[0].shape, 1) // unit
    step = count // 2
    while step:
        low = (lane // step) % 2 == 0
        out = list(pieces)
        for i in range(count):
            if (i // step) % 2 == 0:
                a, c = pieces[i], pieces[i + step]
                out[i] = jnp.where(low, a, pltpu.roll(c, step * unit, 1))
                out[i + step] = jnp.where(low, pltpu.roll(a, LANES - step * unit, 1), c)
        pieces = out
        step //= 2
    return pieces


def pack_kernel(x_ref, o_ref, buf, scr, in_sem, out_sem):
    loads = [
        pltpu.make_async_copy(x_ref.at[:, pl.ds(8 * part, 8), :], buf.at[part], in_sem.at[part])
        for part in range(2)
    ]
    for load in loads:
        load.start()
    sends = [
        pltpu.make_async_copy(
            scr.at[pl.ds(512 * k, 512), :].reshape(4, LANES, LANES), o_ref.at[pl.ds(4 * k, 4)], out_sem.at[k]
        )
        for k in range(8)
    ]
    for part in range(2):
        loads[part].wait()
        rows = buf.at[part].reshape(2048, LANES)
        for tile in range(4):
            for r in range(4):
                row, high = r // 2, r % 2
                parts = [
                    rows[pl.ds((high * 4 + low) * 8 + tile * 2 + row, 32, stride=64), :]
                    for low in range(4)
                ]
                turned = jnp.concatenate(parts, axis=0).T
                scr[pl.ds((512 * part + 128 * tile) * 4 + r, 128, stride=4), :] = turned
            sends[4 * part + tile].start()
    for send in sends:
        send.wait()


def pack(x):
    rows = x.reshape(32, 8, 2, 8, LANES).transpose(0, 1, 3, 2, 4).reshape(256, 16, LANES)
    return pl.pallas_call(
        pack_kernel,
        out_shape=pltpu.HBM((32, LANES, LANES), jnp.float32),
        in_specs=[OFF_CHIP],
        out_specs=OFF_CHIP,
        scratch_shapes=[
            pltpu.VMEM((2, 256, 8, LANES), jnp.float32),
            pltpu.VMEM((4096, LANES), jnp.float32),
            pltpu.SemaphoreType.DMA((2,)),
            pltpu.SemaphoreType.DMA((8,)),
        ],
        compiler_params=VMEM,
        name="pack",
    )(*off_chip(rows))


def unpack_kernel(r_ref, o_ref, buf, sem):
    stores = []
    for high in range(2):
        rows = buf.at[high].reshape(2048, LANES)
        for tile in range(8):
            for row in range(2):
                turned = r_ref[pl.ds(tile * 512 + row * 2 + high, 128, stride=4), :].T
                for low in range(4):
                    rows[pl.ds((low * 8 + tile) * 2 + row, 32, stride=64), :] = turned[
                        32 * low : 32 * low + 32
                    ]
        stores.append(
            pltpu.make_async_copy(buf.at[high], o_ref.at[:, pl.ds(64 * high, 64), :], sem.at[high])
        )
        stores[high].start()
    for store in stores:
        store.wait()


def unpack(blocks):
    rows = pl.pallas_call(
        unpack_kernel,
        out_shape=pltpu.HBM((32, 128, LANES), jnp.float32),
        in_specs=[ON_CHIP],
        out_specs=OFF_CHIP,
        scratch_shapes=[pltpu.VMEM((2, 32, 64, LANES), jnp.float32), pltpu.SemaphoreType.DMA((2,))],
        compiler_params=VMEM,
        name="unpack",
    )(blocks.reshape(4096, LANES))
    return rows.reshape(32, 8, 8, 2, LANES).transpose(0, 1, 3, 2, 4).reshape(32, 8, 2, 1024)


def coef_kernel(reg_ref, onsite_ref, hop_ref, kx_ref, ky_ref, ch_ref, cl_ref):
    def decode(index):
        band = (index % 2) * 4 + ((index // 32) % 2) * 2 + (index // 4) % 2
        x = ((index // 8) % 4) * 2 + (index // 2) % 2
        column = (index // 64) % 2
        return band, x, column

    def one_hot(values, shape, axis):
        return (values == lax.broadcasted_iota(jnp.int32, shape, axis)).astype(jnp.float32)

    b_r, x_r, y_r = decode(lax.broadcasted_iota(jnp.int32, (128, 8), 0))
    band_rows = one_hot(b_r, (128, 8), 1)
    b_c, _, _ = decode(lax.broadcasted_iota(jnp.int32, (8, 256), 1) + 64)
    band_cols = one_hot(b_c, (8, 256), 0)
    reg = reg_ref[...]
    hop = dot(band_rows, hop_ref[...], ((1,), (1,)), HIGHEST)

    def table_of(offset):
        return dot(one_hot(x_r + offset, (128, 8), 1), reg, precision=HIGHEST)

    def hops(codes):
        total = jnp.zeros_like(codes)
        for m in range(MATERIALS):
            total = total + jnp.where(codes == m + 1.0, hop[:, m : m + 1], 0.0)
        return total

    second = lax.broadcasted_iota(jnp.int32, (128, LANES), 0) >= 64

    def aligned(table):
        return jnp.where(second, pltpu.roll(table, LANES - 1, 1), table)

    codes = table_of(0)
    here, up, down = hops(codes), hops(table_of(-1)), hops(table_of(1))
    before, after = pltpu.roll(here, 1, 1), pltpu.roll(here, LANES - 1, 1)
    valid = (codes > 0.5).astype(jnp.float32)
    centre = (0.5 * (4.0 * here + up + down + before + after) - SHIFT) * valid
    fields = [aligned((codes == m + 1.0).astype(jnp.float32)) for m in range(MATERIALS)]
    fields += [aligned(valid), aligned(centre)]
    fields += [aligned(-0.5 * (here + side) * valid) for side in (up, down, before, after)]

    b_r, x_r, y_r = decode(lax.broadcasted_iota(jnp.int32, (128, 256), 0))
    k = lax.broadcasted_iota(jnp.int32, (128, 256), 1)
    b_c, x_c, _ = decode(k + 64)
    dy = k // 64 - 1 - y_r
    dx = x_c - x_r
    same = b_r == b_c

    def spread(matrix):
        return dot(dot(band_rows, matrix, precision=HIGHEST), band_cols, precision=HIGHEST)

    here_at, up_at, down_at = (dy == 0) & (dx == 0), (dy == 0) & (dx == -1), (dy == 0) & (dx == 1)
    before_at, after_at = (dy == -1) & (dx == 0), (dy == 1) & (dx == 0)
    onsite = [
        jnp.where(here_at, spread(0.5 * (onsite_ref[m] + onsite_ref[m].T)), 0.0) for m in range(MATERIALS)
    ]
    kx = spread(0.5 * (0.5 * (kx_ref[...] - kx_ref[...].T)))
    ky = spread(0.5 * (0.5 * (ky_ref[...] - ky_ref[...].T)))
    mixed = (
        jnp.where(down_at, kx, 0.0)
        - jnp.where(up_at, kx, 0.0)
        + jnp.where(after_at, ky, 0.0)
        - jnp.where(before_at, ky, 0.0)
    )
    places = [here_at & same, up_at & same, down_at & same, before_at & same, after_at & same]
    for pair in range(WINDOW // 2):
        lane = 2 * pair + 1
        scalar = [field[:, lane : lane + 1] for field in fields]
        value = scalar[4] * mixed
        for m in range(MATERIALS):
            value = value + scalar[m] * onsite[m]
        for place, weight in zip(places, scalar[5:]):
            value = value + jnp.where(place, weight, 0.0)
        high, low = split((2.0 / SCALE) * value)
        ch_ref[pair] = high
        cl_ref[pair] = low


def coefficients(reg, onsite_table, hop_table, coupling_x, coupling_y):
    shape = pltpu.HBM((WINDOW // 2, 128, 256), jnp.bfloat16)
    return pl.pallas_call(
        coef_kernel,
        out_shape=(shape, shape),
        compiler_params=VMEM,
        name="coefficients",
    )(reg, onsite_table, hop_table, coupling_x, coupling_y)


def halves(even, odd):
    even, odd = (value.reshape(-1, 8, LANES) for value in (even, odd))
    first = lax.broadcasted_iota(jnp.int32, (1, 8, LANES), 1) < 4
    return (
        jnp.where(first, even, pltpu.roll(odd, 4, 1)),
        jnp.where(first, pltpu.roll(even, 4, 1), odd),
    )


def lower_blocks(square):
    first, last = square[:LANES, :LANES], square[LANES:, LANES:]
    left = lax.broadcasted_iota(jnp.int32, (64, LANES), 1) < 64
    corners = jnp.where(left, first[:64], pltpu.roll(last[:64], 64, 1))
    return jnp.concatenate([corners, first[64:], last[64:], square[LANES:, :LANES]], axis=0)


def whole_blocks(rows):
    row = lax.broadcasted_iota(jnp.int32, (LANES, LANES), 0)
    upper = (row < 64) & (lax.broadcasted_iota(jnp.int32, (LANES, LANES), 1) >= 64)

    def mirrored(top, bottom):
        block = jnp.concatenate([top, bottom], axis=0)
        return jnp.where(upper, block.T, block)

    first = mirrored(rows[:64], rows[64:128])
    return first, rows[192:], mirrored(pltpu.roll(rows[:64], 64, 1), rows[128:192])


def ingest(load, pair, field, high, low):
    at = pair * PAIR
    for half in range(2):
        lanes = slice(half * LANES, half * LANES + LANES)
        for slab in range(4):
            pieces = exchange([load((half * 4 + j) * 4 + slab) for j in range(4)], 32)
            for mid in range(2):
                for column, piece in enumerate(halves(pieces[2 * mid], pieces[2 * mid + 1])):
                    field[pl.ds(at + (column * 64 + mid * 32 + slab * 8), 8), lanes] = piece[0]
    rows = pl.ds(at + EDGE, PAIR)
    high[rows, :], low[rows, :] = split(field[pl.ds(at, PAIR), :])


def product(pair, ch_ref, cl_ref, high, low):
    rows = pl.ds(pair * PAIR, 2 * PAIR)
    vh, vl = high[rows, :], low[rows, :]
    c_high, c_low = ch_ref[pair], cl_ref[pair]
    return dot(
        jnp.concatenate([c_high, c_high, c_low], axis=1), jnp.concatenate([vh, vl, vh], axis=0)
    )


def steps(ch_ref, cl_ref, fa, fb, ah, al, bh, bl):
    def store(pair, value, field, high, low):
        field[pl.ds(pair * PAIR, PAIR), :] = value
        rows = pl.ds(pair * PAIR + EDGE, PAIR)
        high[rows, :], low[rows, :] = split(value)

    def first(pair):
        store(pair, 0.5 * product(pair, ch_ref, cl_ref, ah, al), fb, bh, bl)

    def later(old, high, low, source_high, source_low):
        def step(pair):
            rows = pl.ds(pair * PAIR, PAIR)
            value = product(pair, ch_ref, cl_ref, source_high, source_low) - old[rows, :]
            store(pair, value, old, high, low)

        return step

    even, odd = later(fa, ah, al, bh, bl), later(fb, bh, bl, ah, al)
    return first, even, odd, even


def gram_of(high, low):
    dims = ((0,), (0,))
    cross = dot(high, low, dims)
    return dot(high, high, dims) + (cross + cross.T)


def interior_kernel(r_ref, ch_hbm, cl_hbm, fa, fb, ah, al, bh, bl, ch_ref, cl_ref, g_ref, sem):
    loads = [
        pltpu.make_async_copy(ch_hbm, ch_ref, sem.at[0]),
        pltpu.make_async_copy(cl_hbm, cl_ref, sem.at[1]),
    ]
    for load in loads:
        load.start()

    def take(pair, carry):
        rows = pl.ds(pl.multiple_of((pair - OWN_PAIRS[0]) * 8, 8), 8)
        ingest(lambda source: r_ref[source, rows, :], pair, fa, ah, al)
        return carry

    lax.fori_loop(*OWN_PAIRS, take, 0, unroll=2)
    for load in loads:
        load.wait()
    for count, step in enumerate(steps(ch_ref, cl_ref, fa, fb, ah, al, bh, bl)):

        def body(pair, carry, step=step):
            step(pair)
            return carry

        low, high = OWN_PAIRS[0] + 1 + count, OWN_PAIRS[1] - 1 - count
        lax.fori_loop(low, high, body, 0, unroll=high - low)
    rows = slice(INNER[0] * PAIR + EDGE, INNER[1] * PAIR + EDGE)
    g_ref[...] = gram_of(ah[rows, :], al[rows, :])


def interior(received, coef_high, coef_low):
    pairs = WINDOW // 2
    field = pltpu.VMEM((pairs * PAIR, 256), jnp.float32)
    half = pltpu.VMEM((pairs * PAIR + 2 * EDGE, 256), jnp.bfloat16)
    bands = pltpu.VMEM((pairs, PAIR, 256), jnp.bfloat16)
    return pl.pallas_call(
        interior_kernel,
        out_shape=(field,) * 2 + (half,) * 4 + (bands,) * 2 + (pltpu.VMEM((256, 256), jnp.float32),),
        in_specs=[ON_CHIP, OFF_CHIP, OFF_CHIP],
        out_specs=(ON_CHIP,) * 9,
        scratch_shapes=[pltpu.SemaphoreType.DMA((2,))],
        compiler_params=VMEM,
        cost_estimate=pl.CostEstimate(flops=int(8e9), transcendentals=0, bytes_accessed=int(2e7)),
        name="interior",
    )(received, *off_chip(coef_high, coef_low))


def edges_kernel(left_ref, right_ref, *refs):
    (ch_ref, cl_ref, inner_ref), (vh_hbm, vl_hbm, g_ref) = refs[6:9], refs[9:12]
    fa, fb, ah, al, bh, bl = fields = refs[12:18]
    sem = refs[18]
    pairs = WINDOW // 2
    first_row = OWN_PAIRS[0] * PAIR + EDGE

    def results(low, high, index):
        rows = pl.ds(low + EDGE, high - low)
        target = pl.ds(low + EDGE - first_row, high - low)
        return [
            pltpu.make_async_copy(ah.at[rows, :], vh_hbm.at[target, :], sem.at[index]),
            pltpu.make_async_copy(al.at[rows, :], vl_hbm.at[target, :], sem.at[index + 1]),
        ]

    stores = results(INNER[0] * PAIR, INNER[1] * PAIR, 0)
    for store in stores:
        store.start()
    zero = jnp.zeros((EDGE, 256), jnp.bfloat16)
    for ref in (ah, al, bh, bl):
        ref[0:EDGE, :] = zero
        ref[pairs * PAIR + EDGE :, :] = zero
    for ref in (bh, bl):
        ref[(pairs - 1) * PAIR + EDGE : pairs * PAIR + EDGE, :] = jnp.zeros((PAIR, 256), jnp.bfloat16)
    for pair in range(OWN_PAIRS[0]):
        ingest(lambda source, pair=pair: left_ref[source, 8 * pair : 8 * pair + 8, :], pair, fa, ah, al)
    for pair in range(OWN_PAIRS[1], pairs):

        def load(source, start=8 * (pair - OWN_PAIRS[1])):
            count = min(8, 4 * RIGHT - start)
            rows = right_ref[4 * RIGHT * source + start : 4 * RIGHT * source + start + count, :]
            return rows if count == 8 else jnp.concatenate([rows, jnp.zeros_like(rows)], axis=0)

        ingest(load, pair, fa, ah, al)
    reach = ((0, pairs - 1), (1, pairs - 1), (1, pairs - 2), (2, pairs - 2))
    for count, step in enumerate(steps(ch_ref, cl_ref, *fields)):
        low, high = OWN_PAIRS[0] + 1 + count, OWN_PAIRS[1] - 1 - count
        for pair in list(range(reach[count][0], low)) + list(range(high, reach[count][1])):
            step(pair)
    last = OWN_PAIRS[1] * PAIR + EDGE
    stores += results(OWN_PAIRS[0] * PAIR, INNER[0] * PAIR, 2) + results(INNER[1] * PAIR, last, 4)
    for store in stores[2:]:
        store.start()
    before = slice(first_row, INNER[0] * PAIR + EDGE)
    after = slice(INNER[1] * PAIR + EDGE, OWN_PAIRS[1] * PAIR + EDGE)
    high, low = (jnp.concatenate([ref[before, :], ref[after, :]], axis=0) for ref in (ah, al))
    g_ref[...] = lower_blocks(inner_ref[...] + gram_of(high, low))
    for store in stores:
        store.wait()


def filtered_blocks(received, coef_high, coef_low):
    count = lax.axis_size(ALL)
    chain = [(i, i + 1) for i in range(count - 1)]
    leading = received.reshape(count, 32, 4, LANES)[:, :RIGHT]
    right = lax.ppermute(leading, ALL, [(j, i) for i, j in chain]).reshape(-1, LANES)
    left = lax.ppermute(received[:, 128 - 4 * LEFT :], ALL, chain)
    state = interior(received, coef_high, coef_low)
    half = pltpu.HBM((2048 + EDGE, 256), jnp.bfloat16)
    fields = [pltpu.VMEM(value.shape, value.dtype) for value in state[:6]]
    return pl.pallas_call(
        edges_kernel,
        out_shape=(half, half, pltpu.VMEM((PACKED, LANES), jnp.float32), *fields),
        in_specs=[ON_CHIP] * 11,
        out_specs=(OFF_CHIP,) * 2 + (ON_CHIP,) * 7,
        input_output_aliases={i + 2: i + 3 for i in range(6)},
        scratch_shapes=[pltpu.SemaphoreType.DMA((6,))],
        compiler_params=VMEM,
        name="edges",
    )(left, right, *state)[:3]


def moment_kernel(vh_ref, vl_ref, ch_ref, cl_ref, g_ref, m_ref, bh, bl):
    block, edge = 128, 64

    def image(pair, rows, drop=0):
        vh, vl = vh_ref[rows, :], vl_ref[rows, :]
        c_high, c_low = ch_ref[pair, :, drop:], cl_ref[pair, :, drop:]
        value = dot(
            jnp.concatenate([c_high, c_high, c_low], axis=1), jnp.concatenate([vh, vl, vh], axis=0)
        )
        at = pl.ds((pair - 2) * block, block)
        bh[at, :], bl[at, :] = split(value)

    def body(pair, carry):
        image(pair, pl.ds(pl.multiple_of((pair - 3) * block + edge, edge), 256))
        return carry

    image(2, slice(0, block + edge), edge)
    lax.fori_loop(3, 18, body, 0, unroll=3)
    rows = slice(16 * block - edge, 16 * block)
    c_high, c_low = ch_ref[18, 0:edge, 0:edge], cl_ref[18, 0:edge, 0:edge]
    value = dot(c_high, vh_ref[rows, :]) + (dot(c_high, vl_ref[rows, :]) + dot(c_low, vh_ref[rows, :]))
    bh[16 * block :, :], bl[16 * block :, :] = split(value)
    dims = ((0,), (0,))
    high = vh_ref[...]
    moment = dot(high, bh[...], dims) + (dot(high, bl[...], dims) + dot(vl_ref[...], bh[...], dims))
    m_ref[...] = (0.5 * SCALE) * lower_blocks(moment) + SHIFT * g_ref[...]


def moment_of(vh, vl, coef_high, coef_low, gram):
    return pl.pallas_call(
        moment_kernel,
        out_shape=jax.ShapeDtypeStruct((PACKED, LANES), jnp.float32),
        scratch_shapes=[pltpu.VMEM((16 * 128 + 64, 256), jnp.bfloat16)] * 2,
        compiler_params=VMEM,
        cost_estimate=pl.CostEstimate(flops=int(4e9), transcendentals=0, bytes_accessed=int(1e7)),
        name="moment",
    )(*off_chip(vh, vl, coef_high, coef_low), gram)


def panel_solve(block, lines):
    row = lax.broadcasted_iota(jnp.int32, (8, LANES), 0)

    def spread(tile, k):
        return jnp.broadcast_to(tile[k % 8 : k % 8 + 1], tile.shape)

    cols = [
        [jnp.broadcast_to(block[8 * t : 8 * t + 8, j : j + 1], (8, LANES)) for t in range(4)]
        for j in range(32)
    ]
    lines = [
        [lines[8 * t : 8 * t + 8, LANES * h : LANES * h + LANES] for h in range(2)] for t in range(4)
    ]
    pivots = [jnp.ones((8, LANES), jnp.float32) for t in range(4)]
    for k in range(32):
        own = k // 8
        pivot = spread(cols[k][own], k)
        pivots[own] = jnp.where(row == k % 8, pivot, pivots[own])
        scale = 1.0 / pivot
        ratio = {t: cols[k][t] * scale for t in range(own, 4)}
        line = [spread(part, k) for part in lines[own]]
        for j in range(k + 1, 32):
            weight = spread(cols[k][j // 8], j)
            for t in range(j // 8, 4):
                cols[j][t] = cols[j][t] - ratio[t] * weight
        ratio[own] = jnp.where(row > k % 8, ratio[own], 0.0)
        for t in range(own, 4):
            lines[t] = [part - ratio[t] * above for part, above in zip(lines[t], line)]
    roots = [lax.rsqrt(pivots[t]) for t in range(4)]
    return jnp.concatenate(
        [jnp.concatenate([part * roots[t] for part in lines[t]], axis=1) for t in range(4)], axis=0
    )


def half_inverse(aug):
    def panel(p, carry):
        rows = pl.ds(pl.multiple_of(32 * p, 32), 32)
        lines = aug[rows, :]
        lines = panel_solve(pltpu.roll(lines[:, :LANES], LANES - 32 * p, 1), lines)
        aug[rows, :] = lines

        @pl.when(p < 3)
        def update():
            lane = lax.broadcasted_iota(jnp.int32, (32, LANES), 1)
            upper = jnp.where(lane >= 32 * (p + 1), lines[:, :LANES], 0.0)
            aug[...] = aug[...] - dot(upper, lines, ((0,), (0,)), HIGHEST)

        return carry

    lax.fori_loop(0, 4, panel, 0)


def basis_kernel(entries, both_ref, vh_hbm, vl_hbm, w_ref, o_hbm, gram, aug, vh, vl, scr, out, sem, out_sem):
    loads = [
        pltpu.make_async_copy(vh_hbm.at[OWN, :], vh, sem.at[0]),
        pltpu.make_async_copy(vl_hbm.at[OWN, :], vl, sem.at[1]),
    ]
    for load in loads:
        load.start()
    row = lax.broadcasted_iota(jnp.int32, (LANES, LANES), 0)
    eye = (row == lax.broadcasted_iota(jnp.int32, (LANES, LANES), 1)).astype(jnp.float32)
    for d in range(32):
        gram[10 * d : 10 * d + 10, :] = both_ref[20 * d : 20 * d + 10, :] * (1.0 / entries)
    above, below, after = whole_blocks(gram[...])
    aug[:, :LANES] = above
    aug[:, LANES:] = eye
    half_inverse(aug)
    first = aug[:, LANES:]
    upper = dot(first, below, ((1,), (1,)), HIGHEST)
    aug[:, :LANES] = after - dot(upper, upper, ((0,), (0,)), HIGHEST)
    aug[:, LANES:] = eye
    corner = dot(upper, first, ((0,), (0,)), HIGHEST)
    half_inverse(aug)
    second = aug[:, LANES:]
    w_ref[:LANES, :LANES] = first
    w_ref[:LANES, LANES:] = jnp.zeros((LANES, LANES), jnp.float32)
    w_ref[LANES:, :LANES] = -dot(second, corner, precision=HIGHEST)
    w_ref[LANES:, LANES:] = second
    for load in loads:
        load.wait()
    sends = [pltpu.make_async_copy(out.at[d], o_hbm.at[d], out_sem.at[d]) for d in range(32)]
    for half in range(2):
        used = LANES * (half + 1)
        wh, wl = split(w_ref[LANES * half : used, :used])
        values = [vh[:, :used], vl[:, :used], vh[:, :used]]
        scr[...] = dot(
            jnp.concatenate(values, axis=1), jnp.concatenate([wh, wh, wl], axis=1), ((1,), (1,))
        )
        for slab in range(4):
            pieces = []
            for mid in range(2):
                columns = []
                for column in range(2):
                    at = column * 64 + mid * 32 + slab * 8
                    columns.append(
                        jnp.concatenate(
                            [scr[pair * 128 + at : pair * 128 + at + 8, :] for pair in range(16)], axis=0
                        )
                    )
                pieces += [value.reshape(128, LANES) for value in halves(*columns)]
            for j, piece in enumerate(exchange(pieces, 32)):
                d = (half * 4 + j) * 4 + slab
                out[d] = piece
                sends[d].start()
    for send in sends:
        send.wait()


def basis(both, entries, vh, vl):
    return pl.pallas_call(
        functools.partial(basis_kernel, entries),
        out_shape=(
            jax.ShapeDtypeStruct((256, 256), jnp.float32),
            pltpu.HBM((32, 128, LANES), jnp.float32),
        ),
        in_specs=[ON_CHIP, OFF_CHIP, OFF_CHIP],
        out_specs=(ON_CHIP, OFF_CHIP),
        scratch_shapes=[
            pltpu.VMEM((PACKED, LANES), jnp.float32),
            pltpu.VMEM((LANES, 256), jnp.float32),
            pltpu.VMEM((2048, 256), jnp.bfloat16),
            pltpu.VMEM((2048, 256), jnp.bfloat16),
            pltpu.VMEM((2048, LANES), jnp.float32),
            pltpu.VMEM((32, LANES, LANES), jnp.float32),
            pltpu.SemaphoreType.DMA((2,)),
            pltpu.SemaphoreType.DMA((32,)),
        ],
        compiler_params=VMEM,
        cost_estimate=pl.CostEstimate(flops=int(4e9), transcendentals=0, bytes_accessed=int(2e7)),
        name="basis",
    )(both.reshape(2 * PACKED, LANES), *off_chip(vh, vl))


def parts_of(blocks):
    return blocks.reshape(lax.axis_size(ALL), -1, 2, LANES)


def swap(parts):
    rows = parts.reshape((-1,) + parts.shape[-2:])
    return lax.all_to_all(rows, ALL, 0, 0, tiled=True).reshape(parts.shape)


def for_all(share):
    return jnp.broadcast_to(share[None], (lax.axis_size(ALL),) + share.shape)


def project_kernel(entries, moment_ref, w_ref, p_ref):
    first = pl.multiple_of(32 * lax.axis_index("blk"), 32)
    mine = w_ref[pl.ds(first, 32), :]
    left, right = mine[:, :LANES], mine[:, LANES:]
    above, below, last = whole_blocks(moment_ref[...])
    half_done = jnp.concatenate(
        [
            dot(left, above, precision=HIGHEST) + dot(right, below, precision=HIGHEST),
            dot(left, below, ((1,), (1,)), HIGHEST) + dot(right, last, precision=HIGHEST),
        ],
        axis=1,
    ) * (1.0 / entries)
    p_ref[...] = dot(half_done, w_ref[...], ((1,), (1,)), HIGHEST)


def project(moment, inverse, entries):
    return pl.pallas_call(
        functools.partial(project_kernel, entries),
        out_shape=jax.ShapeDtypeStruct((32, 256), jnp.float32),
        in_specs=[ON_CHIP] * 2,
        out_specs=ON_CHIP,
        compiler_params=VMEM,
        name="project",
    )(moment, inverse)


def fast(states_in, region, onsite_table, hop_table, coupling_x, coupling_y):
    device = lax.axis_index("blk") * lax.axis_size("slab") + lax.axis_index("slab")
    entries = float(BANDS * 8 * 1024)
    codes = lax.all_gather((region + 1).astype(jnp.float32), "slab", axis=0, tiled=True)
    received = swap(pack(states_in))
    codes = jnp.pad(codes, ((0, 0), (LEFT + 1, LANES)))
    codes = lax.dynamic_slice(codes, (0, 32 * device), (8, LANES))
    coef_high, coef_low = coefficients(codes, onsite_table, hop_table, coupling_x, coupling_y)
    vh, vl, own_gram = filtered_blocks(received, coef_high, coef_low)
    own_moment = moment_of(vh, vl, coef_high, coef_low, own_gram)
    share = swap(parts_of(own_gram)).sum(0)
    both = swap(jnp.concatenate([for_all(share), parts_of(own_moment)], axis=1))
    inverse, blocks = basis(both, entries, vh, vl)
    moment = swap(for_all(both[:, 5:].sum(0))).reshape(PACKED, LANES)
    blocks, moment = lax.optimization_barrier((blocks, moment))
    states_out = unpack(swap(blocks))
    projected = project(moment, inverse, entries)
    return states_out, projected


DEGREE = 4


def extended(array, sides, width):
    for axis, dim in sides:
        size, length = (lax.axis_size(axis), array.shape[dim])
        up = [(i, (i + 1) % size) for i in range(size - 1)]
        down = [(j, i) for i, j in up]
        last = lax.slice_in_dim(array, length - width, length, axis=dim)
        leading = lax.slice_in_dim(array, 0, width, axis=dim)
        before = lax.ppermute(last, axis, up)
        after = lax.ppermute(leading, axis, down)
        array = jnp.concatenate([before, array, after], axis=dim)
    return array


def mixing(onsite_table, coupling_x, coupling_y):
    onsite = 0.5 * (onsite_table + jnp.swapaxes(onsite_table, 1, 2))
    blocks = [onsite[material] for material in range(onsite.shape[0])]
    return jnp.concatenate(
        blocks + [0.5 * (coupling_x - coupling_x.T), 0.5 * (coupling_y - coupling_y.T)], axis=1
    )


def masks_of(region):
    codes = jnp.arange(MATERIALS, dtype=jnp.int32)
    return (region[None] == codes[:, None, None]).astype(jnp.float32)


def apply_padded(padded, hop_padded, material_masks, mixing_matrix):
    centre = padded[:, :, 1:-1, 1:-1]
    hop_centre = hop_padded[:, 1:-1, 1:-1]
    kinetic = jnp.zeros_like(centre)
    sides = (
        (padded[:, :, 2:, 1:-1], hop_padded[:, 2:, 1:-1]),
        (padded[:, :, :-2, 1:-1], hop_padded[:, :-2, 1:-1]),
        (padded[:, :, 1:-1, 2:], hop_padded[:, 1:-1, 2:]),
        (padded[:, :, 1:-1, :-2], hop_padded[:, 1:-1, :-2]),
    )
    for field_side, hop_side in sides:
        kinetic = kinetic + (0.5 * (hop_centre + hop_side))[None] * (centre - field_side)
    deriv_rows = 0.5 * (padded[:, :, 2:, 1:-1] - padded[:, :, :-2, 1:-1])
    deriv_cols = 0.5 * (padded[:, :, 1:-1, 2:] - padded[:, :, 1:-1, :-2])
    pieces = [
        material_masks[material][None, None] * centre for material in range(material_masks.shape[0])
    ]
    stacked = jnp.concatenate(pieces + [deriv_rows, deriv_cols], axis=1)
    mixed = jnp.einsum("bc,scxy->sbxy", mixing_matrix, stacked, precision=lax.Precision.HIGHEST)
    return mixed + kinetic


def chebyshev(field, apply_fn):

    def scaled(value):
        return (apply_fn(value) - SHIFT * value) / SCALE

    previous = field
    current = scaled(field)
    for repeat in range(DEGREE - 1):
        previous, current = (current, 2.0 * scaled(current) - previous)
    return current


def inner(left, right):
    return jnp.dot(
        left, right.T, precision=lax.Precision.HIGHEST, preferred_element_type=jnp.float32
    )


def general(states_in, region, onsite_table, hop_table, coupling_x, coupling_y):
    mixing_matrix = mixing(onsite_table, coupling_x, coupling_y)
    material_masks = masks_of(region)
    hop_field = jnp.einsum(
        "mb,mxy->bxy", hop_table, material_masks, precision=lax.Precision.HIGHEST
    )
    hop_rows = extended(hop_field, (("slab", 1),), 1)
    hop_padded = jnp.pad(hop_rows, ((0, 0), (0, 0), (1, 1)))

    def apply_rows(field):
        padded = extended(field, (("slab", 2),), 1)
        padded = jnp.pad(padded, ((0, 0), (0, 0), (0, 0), (1, 1)))
        return apply_padded(padded, hop_padded, material_masks, mixing_matrix)

    filtered = chebyshev(states_in, apply_rows)
    block_count = lax.axis_size("blk")
    slab_count = lax.axis_size("slab")
    states_all = filtered.shape[0] * block_count
    row_count = filtered.shape[2]
    width_all = filtered.shape[3]
    entries = float(BANDS * row_count * slab_count * width_all)
    image = apply_rows(filtered)
    cell_states, cell_image = (
        lax.all_to_all(filtered, "blk", split_axis=3, concat_axis=0, tiled=True),
        lax.all_to_all(image, "blk", split_axis=3, concat_axis=0, tiled=True),
    )
    states_flat = cell_states.reshape(states_all, -1)
    image_flat = cell_image.reshape(states_all, -1)
    moment = lax.psum(inner(states_flat, image_flat) / entries, ("blk", "slab"))

    def panel_step(panel, carry):
        basis_rows, factor_rows = carry
        offset = panel * PANEL
        panel_states = lax.dynamic_slice_in_dim(states_flat, offset, PANEL, 0)
        coeffs = lax.psum(inner(basis_rows, panel_states) / entries, ("blk", "slab"))
        residue = panel_states - jnp.dot(
            coeffs.T,
            basis_rows,
            precision=lax.Precision.HIGHEST,
            preferred_element_type=jnp.float32,
        )
        panel_gram = lax.psum(inner(residue, residue) / entries, ("blk", "slab"))
        panel_factor = jnp.linalg.cholesky(panel_gram)
        panel_basis = lax.linalg.triangular_solve(panel_factor, residue, left_side=True, lower=True)
        basis_rows = lax.dynamic_update_slice_in_dim(basis_rows, panel_basis, offset, 0)
        factor_row = lax.dynamic_update_slice_in_dim(coeffs.T, panel_factor, offset, 1)
        factor_rows = lax.dynamic_update_slice_in_dim(factor_rows, factor_row, offset, 0)
        return (basis_rows, factor_rows)

    start_state = (jnp.zeros_like(states_flat), jnp.zeros((states_all, states_all), jnp.float32))
    basis_flat, factor = lax.fori_loop(0, states_all // PANEL, panel_step, start_state)
    half_done = lax.linalg.triangular_solve(factor, moment, left_side=True, lower=True)
    projected = lax.linalg.triangular_solve(factor, half_done.T, left_side=True, lower=True).T
    basis_cells = basis_flat.reshape(cell_states.shape)
    states_out = lax.all_to_all(basis_cells, "blk", split_axis=0, concat_axis=3, tiled=True)
    owned = states_all // block_count
    projected_rows = lax.dynamic_slice_in_dim(projected, lax.axis_index("blk") * owned, owned, 0)
    return (states_out, projected_rows)


def per_device(states_in, region, *tables):
    known = (lax.axis_size("blk"), lax.axis_size("slab")) == (8, 4)
    run = fast if known and states_in.shape == (32, 8, 2, 1024) else general
    return run(states_in, region, *tables)


def solution(mesh):
    return jax.shard_map(
        per_device,
        mesh=mesh,
        in_specs=(P("blk", None, "slab", None), P("slab", None), P(), P(), P(), P()),
        out_specs=(P("blk", None, "slab", None), P("blk", None)),
        check_vma=False,
    )
```
